32 devices in a mesh: wide: 8 (over z, y), narrow: 4 (over x, core).
Axes of the slice: x: 2, y: 2, z: 4, core: 2. Of those that a mesh axis runs over, the one named last changes fastest.
Arguments:
- tokens: bfloat16 [32, 680, 1024], P(('wide', 'narrow')), may hold values from -6 to 6
- labels: int32 [32], P(('wide', 'narrow')), may hold values from 0 to 1000
- stop_scale: int32 [32], P(('wide', 'narrow')), may hold values from 6 to 10
- class_table: bfloat16 [1001, 1024], P(None, ('wide', 'narrow')), may hold values from -6 to 6
- ada_weight: bfloat16 [1024, 6144], P(('wide', 'narrow')), may hold values from -0.1875 to 0.1875
- ada_bias: bfloat16 [6144], P(('wide', 'narrow')), may hold values from -3 to 3
- qkv_weight: bfloat16 [1024, 3072], P(('wide', 'narrow')), may hold values from -0.1875 to 0.1875
- head_scale: float32 [16], replicated, may hold values from 2.1 to 3.1
- out_weight: bfloat16 [1024, 1024], P(('wide', 'narrow')), may hold values from -0.75 to 0.75
- up_weight: bfloat16 [1024, 4096], P(('wide', 'narrow')), may hold values from -0.1875 to 0.1875
- up_bias: bfloat16 [4096], P(('wide', 'narrow')), may hold values from -3 to 3
- down_weight: bfloat16 [4096, 1024], P(('wide', 'narrow')), may hold values from -0.09375 to 0.09375
- cotangent: bfloat16 [32, 680, 1024], P(('wide', 'narrow')), may hold values from -6 to 6
Outputs:
- block_out: bfloat16 [32, 680, 1024], P(('wide', 'narrow'))
- input_grad: float32 [32, 680, 1024], P(('wide', 'narrow'))
- class_table_grad: float32 [1001, 1024], P(None, ('wide', 'narrow'))
- ada_weight_grad: float32 [1024, 6144], P(('wide', 'narrow'))
- ada_bias_grad: float32 [6144], P(('wide', 'narrow'))
- qkv_weight_grad: float32 [1024, 3072], P(('wide', 'narrow'))
- head_scale_grad: float32 [16], replicated
- out_weight_grad: float32 [1024, 1024], P(('wide', 'narrow'))
- up_weight_grad: float32 [1024, 4096], P(('wide', 'narrow'))
- up_bias_grad: float32 [4096], P(('wide', 'narrow'))
- down_weight_grad: float32 [4096, 1024], P(('wide', 'narrow'))
The draws below stay inside these ranges and needn't reach their ends.
Inputs may be any that keep to these rules, and one draw needn't show every extreme that they name: `labels`: class index of each image. Each image keeps its first stop_scale scales; its later positions are padding.
All inputs are finite; a program needn't handle non-finite values.
Results may differ from the reference program's by a relative error of at most 0.023.
Values may be sent and summed in bfloat16 or wider, within the bound.
No kernel may reach another device: no remote copies, remote signals or barrier semaphores. Data moves between devices by JAX's collectives and lax.ppermute only.
A program may use at most 320 MiB of HBM per device.

```python
import jax
import jax.numpy as jnp
import numpy as np
from jax import lax

D = 1024
HEADS = 16
HDIM = 64
FF = 4096
CLASSES = 1001
SCALES = 10
SEQ = 680
IMAGES = 32


def with_ends(drawn, rng, least, largest):
    extent = drawn.shape
    index_at = [jax.random.randint(jax.random.fold_in(rng, axis), (), 0, extent[axis]) for axis in range(len(extent))]
    drawn = drawn.at[tuple(index_at)].set(least)
    longest = extent.index(max(extent))
    index_at[longest] = (index_at[longest] + 1) % extent[longest]
    return drawn.at[tuple(index_at)].set(largest)


def strengthened(array, stream_key, source, target, parts, factor):
    owner, partner = [(jnp.arange(array.shape[axis_at]) // (array.shape[axis_at] // parts)).reshape([-1 if axis == axis_at else 1 for axis in range(array.ndim)]) for axis_at in (source, target)]
    chosen = jax.random.permutation(stream_key, parts)[partner]
    strong = (owner == chosen) | (owner == (partner + parts // 2) % parts)
    return jnp.where(strong, factor * array, array)


def steps_of(own_key, dims, cuts, smallest, high):
    factor_of = 1.0
    for position, parts in cuts:
        steps = jax.random.uniform(jax.random.fold_in(jax.random.fold_in(own_key, 6), position), (parts,), jnp.float32, smallest / len(cuts), high / len(cuts))
        factor_of = factor_of * jnp.repeat(jnp.exp(steps), dims[position] // parts).reshape((-1,) + (1,) * (len(dims) - 1 - position))
    return factor_of


def bell_draw(stream_key, extent, deviation, most, cuts=(), kind=jnp.bfloat16):
    loudness = steps_of(stream_key, extent, cuts, -0.22, 0.18) if cuts else 1.0
    values = jax.random.normal(stream_key, extent, jnp.float32) * deviation * loudness
    return jnp.minimum(jnp.maximum(values, -most), most).astype(kind)


def heavy_noise(own_key, shape, width, reach, cuts, heavy, kind=jnp.bfloat16):
    drawn = width * jax.random.normal(own_key, shape, jnp.float32)
    if cuts:
        drawn = drawn * steps_of(own_key, shape, cuts, -0.22, 0.18)
    return jnp.clip(strengthened(drawn, jax.random.fold_in(own_key, 3), *heavy), -reach, reach).astype(kind)


def setup_inputs(seed: int = 0) -> dict:
    key_of = jax.random.split(jax.random.key(seed), 14)
    tokens = bell_draw(key_of[0], (IMAGES, SEQ, D), 1.0, 6.0, ((0, 32),))
    labels = with_ends(jax.random.randint(key_of[1], (IMAGES,), 0, CLASSES), jax.random.fold_in(key_of[1], 1), 0, CLASSES - 1).astype(jnp.int32)
    stop_scale = with_ends(jax.random.randint(key_of[2], (IMAGES,), max(SCALES - 4, 1), SCALES + 1), jax.random.fold_in(key_of[2], 1), max(SCALES - 4, 1), SCALES).astype(jnp.int32)
    class_table = bell_draw(key_of[3], (CLASSES, D), 1.0, 6.0, ((1, 32),))
    ada_weight = bell_draw(key_of[4], (D, 6 * D), D ** -0.5, 0.1875, ((0, 32),))
    ada_bias = bell_draw(key_of[5], (6 * D,), 0.5, 3.0, ((0, 32),))
    qkv_weight = bell_draw(key_of[6], (D, 3 * D), D ** -0.5, 0.1875, ((0, 32),))
    head_scale = jnp.clip(jax.random.uniform(key_of[7], (HEADS,), jnp.float32, 2.1, 3.1), 2.1, 3.1)
    out_weight = bell_draw(key_of[8], (D, D), (D // 16) ** -0.5, 0.75, ((0, 32),))
    up_weight = bell_draw(key_of[9], (D, FF), D ** -0.5, 0.1875, ((0, 32),))
    up_bias = bell_draw(key_of[10], (FF,), 0.5, 3.0, ((0, 32),))
    down_weight = bell_draw(key_of[11], (FF, D), FF ** -0.5, 0.09375, ((0, 32),))
    cotangent = heavy_noise(key_of[12], (IMAGES, SEQ, D), 1.0, 6.0, ((0, 32),), (0, 2, 32, 2.75))
    return {"tokens": tokens, "labels": labels, "stop_scale": stop_scale, "class_table": class_table, "ada_weight": ada_weight, "ada_bias": ada_bias, "qkv_weight": qkv_weight, "head_scale": head_scale, "out_weight": out_weight, "up_weight": up_weight, "up_bias": up_bias, "down_weight": down_weight, "cotangent": cotangent}


scale_sides = (1, 2, 3, 4, 5, 6, 8, 10, 13, 16)

@jax.custom_vjp
def low(v):
    return lax.optimization_barrier(v.astype(jnp.bfloat16)).astype(jnp.float32)

@jax.custom_vjp
def low_back(v):
    return v

def low_keep(v):
    return (low(v), None)

def low_pass(kept, grad):
    return (grad,)

def back_keep(v):
    return (v, None)

def back_low(kept, grad):
    return (low(grad),)
low.defvjp(low_keep, low_pass)
low_back.defvjp(back_keep, back_low)

def position_scale(scale_count):
    return np.concatenate([np.full(side_size * side_size, level_index, dtype=np.int32) for level_index, side_size in enumerate(scale_sides[:scale_count])])

def normalized(inputs):
    centred = inputs - lax.optimization_barrier(jnp.mean(inputs, axis=-1, keepdims=True))
    return centred * lax.rsqrt(lax.optimization_barrier(jnp.mean(centred * centred, axis=-1, keepdims=True)) + 1e-06)

def modulate(inputs, scale_vec, shift_vec):
    return normalized(inputs) * (1.0 + scale_vec[:, None, :]) + shift_vec[:, None, :]

def unit_rows(inputs):
    return inputs * lax.rsqrt(lax.optimization_barrier(jnp.sum(inputs * inputs, axis=-1, keepdims=True)) + 1e-06)

def gelu_tanh(inputs):
    return jax.nn.gelu(inputs, approximate=True)

def block_forward(parameters, inputs, labels, stop_scale):
    class_table, ada_weight, ada_bias, qkv_weight, head_scale, out_weight, up_weight, up_bias, down_weight = parameters
    highest = lax.Precision.HIGHEST
    levels = position_scale(SCALES)
    allowed = jnp.asarray(levels[None, :] <= levels[:, None])
    live_mask = (jnp.asarray(levels)[None, :] < stop_scale[:, None]).astype(jnp.float32)[:, :, None]
    onehot = (labels[:, None] == jnp.arange(CLASSES, dtype=jnp.int32)[None, :]).astype(jnp.float32)
    condition = jnp.dot(onehot, class_table, precision=highest)
    cond_act = low(jax.nn.silu(condition))
    modulation = low_back(jnp.dot(cond_act, ada_weight, precision=highest) + ada_bias)
    gate_one, gate_two, scale_one, scale_two, shift_one, shift_two = jnp.split(modulation, 6, axis=-1)
    attn_in = low(modulate(inputs, scale_one, shift_one))
    qkv_rows = low_back(jnp.einsum('gsd,de->gse', attn_in, qkv_weight, precision=highest))
    query_raw, key_raw, value_raw = jnp.split(qkv_rows, 3, axis=-1)
    head_shape = inputs.shape[:2] + (HEADS, HDIM)
    queries = low(unit_rows(query_raw.reshape(head_shape)) * jnp.exp(head_scale)[:, None])
    key_unit = low(unit_rows(key_raw.reshape(head_shape)))
    values = low(value_raw.reshape(head_shape))
    scores = low_back(jnp.einsum('gqhc,gkhc->ghqk', queries, key_unit, precision=highest))
    masked = jnp.where(allowed, scores, -1e+30)
    row_peak = lax.optimization_barrier(jnp.max(masked, axis=-1, keepdims=True))
    weights = jnp.exp(masked - row_peak)
    probs_low = low(weights / lax.optimization_barrier(jnp.sum(weights, axis=-1, keepdims=True)))
    attended = jnp.einsum('ghqk,gkhc->gqhc', probs_low, values, precision=highest).reshape(inputs.shape)
    attended = low_back(low(attended))
    projected = low_back(jnp.einsum('gsd,de->gse', attended, out_weight, precision=highest))
    residual = inputs + gate_one[:, None, :] * projected
    mlp_in = low(modulate(residual, scale_two, shift_two))
    hidden = low_back(jnp.einsum('gsd,df->gsf', mlp_in, up_weight, precision=highest) + up_bias)
    activated = low(gelu_tanh(hidden))
    mlp_out = low_back(jnp.einsum('gsf,fd->gsd', activated, down_weight, precision=highest))
    return (residual + gate_two[:, None, :] * mlp_out) * live_mask

def reference(tokens, labels, stop_scale, class_table, ada_weight, ada_bias, qkv_weight, head_scale, out_weight, up_weight, up_bias, down_weight, cotangent):
    parameters = tuple((weight_arg.astype(jnp.float32) for weight_arg in (class_table, ada_weight, ada_bias, qkv_weight, head_scale, out_weight, up_weight, up_bias, down_weight)))
    per_step = 4
    step_count = IMAGES // per_step
    grouped = (tokens.astype(jnp.float32).reshape(step_count, per_step, SEQ, D), labels.reshape(step_count, per_step), stop_scale.reshape(step_count, per_step), cotangent.astype(jnp.float32).reshape(step_count, per_step, SEQ, D))

    def one_group(totals, pieces):
        group_tokens, group_labels, group_stops, group_grad = pieces

        def forward(params_in, inputs_in):
            return block_forward(params_in, inputs_in, group_labels, group_stops)
        result, pullback = jax.vjp(forward, parameters, group_tokens)
        param_grads, input_grads = pullback(group_grad)
        totals = jax.tree.map(jnp.add, totals, param_grads)
        return (totals, (result.astype(jnp.bfloat16), input_grads))
    starting = jax.tree.map(jnp.zeros_like, parameters)
    totals, (outputs, input_grads) = lax.scan(one_group, starting, grouped)
    return (outputs.reshape(IMAGES, SEQ, D), input_grads.reshape(IMAGES, SEQ, D), totals[0], totals[1], totals[2], totals[3], totals[4], totals[5], totals[6], totals[7], totals[8])
```

```python
from functools import partial

import jax
import jax.numpy as jnp
import numpy as np
from jax import lax
from jax.experimental import pallas as pl
from jax.experimental.pallas import tpu as pltpu
from jax.sharding import PartitionSpec as P

HDIM = 64
SCALES = 10
AXES = ("wide", "narrow")
BF = jnp.bfloat16
F32 = jnp.float32

scale_sides = (1, 2, 3, 4, 5, 6, 8, 10, 13, 16)
head_block = 4


def position_scale(scale_count):
    return np.concatenate(
        [
            np.full(side_size * side_size, level_index, dtype=np.int32)
            for level_index, side_size in enumerate(scale_sides[:scale_count])
        ]
    )


def normalized(inputs):
    centred = inputs - jnp.mean(inputs, axis=-1, keepdims=True)
    return centred * lax.rsqrt(jnp.mean(centred * centred, axis=-1, keepdims=True) + 1e-06)


def modulate(inputs, scale_vec, shift_vec):
    return normalized(inputs) * (1.0 + scale_vec[:, None, :]) + shift_vec[:, None, :]


def unit_rows(inputs):
    return inputs * lax.rsqrt(jnp.sum(inputs * inputs, axis=-1, keepdims=True) + 1e-06)


def split_heads(matrix, image_count, seq_len):
    blocks = matrix.reshape(image_count, seq_len, -1, head_block, HDIM)
    return jnp.moveaxis(blocks, 2, 1).reshape(-1, seq_len, head_block, HDIM)


def join_heads(blocks, image_count, seq_len):
    shaped = blocks.reshape(image_count, -1, seq_len, head_block, HDIM)
    return jnp.moveaxis(shaped, 1, 2).reshape(image_count * seq_len, -1)


def masked_scores(query_block, key_block, allowed):
    scores = jnp.einsum("qhc,khc->hqk", query_block, key_block, preferred_element_type=F32)
    return jnp.where(allowed[None], scores, -1e30)


def attend_forward(pieces, allowed):
    query_block, key_block, value_block = pieces
    scores = masked_scores(query_block, key_block, allowed)
    row_peak = jnp.max(scores, axis=-1, keepdims=True)
    log_total = row_peak + jnp.log(jnp.sum(jnp.exp(scores - row_peak), axis=-1, keepdims=True))
    probs_low = jnp.exp(scores - log_total).astype(BF)
    attended = jnp.einsum("hqk,khc->qhc", probs_low, value_block, preferred_element_type=F32)
    return (attended, log_total)


def attend_backward(pieces, allowed):
    query_block, key_block, value_block, grad_block, log_total = pieces
    scores = masked_scores(query_block, key_block, allowed)
    probs = jnp.exp(scores - log_total)
    probs_low = probs.astype(BF)
    grad_probs = jnp.einsum("qhc,khc->hqk", grad_block, value_block, preferred_element_type=F32)
    row_inner = jnp.sum(probs * grad_probs, axis=-1, keepdims=True)
    grad_scores = (probs * (grad_probs - row_inner)).astype(BF)
    grad_values = jnp.einsum("hqk,qhc->khc", probs_low, grad_block, preferred_element_type=F32)
    grad_queries = jnp.einsum("hqk,khc->qhc", grad_scores, key_block, preferred_element_type=F32)
    grad_keys = jnp.einsum("hqk,qhc->khc", grad_scores, query_block, preferred_element_type=F32)
    return (grad_queries, grad_keys, grad_values)


def swap(block, count, mask):
    return lax.ppermute(block, AXES, [(i, i ^ mask) for i in range(count)])


def place_body(me_ref, *refs, blocks):
    half = len(refs) // 2
    for src, dst in zip(refs[:half], refs[half:]):
        dst[...] = src[0]


def gather_rows(shard, count, me):
    rows, width = shard.shape
    bits = count.bit_length() - 1
    if count != 1 << bits or bits < 3 or rows % 16 or width % 256:
        return lax.all_gather(shard, AXES, axis=0, tiled=True)
    block, order = shard[None], []
    for bit in range(bits - 1, 2, -1):
        block = jnp.concatenate([block, swap(block, count, 1 << bit)])
        order.append(bit)
    half = width // 2
    parts = []
    for cols, two in ((block[:, :, :half], (2, 1)), (block[:, :, half:], (1, 2))):
        for bit in two:
            cols = jnp.concatenate([cols, swap(cols, count, 1 << bit)])
        parts.append((cols, swap(cols, count, 1), order + list(two)))
    out = []
    total = count // 2
    for own, other, seq in parts:
        code = [0]
        for bit in seq:
            code = code + [c | (1 << bit) for c in code]
        code = jnp.asarray(np.array(code, np.int32)) ^ me
        out.append(place(own, other, code, total, rows, half))
    return out


def place(own, other, code, total, rows, width):
    def body(code_ref, own_ref, other_ref, out_ref):
        core = code_ref[pl.program_id(0)] & 1

        @pl.when(core == 0)
        def _():
            out_ref[0] = own_ref[0]
            out_ref[1] = other_ref[0]

        @pl.when(core == 1)
        def _():
            out_ref[1] = own_ref[0]
            out_ref[0] = other_ref[0]

    out = pl.pallas_call(
        body,
        grid_spec=pltpu.PrefetchScalarGridSpec(
            num_scalar_prefetch=1,
            grid=(total,),
            in_specs=[pl.BlockSpec((1, rows, width), lambda m, code: (m, 0, 0))] * 2,
            out_specs=pl.BlockSpec((2, rows, width), lambda m, code: (code[m] // 2, 0, 0)),
        ),
        out_shape=jax.ShapeDtypeStruct((2 * total, rows, width), own.dtype),
        name="place",
    )(code, own, other)
    return out.reshape(2 * total * rows, width)


def halve(pieces, axis, bit_value, count, mask):
    total = pieces[0]
    if len(pieces) > 1:
        total = (pieces[0].astype(F32) + pieces[1].astype(F32)).astype(BF)
    keep = lax.dynamic_index_in_dim(total, bit_value, axis, keepdims=False)
    send = lax.dynamic_index_in_dim(total, 1 - bit_value, axis, keepdims=False)
    return [keep, swap(send, count, mask)]


def scatter_rows(grad, count, me):
    rows, width = grad.shape
    bits = count.bit_length() - 1
    own = rows // count
    if count != 1 << bits or bits < 3 or width % 256:
        return lax.psum_scatter(grad.astype(F32), AXES, scatter_dimension=0, tiled=True)
    bit = [lax.rem(lax.div(me, np.int32(1 << b)), np.int32(2)) for b in range(bits)]
    pieces = halve([grad.reshape((2,) * bits + (own, width))], bits - 1, bit[0], count, 1)
    half = width // 2
    done = []
    for cols, two in ((slice(0, half), (1, 2)), (slice(half, width), (2, 1))):
        part = [p[..., cols] for p in pieces]
        left = list(range(bits - 1, 0, -1))
        for b in two:
            part = halve(part, left.index(b), bit[b], count, 1 << b)
            left.remove(b)
        done.append(part)
    pieces = [jnp.concatenate([a, b], axis=-1) for a, b in zip(*done)]
    for b in range(3, bits):
        pieces = halve(pieces, left.index(b), bit[b], count, 1 << b)
        left.remove(b)
    return (pieces[0].astype(F32) + pieces[1].astype(F32)).reshape(own, width)


def mlp_body(x_ref, g_ref, up_ref, down_ref, bias_ref, out_ref, gx_ref, up_g, down_g, bias_g):
    @pl.when(pl.program_id(0) == 0)
    def _():
        out_ref[...] = jnp.zeros_like(out_ref)
        gx_ref[...] = jnp.zeros_like(gx_ref)

    x, g, up, down = x_ref[...], g_ref[...], up_ref[...], down_ref[...]
    hidden = jnp.dot(x, up, preferred_element_type=F32) + bias_ref[...]
    root = np.float32(np.sqrt(2.0 / np.pi))
    square = hidden * hidden
    bend = jnp.tanh(root * hidden * (1.0 + 0.044715 * square))
    act = (0.5 * hidden * (1.0 + bend)).astype(BF)
    out_ref[...] += jnp.dot(act, down, preferred_element_type=F32)
    grad_act = lax.dot_general(g, down, (((1,), (1,)), ((), ())), preferred_element_type=F32)
    slope = 0.5 * (1.0 + bend) + 0.5 * hidden * (1.0 - bend * bend) * root * (
        1.0 + (3 * 0.044715) * square
    )
    grad_hidden_wide = grad_act * slope
    grad_hidden = grad_hidden_wide.astype(BF)
    bias_g[...] = jnp.sum(grad_hidden.astype(F32), axis=0, keepdims=True)
    gx_ref[...] += lax.dot_general(
        grad_hidden, up, (((1,), (1,)), ((), ())), preferred_element_type=F32
    )
    down_g[...] = lax.dot_general(
        act, g, (((0,), (0,)), ((), ())), preferred_element_type=F32
    ).astype(BF)
    up_g[...] = lax.dot_general(
        x, grad_hidden, (((0,), (0,)), ((), ())), preferred_element_type=F32
    ).astype(BF)


def mlp(x, g, weights, bias, block=512):
    tokens, width = x.shape
    hidden = bias.shape[1]
    per = width // block
    whole = lambda f: (0, 0)
    return pl.pallas_call(
        mlp_body,
        grid=(hidden // block,),
        in_specs=[
            pl.BlockSpec((tokens, width), whole),
            pl.BlockSpec((tokens, width), whole),
            pl.BlockSpec((width, block), lambda f: (0, f)),
            pl.BlockSpec((block, width), lambda f: (f % per, hidden // width + f // per)),
            pl.BlockSpec((1, block), lambda f: (0, f)),
        ],
        out_specs=[
            pl.BlockSpec((tokens, width), whole),
            pl.BlockSpec((tokens, width), whole),
            pl.BlockSpec((width, block), lambda f: (0, f)),
            pl.BlockSpec((block, width), lambda f: (f % per, f // per)),
            pl.BlockSpec((1, block), lambda f: (0, f)),
        ],
        out_shape=[
            jax.ShapeDtypeStruct((tokens, width), F32),
            jax.ShapeDtypeStruct((tokens, width), F32),
            jax.ShapeDtypeStruct((width, hidden), BF),
            jax.ShapeDtypeStruct((width, hidden), BF),
            jax.ShapeDtypeStruct((1, hidden), F32),
        ],
        compiler_params=pltpu.CompilerParams(vmem_limit_bytes=58 << 20),
        cost_estimate=pl.CostEstimate(
            flops=12 * tokens * width * hidden, bytes_accessed=8 * width * hidden, transcendentals=tokens * hidden
        ),
        name="mlp",
    )(x, g, weights, weights, bias)


def split_low(value):
    high = value.astype(BF)
    return high, (value - high.astype(F32)).astype(BF)


def per_device(
    tokens,
    labels,
    stop_scale,
    class_table,
    ada_weight,
    ada_bias,
    qkv_weight,
    head_scale,
    out_weight,
    up_weight,
    up_bias,
    down_weight,
    cotangent,
    count,
):
    image_count, seq_len, model_width = tokens.shape
    row_count = image_count * seq_len
    me = lax.axis_index(AXES).astype(jnp.int32)
    levels = position_scale(SCALES)
    allowed = jnp.asarray(levels[None, :] <= levels[:, None])
    live_mask = (jnp.asarray(levels)[None, :] < stop_scale[:, None]).astype(F32)[:, :, None]
    class_count = class_table.shape[0]
    own = model_width // count
    ratio = down_weight.shape[0] // own
    hidden_width = up_weight.shape[1]

    def hidden_order(matrix):
        lead = matrix.shape[:-1]
        cut = matrix.reshape(lead + (count, ratio, own))
        return jnp.swapaxes(cut, -3, -2).reshape(lead + (hidden_width,))

    def hidden_back(matrix):
        lead = matrix.shape[:-1]
        cut = matrix.reshape(lead + (ratio, count, own))
        return jnp.swapaxes(cut, -3, -2).reshape(lead + (hidden_width,))

    down_wide = jnp.swapaxes(down_weight.reshape(ratio, own, model_width), 0, 1).reshape(
        own, hidden_width
    )
    mlp_shard = jnp.concatenate([hidden_order(up_weight), down_wide], axis=1)
    mlp_full = lax.all_gather(mlp_shard, AXES, axis=0, tiled=True)

    labels_all = lax.all_to_all(
        jnp.broadcast_to(labels[None, :], (count, image_count)), AXES, 0, 0, tiled=True
    ).reshape(-1)
    onehot = labels_all[:, None] == jnp.arange(class_count, dtype=jnp.int32)[None, :]
    condition = jnp.dot(onehot.astype(BF), class_table, preferred_element_type=F32)
    cond_act = jax.nn.silu(condition).astype(BF)
    modul_part = jnp.dot(cond_act, ada_weight, preferred_element_type=F32)
    bias_own = ada_bias.shape[0]
    bias_row = lax.dynamic_update_slice(
        jnp.zeros((6 * model_width,), F32), ada_bias.astype(F32), (me * bias_own,)
    )
    modul_part = modul_part + bias_row[None, :]
    up_bias_rows = jnp.broadcast_to(
        up_bias.astype(F32)[None, :], (count * image_count, up_bias.shape[0])
    )
    modul_all = lax.all_to_all(
        jnp.concatenate([modul_part, up_bias_rows], axis=1), AXES, 0, 0, tiled=True
    ).reshape(count, image_count, -1)
    modulation = jnp.sum(modul_all[:, :, : 6 * model_width], axis=0)
    up_bias_full = modul_all[:, 0, 6 * model_width :].reshape(1, hidden_width)
    gate_one, gate_two, scale_one, scale_two, shift_one, shift_two = jnp.split(
        modulation, 6, axis=-1
    )

    attn_shard = jnp.concatenate([qkv_weight, out_weight], axis=1)
    gathered = gather_rows(attn_shard, count, me)
    attn_full = (
        jnp.concatenate(gathered, axis=1) if isinstance(gathered, list) else gathered
    )
    qkv_full = attn_full[:, : 3 * model_width]
    out_full = attn_full[:, 3 * model_width :]

    inputs = tokens.astype(F32)
    attn_in = modulate(inputs, scale_one, shift_one).astype(BF).reshape(row_count, model_width)
    qkv_rows = jnp.dot(attn_in, qkv_full, preferred_element_type=F32)
    query_raw, key_raw, value_raw = jnp.split(qkv_rows, 3, axis=-1)

    def scaled_query(query_input, log_scale):
        return unit_rows(query_input.reshape(row_count, -1, HDIM)) * jnp.exp(log_scale)[:, None]

    def key_unit_rows(key_input):
        return unit_rows(key_input.reshape(row_count, -1, HDIM))

    query_low = scaled_query(query_raw, head_scale).astype(BF).reshape(row_count, model_width)
    key_low = key_unit_rows(key_raw).astype(BF).reshape(row_count, model_width)
    value_low = value_raw.astype(BF)
    head_pieces = (
        split_heads(query_low, image_count, seq_len),
        split_heads(key_low, image_count, seq_len),
        split_heads(value_low, image_count, seq_len),
    )
    attended_blocks, log_totals = lax.map(partial(attend_forward, allowed=allowed), head_pieces)
    attended = join_heads(attended_blocks, image_count, seq_len).astype(BF)
    projected = jnp.dot(attended, out_full, preferred_element_type=F32).reshape(
        image_count, seq_len, model_width
    )
    residual = inputs + gate_one[:, None, :] * projected
    mlp_in = (
        modulate(residual, scale_two, shift_two).astype(BF).reshape(row_count, model_width)
    )
    grad_out = cotangent.astype(F32) * live_mask
    grad_mlp = (gate_two[:, None, :] * grad_out).astype(BF).reshape(row_count, model_width)

    mlp_out, grad_mlp_in, up_grad, down_grad, up_bias_grad = mlp(
        mlp_in, grad_mlp, mlp_full, hidden_order(up_bias_full)
    )
    mlp_out = mlp_out.reshape(image_count, seq_len, model_width)
    grad_mlp_in = grad_mlp_in.reshape(image_count, seq_len, model_width)
    down_own = scatter_rows(down_grad, count, me)
    up_own = scatter_rows(up_grad, count, me)
    block_out = ((residual + gate_two[:, None, :] * mlp_out) * live_mask).astype(BF)
    gate_two_grad = jnp.sum(grad_out * mlp_out, axis=1)
    second_back = jax.vjp(modulate, residual, scale_two, shift_two)[1]
    grad_resid_part, scale_two_grad, shift_two_grad = second_back(grad_mlp_in)
    grad_resid = grad_out + grad_resid_part
    gate_one_grad = jnp.sum(grad_resid * projected, axis=1)
    grad_proj = (gate_one[:, None, :] * grad_resid).astype(BF).reshape(row_count, model_width)
    out_grad = jnp.einsum("rd,re->de", attended, grad_proj, preferred_element_type=F32)
    grad_attended = jnp.einsum("re,de->rd", grad_proj, out_full, preferred_element_type=F32).astype(
        BF
    )
    grad_blocks = lax.map(
        partial(attend_backward, allowed=allowed),
        head_pieces + (split_heads(grad_attended, image_count, seq_len), log_totals),
    )
    grad_query_scaled = join_heads(grad_blocks[0], image_count, seq_len)
    grad_key_unit = join_heads(grad_blocks[1], image_count, seq_len)
    grad_values = join_heads(grad_blocks[2], image_count, seq_len)
    query_back = jax.vjp(scaled_query, query_raw, head_scale)[1]
    grad_query_raw, head_scale_part = query_back(grad_query_scaled.reshape(row_count, -1, HDIM))
    key_back = jax.vjp(key_unit_rows, key_raw)[1]
    grad_key_raw = key_back(grad_key_unit.reshape(row_count, -1, HDIM))[0]
    grad_qkv = jnp.concatenate([grad_query_raw, grad_key_raw, grad_values], axis=-1).astype(BF)
    qkv_grad = jnp.einsum("rd,re->de", attn_in, grad_qkv, preferred_element_type=F32)
    attn_own = scatter_rows(
        jnp.concatenate([qkv_grad.astype(BF), out_grad.astype(BF)], axis=1), count, me
    )
    grad_attn_in = jnp.einsum("re,de->rd", grad_qkv, qkv_full, preferred_element_type=F32).reshape(
        image_count, seq_len, model_width
    )
    first_back = jax.vjp(modulate, inputs, scale_one, shift_one)[1]
    grad_token_part, scale_one_grad, shift_one_grad = first_back(grad_attn_in)
    input_grad = grad_resid + grad_token_part
    grad_modul = jnp.concatenate(
        [
            gate_one_grad,
            gate_two_grad,
            scale_one_grad,
            scale_two_grad,
            shift_one_grad,
            shift_two_grad,
        ],
        axis=-1,
    ).astype(BF)
    bias_high, bias_low = split_low(hidden_back(up_bias_grad).reshape(count, -1))
    head_high, head_low = split_low(head_scale_part)
    heads = head_scale.shape[0]
    common = jnp.concatenate([grad_modul.reshape(-1), head_high, head_low])
    small = jnp.concatenate(
        [jnp.broadcast_to(common[None, :], (count, common.shape[0])), bias_high, bias_low], axis=1
    )
    small = lax.all_to_all(small, AXES, 0, 0, tiled=True)
    modul_cols = image_count * 6 * model_width
    grad_modul_all = small[:, :modul_cols].reshape(count * image_count, 6 * model_width)
    tail = jnp.sum(small[:, modul_cols:].astype(F32), axis=0)
    head_scale_grad = tail[:heads] + tail[heads : 2 * heads]
    tail = tail[2 * heads :].reshape(2, -1)
    up_bias_own = tail[0] + tail[1]
    ada_bias_own = jnp.sum(
        lax.dynamic_slice_in_dim(grad_modul_all, me * bias_own, bias_own, axis=1).astype(F32), axis=0
    )
    ada_own = lax.dot_general(
        cond_act, grad_modul_all, (((0,), (0,)), ((), ())), preferred_element_type=F32
    )
    grad_cond_act = lax.dot_general(
        grad_modul_all, ada_weight, (((1,), (1,)), ((), ())), preferred_element_type=F32
    )
    grad_condition = jax.vjp(jax.nn.silu, condition)[1](grad_cond_act)[0]
    table_own = lax.dot_general(
        onehot.astype(F32),
        grad_condition,
        (((0,), (0,)), ((), ())),
        precision=lax.Precision.HIGHEST,
        preferred_element_type=F32,
    )
    qkv_own = attn_own[:, : 3 * model_width]
    out_own = attn_own[:, 3 * model_width :]
    up_own = hidden_back(up_own)
    down_own = jnp.swapaxes(down_own.reshape(own, ratio, model_width), 0, 1).reshape(
        ratio * own, model_width
    )
    return (
        block_out,
        input_grad,
        table_own,
        ada_own,
        ada_bias_own,
        qkv_own,
        head_scale_grad,
        out_own,
        up_own,
        up_bias_own,
        down_own,
    )


def solution(mesh):
    count = mesh.shape["wide"] * mesh.shape["narrow"]
    both = AXES
    in_specs = (
        P(both, None, None),
        P(both),
        P(both),
        P(None, both),
        P(both, None),
        P(both),
        P(both, None),
        P(),
        P(both, None),
        P(both, None),
        P(both),
        P(both, None),
        P(both, None, None),
    )
    out_specs = (
        P(both, None, None),
        P(both, None, None),
        P(None, both),
        P(both, None),
        P(both),
        P(both, None),
        P(),
        P(both, None),
        P(both, None),
        P(both),
        P(both, None),
    )
    return jax.shard_map(
        partial(per_device, count=count),
        mesh=mesh,
        in_specs=in_specs,
        out_specs=out_specs,
        check_vma=False,
    )
```

```python
from functools import partial

import jax
import jax.numpy as jnp
import numpy as np
from jax import lax
from jax.experimental import pallas as pl
from jax.experimental.pallas import tpu as pltpu
from jax.sharding import PartitionSpec as P

HDIM = 64
SCALES = 10
AXES = ("wide", "narrow")
BF = jnp.bfloat16
F32 = jnp.float32

scale_sides = (1, 2, 3, 4, 5, 6, 8, 10, 13, 16)


def position_scale(scale_count):
    return np.concatenate(
        [
            np.full(side_size * side_size, level_index, dtype=np.int32)
            for level_index, side_size in enumerate(scale_sides[:scale_count])
        ]
    )


BLOCKS = 32
LEVEL_ENDS = np.cumsum(np.square(np.array(scale_sides))).astype(np.int32)
LAST = (((1,), (1,)), ((), ()))
FIRST = (((0,), (0,)), ((), ()))
PARAMS = pltpu.CompilerParams(vmem_limit_bytes=58 << 20)


def dot(left, right, dims=(((1,), (0,)), ((), ()))):
    return lax.dot_general(left, right, dims, preferred_element_type=F32)


def split_low(value):
    high = value.astype(BF)
    return high, (value - high.astype(F32)).astype(BF)


def row_chunks(total, step=80):
    return [slice(i, min(i + step, total)) for i in range(0, total, step)]


def norm_parts(value):
    centred = value - jnp.mean(value, axis=-1, keepdims=True)
    inverse = lax.rsqrt(jnp.mean(centred * centred, axis=-1, keepdims=True) + 1e-06)
    return centred * inverse, inverse


def cost(flops, read, exps=0, scale=20):
    return pl.CostEstimate(flops=int(scale * flops), bytes_accessed=int(scale * read), transcendentals=int(scale * exps))


def whole(shape):
    return pl.BlockSpec(shape, lambda *_: (0,) * len(shape))


def fill(dst, code, own, other, block):
    for m in range(own.shape[0]):
        at = code[m]
        dst[pl.ds(pl.multiple_of(at * block, block), block), :] = own[m]
        at = at ^ 1
        dst[pl.ds(pl.multiple_of(at * block, block), block), :] = other[m]


def halves_of(value, core, count=None):
    rows, cols = value.shape
    block = rows // (count or BLOCKS)
    cut = value.reshape(rows // (2 * block), 2, block, cols)
    even, odd = cut[:, 0], cut[:, 1]
    return (
        jnp.where(core == 0, even, odd).astype(BF),
        jnp.where(core == 0, odd, even).astype(BF),
    )


def qkv_body(
    code_ref, x_ref, mod_ref, own_a, other_a, own_b, other_b, gain_ref, seg_ref,
    attn_ref, out_ref, inv_ref, w_ref,
):
    step = pl.program_id(0)
    block = own_a.shape[1]

    @pl.when(step == 0)
    def _():
        for rows in row_chunks(x_ref.shape[0]):
            unit, _ = norm_parts(x_ref[rows, :].astype(F32))
            attn_ref[rows, :] = (unit * (1.0 + mod_ref[2:3, :]) + mod_ref[4:5, :]).astype(BF)

    @pl.when(step < 2)
    def _():
        fill(w_ref, code_ref.at[0], own_a, other_a, block)
        raw = dot(attn_ref[...], w_ref[...])
        seg = seg_ref[...]
        high, low = split_low(raw * raw)
        inverse = lax.rsqrt(dot(high, seg) + dot(low, seg) + 1e-06)
        high, low = split_low(inverse)
        spread = dot(high, seg, LAST) + dot(low, seg, LAST)
        gain = jnp.where(step == 0, gain_ref[...], 1.0)
        out_ref[...] = (raw * spread * gain).astype(BF)
        inv_ref[...] = spread

    @pl.when(step >= 2)
    def _():
        fill(w_ref, code_ref.at[1], own_b, other_b, block)

    @pl.when(step == 2)
    def _():
        out_ref[...] = dot(attn_ref[...], w_ref[...]).astype(BF)


def qkv_rows(x, mod, pieces, gain, seg):
    tokens, width = x.shape
    code, own_a, other_a, own_b, other_b = pieces
    part = (own_a.shape[0], own_a.shape[1], width)
    first = pl.BlockSpec(part, lambda n: (0, 0, jnp.minimum(n, 1)))
    second = pl.BlockSpec(part, lambda n: (0, 0, jnp.maximum(n - 2, 0)))
    return pl.pallas_call(
        qkv_body,
        grid=(4,),
        in_specs=[
            pl.BlockSpec(memory_space=pltpu.SMEM),
            whole((tokens, width)),
            whole(mod.shape),
            first,
            first,
            second,
            second,
            whole(gain.shape),
            whole(seg.shape),
        ],
        out_specs=[
            whole((tokens, width)),
            pl.BlockSpec((tokens, width), lambda n: (0, jnp.minimum(n, 2))),
            pl.BlockSpec((tokens, width), lambda n: (0, jnp.minimum(n, 1))),
            pl.BlockSpec((width, width), lambda n: (0, n)),
        ],
        out_shape=[
            jax.ShapeDtypeStruct((tokens, width), BF),
            jax.ShapeDtypeStruct((tokens, 3 * width), BF),
            jax.ShapeDtypeStruct((tokens, 2 * width), F32),
            jax.ShapeDtypeStruct((width, 4 * width), BF),
        ],
        compiler_params=PARAMS,
        cost_estimate=cost(6 * tokens * width * width, 16 * tokens * width + 16 * width * width, 0, 1),
        name="qkv",
    )(code, x, mod, own_a, other_a, own_b, other_b, gain, seg)


def attend_body(q_ref, k_ref, v_ref, start_ref, out_ref, low_ref, inv_ref):
    q, k, v = q_ref[...], k_ref[...], v_ref[...]
    lane = lax.broadcasted_iota(jnp.int32, q.shape, 1)
    zero = jnp.zeros_like(q)
    one = jnp.ones_like(q)
    tokens = q.shape[0]
    queries = [jnp.where(lane < HDIM, q, zero), jnp.where(lane >= HDIM, q, zero)]
    values = [
        jnp.where(lane < HDIM, v, jnp.where(lane == HDIM, one, zero)),
        jnp.where(lane >= HDIM, v, jnp.where(lane == 0, one, zero)),
    ]
    for first, last, keys in ((0, 240, 256), (240, 416, 432), (416, tokens, tokens)):
        row = lax.broadcasted_iota(jnp.int32, (last - first, keys), 0) + first
        seen = row >= start_ref[:, :keys]
        tiles, sums = [], []
        for h in range(2):
            score = dot(queries[h][first:last], k[:keys], LAST)
            weight = jnp.where(seen, jnp.exp(score), 0.0).astype(BF)
            tile = dot(weight, values[h][:keys])
            inverse = 1.0 / tile[:, HDIM * (1 - h) : HDIM * (1 - h) + 1]
            tiles.append(tile * inverse)
            sums.append(jnp.broadcast_to(inverse, tile.shape))
        left = lane[first:last] < HDIM
        high, low = split_low(jnp.where(left, tiles[0], tiles[1]))
        out_ref[first:last, :] = high
        low_ref[first:last, :] = low
        inv_ref[first:last, :] = jnp.where(left, sums[0], sums[1])


def attend(qkv, start):
    tokens = qkv.shape[0]
    pairs = qkv.shape[1] // (6 * HDIM)
    pair = lambda base: pl.BlockSpec((tokens, 2 * HDIM), lambda p: (0, base + p))
    return pl.pallas_call(
        attend_body,
        grid=(pairs,),
        in_specs=[pair(0), pair(pairs), pair(2 * pairs), whole(start.shape)],
        out_specs=[pair(0), pair(0), pair(0)],
        out_shape=[
            jax.ShapeDtypeStruct((tokens, 2 * HDIM * pairs), BF),
            jax.ShapeDtypeStruct((tokens, 2 * HDIM * pairs), BF),
            jax.ShapeDtypeStruct((tokens, 2 * HDIM * pairs), F32),
        ],
        compiler_params=PARAMS,
        cost_estimate=cost(
            16 * pairs * tokens * tokens * HDIM, 20 * tokens * HDIM * pairs, 2 * pairs * tokens * tokens, 1
        ),
        name="attend",
    )(qkv, qkv, qkv, start)


def attend_back_body(
    q_ref, k_ref, v_ref, g_ref, att_ref, low_ref, inv_ref, rq_ref, rk_ref, gain_ref, limit_ref,
    grad_ref, hs_ref, acc_q, acc_k, acc_v,
):
    q, k, v = q_ref[...], k_ref[...], v_ref[...]
    tokens = q.shape[0]
    lane = lax.broadcasted_iota(jnp.int32, q.shape, 1)
    zero, one = jnp.zeros_like(q), jnp.ones_like(q)
    left = lane < HDIM

    def head_sums(value):
        first = jnp.sum(jnp.where(left, value, 0.0), axis=1, keepdims=True)
        second = jnp.sum(jnp.where(left, 0.0, value), axis=1, keepdims=True)
        return first, second

    scaled = (g_ref[...].astype(F32) * inv_ref[...]).astype(BF)
    fine = att_ref[...].astype(F32) + low_ref[...].astype(F32)
    inner = head_sums(scaled.astype(F32) * fine)
    acc_q[...] = jnp.zeros_like(acc_q)
    for h in range(2):
        mine = left if h == 0 else lane >= HDIM
        spare = HDIM * (1 - h)
        q_own = jnp.where(mine, q, zero)
        k_own = jnp.where(mine, k, zero)
        g_own = jnp.where(mine, scaled, zero)
        high, low = split_low(-inner[h])
        wide = q.shape
        g_more = jnp.where(
            lane == spare,
            jnp.broadcast_to(high, wide),
            jnp.where(lane == spare + 1, jnp.broadcast_to(low, wide), g_own),
        )
        v_more = jnp.where(mine, v, jnp.where((lane >= spare) & (lane < spare + 2), one, zero))
        for first, last, row in ((0, 256, 0), (256, 432, 128), (432, tokens, 384)):
            score = dot(k[first:last], q_own[row:], LAST)
            key = lax.broadcasted_iota(jnp.int32, score.shape, 0) + first
            weight = jnp.where(key < limit_ref[:, row:], jnp.exp(score), 0.0).astype(BF)
            slope = dot(v_more[first:last], g_more[row:], LAST)
            slope = (weight.astype(F32) * slope).astype(BF)
            dv = dot(weight, g_own[row:])
            dk = dot(slope, q_own[row:])
            if h == 0:
                acc_v[first:last, :] = dv
                acc_k[first:last, :] = dk
            else:
                acc_v[first:last, :] += dv
                acc_k[first:last, :] += dk
            acc_q[row:, :] += dot(slope, k_own[first:last], FIRST)
    gain = gain_ref[...]
    dq, dk = acc_q[...], acc_k[...]
    q, k = q.astype(F32), k.astype(F32)
    along = dq * q
    first, second = head_sums(along)
    grad_ref[0] = (
        rq_ref[...] * (dq * gain - q * (jnp.where(left, first, second) / gain))
    ).astype(BF)
    hs_ref[...] = jnp.broadcast_to(jnp.sum(along, axis=0, keepdims=True), hs_ref.shape)
    first, second = head_sums(dk * k)
    grad_ref[1] = (rk_ref[...] * (dk - k * jnp.where(left, first, second))).astype(BF)
    grad_ref[2] = acc_v[...].astype(BF)


def attend_back(qkv, grad, attended, low, inverse, norms, gain, limit, base, some):
    tokens = qkv.shape[0]
    pairs = qkv.shape[1] // (6 * HDIM)
    pair = lambda at: pl.BlockSpec((tokens, 2 * HDIM), lambda p: (0, at + base + p))
    return pl.pallas_call(
        attend_back_body,
        grid=(some,),
        in_specs=[
            pair(0),
            pair(pairs),
            pair(2 * pairs),
            pair(0),
            pair(0),
            pair(0),
            pair(0),
            pair(0),
            pair(pairs),
            pl.BlockSpec((1, 2 * HDIM), lambda p: (0, base + p)),
            whole(limit.shape),
        ],
        out_specs=[
            pl.BlockSpec((3, tokens, 2 * HDIM), lambda p: (0, 0, p)),
            pl.BlockSpec((8, 2 * HDIM), lambda p: (0, p)),
        ],
        out_shape=[
            jax.ShapeDtypeStruct((3, tokens, 2 * HDIM * some), BF),
            jax.ShapeDtypeStruct((8, 2 * HDIM * some), F32),
        ],
        scratch_shapes=[pltpu.VMEM((tokens, 2 * HDIM), F32)] * 3,
        compiler_params=PARAMS,
        cost_estimate=cost(
            40 * some * tokens * tokens * HDIM, 60 * tokens * HDIM * some, 2 * some * tokens * tokens
        ),
        name="attend_back",
    )(qkv, qkv, qkv, grad, attended, low, inverse, norms, norms, gain, limit)


def project_body(live_ref, x_ref, att_ref, w_ref, mod_ref, cot_ref, proj_ref, mlp_ref, grad_ref):
    proj_ref[...] = dot(att_ref[...], w_ref[...])
    for rows in row_chunks(x_ref.shape[0]):
        residual = x_ref[rows, :].astype(F32) + mod_ref[0:1, :] * proj_ref[rows, :]
        unit, _ = norm_parts(residual)
        mlp_ref[rows, :] = (unit * (1.0 + mod_ref[3:4, :]) + mod_ref[5:6, :]).astype(BF)
        at = lax.broadcasted_iota(jnp.int32, residual.shape, 0) + rows.start
        live = jnp.where(at < live_ref[0], 1.0, 0.0)
        grad_ref[rows, :] = (mod_ref[1:2, :] * (cot_ref[rows, :].astype(F32) * live)).astype(BF)


def project(live, x, attended, w_vo, mod, cot):
    tokens, width = x.shape
    full = whole((tokens, width))
    return pl.pallas_call(
        project_body,
        grid=(1,),
        in_specs=[
            pl.BlockSpec(memory_space=pltpu.SMEM),
            full,
            full,
            pl.BlockSpec((width, width), lambda _: (0, 3)),
            whole(mod.shape),
            full,
        ],
        out_specs=[full] * 3,
        out_shape=[jax.ShapeDtypeStruct((tokens, width), t) for t in (F32, BF, BF)],
        compiler_params=PARAMS,
        cost_estimate=cost(2 * tokens * width * width, 14 * tokens * width + 2 * width * width, 0, 1),
        name="project",
    )(live, x, attended, w_vo, mod, cot)


def residual_back_body(
    live_ref, x_ref, proj_ref, out_ref, gx_ref, cot_ref, mod_ref, w_ref,
    block_ref, resid_ref, gatt_ref, gproj, sums_ref,
):
    totals = [0.0] * 4
    for rows in row_chunks(x_ref.shape[0]):
        proj, mlp_out, g = proj_ref[rows, :], out_ref[rows, :], gx_ref[rows, :]
        residual = x_ref[rows, :].astype(F32) + mod_ref[0:1, :] * proj
        at = lax.broadcasted_iota(jnp.int32, residual.shape, 0) + rows.start
        live = jnp.where(at < live_ref[0], 1.0, 0.0)
        block_ref[rows, :] = ((residual + mod_ref[1:2, :] * mlp_out) * live).astype(BF)
        grad_out = cot_ref[rows, :].astype(F32) * live
        unit, inverse = norm_parts(residual)
        dn = g * (1.0 + mod_ref[3:4, :])
        mean_dn = jnp.mean(dn, axis=-1, keepdims=True)
        mean_in = jnp.mean(dn * unit, axis=-1, keepdims=True)
        grad_resid = grad_out + inverse * (dn - mean_dn - unit * mean_in)
        resid_ref[rows, :] = grad_resid
        gproj[rows, :] = (mod_ref[0:1, :] * grad_resid).astype(BF)
        for i, part in enumerate((grad_resid * proj, grad_out * mlp_out, g * unit, g)):
            totals[i] = totals[i] + jnp.sum(part, axis=0, keepdims=True)
    for i in range(4):
        sums_ref[i : i + 1, :] = totals[i]
    sums_ref[4:, :] = jnp.zeros((4, sums_ref.shape[1]), F32)
    gatt_ref[...] = dot(gproj[...], w_ref[...], LAST).astype(BF)


def residual_back(live, x, proj, mlp_out, gx, cot, mod, weights):
    tokens, width = x.shape
    full = whole((tokens, width))
    return pl.pallas_call(
        residual_back_body,
        grid=(1,),
        in_specs=[
            pl.BlockSpec(memory_space=pltpu.SMEM),
            full,
            full,
            full,
            full,
            full,
            whole(mod.shape),
            pl.BlockSpec((width, width), lambda _: (0, 3)),
        ],
        out_specs=[full, full, full, full, whole((8, width))],
        out_shape=[jax.ShapeDtypeStruct((tokens, width), t) for t in (BF, F32, BF, BF)]
        + [jax.ShapeDtypeStruct((8, width), F32)],
        compiler_params=PARAMS,
        cost_estimate=cost(2 * tokens * width * width, 28 * tokens * width + 4 * width * width),
        name="residual_back",
    )(live, x, proj, mlp_out, gx, cot, mod, weights)


def weight_grad_body(core_ref, x_ref, g_ref, att_ref, proj_ref, keep_a, send_a, keep_b, send_b):
    step = pl.program_id(0)
    core = core_ref[0]

    @pl.when(step < 2)
    def _():
        keep_a[...], send_a[...] = halves_of(dot(x_ref[...], g_ref[0], FIRST), core)

    @pl.when(step == 2)
    def _():
        keep_b[...], send_b[...] = halves_of(dot(x_ref[...], g_ref[0], FIRST), core)

    @pl.when(step == 3)
    def _():
        keep_b[...], send_b[...] = halves_of(dot(att_ref[...], proj_ref[...], FIRST), core)


def weight_grad(core, x, g, attended, grad_proj):
    tokens, width = x.shape
    full = whole((tokens, width))
    part = (BLOCKS // 2, width // BLOCKS, width)
    first = pl.BlockSpec(part, lambda n: (0, 0, jnp.minimum(n, 1)))
    second = pl.BlockSpec(part, lambda n: (0, 0, jnp.maximum(n - 2, 0)))
    return pl.pallas_call(
        weight_grad_body,
        grid=(4,),
        in_specs=[
            pl.BlockSpec(memory_space=pltpu.SMEM),
            full,
            pl.BlockSpec((1, tokens, width), lambda n: (jnp.minimum(n, 2), 0, 0)),
            full,
            full,
        ],
        out_specs=[first, first, second, second],
        out_shape=[jax.ShapeDtypeStruct(part[:2] + (2 * width,), BF)] * 4,
        compiler_params=PARAMS,
        cost_estimate=cost(8 * tokens * width * width, 12 * tokens * width + 8 * width * width),
        name="weight_grad",
    )(core, x, g, attended, grad_proj)


def input_back_body(x_ref, resid_ref, mod_ref, g_ref, w_ref, out_ref, sums_ref):
    step = pl.program_id(0)
    part = dot(g_ref[0], w_ref[...], LAST)

    @pl.when(step == 0)
    def _():
        out_ref[...] = part

    @pl.when(step > 0)
    def _():
        out_ref[...] += part

    @pl.when(step == 2)
    def _():
        totals = [0.0] * 2
        for rows in row_chunks(x_ref.shape[0]):
            g = out_ref[rows, :]
            unit, inverse = norm_parts(x_ref[rows, :].astype(F32))
            dn = g * (1.0 + mod_ref[2:3, :])
            mean_dn = jnp.mean(dn, axis=-1, keepdims=True)
            mean_in = jnp.mean(dn * unit, axis=-1, keepdims=True)
            out_ref[rows, :] = resid_ref[rows, :] + inverse * (dn - mean_dn - unit * mean_in)
            for i, part in enumerate((g * unit, g)):
                totals[i] = totals[i] + jnp.sum(part, axis=0, keepdims=True)
        for i in range(2):
            sums_ref[i : i + 1, :] = totals[i]
        sums_ref[2:, :] = jnp.zeros((6, x_ref.shape[1]), F32)


def input_back(x, resid, mod, g, weights):
    tokens, width = x.shape
    full = whole((tokens, width))
    return pl.pallas_call(
        input_back_body,
        grid=(3,),
        in_specs=[
            full,
            full,
            whole(mod.shape),
            pl.BlockSpec((1, tokens, width), lambda n: (n, 0, 0)),
            pl.BlockSpec((width, width), lambda n: (0, n)),
        ],
        out_specs=[full, whole((8, width))],
        out_shape=[
            jax.ShapeDtypeStruct((tokens, width), F32),
            jax.ShapeDtypeStruct((8, width), F32),
        ],
        compiler_params=PARAMS,
        cost_estimate=cost(6 * tokens * width * width, 16 * tokens * width + 6 * width * width),
        name="input_back",
    )(x, resid, mod, g, weights)


def mlp_body(
    info_ref, x_ref, g_ref, own_a, other_a, own_b, other_b, bias_ref, *refs, first
):
    if first:
        out_ref, gx_ref, keep_a, send_a, keep_b, send_b, bias_g, up_w, down_w = refs
    else:
        out_in, gx_in, out_ref, gx_ref, keep_a, send_a, keep_b, send_b, bias_g, up_w, down_w = refs
    core = info_ref[2, 0]
    block = own_a.shape[1]

    @pl.when(pl.program_id(0) == 0)
    def _():
        out_ref[...] = jnp.zeros_like(out_ref) if first else out_in[...]
        gx_ref[...] = jnp.zeros_like(gx_ref) if first else gx_in[...]

    step = pl.program_id(0)
    size = up_w.shape[1]
    per = down_w.shape[0] // size
    fill(up_w, info_ref.at[0], own_a, other_a, block)

    @pl.when(step % per == 0)
    def _():
        fill(down_w, info_ref.at[1], own_b, other_b, block)

    root = np.float32(np.sqrt(2.0 / np.pi))
    x, g, up = x_ref[...], g_ref[...], up_w[...]
    down = down_w[pl.ds(pl.multiple_of(step % per * size, size), size), :]
    hidden = dot(x, up) + bias_ref[...]
    square = hidden * hidden
    bend = jnp.tanh(root * hidden * (1.0 + 0.044715 * square))
    act = (0.5 * hidden * (1.0 + bend)).astype(BF)
    out_ref[...] += dot(act, down)
    slope = 0.5 * (1.0 + bend) + 0.5 * hidden * (1.0 - bend * bend) * root * (
        1.0 + (3 * 0.044715) * square
    )
    grad_hidden = (dot(g, down, LAST) * slope).astype(BF)
    bias_g[...] = jnp.sum(grad_hidden.astype(F32), axis=0, keepdims=True)
    gx_ref[...] += dot(grad_hidden, up, LAST)
    keep_b[...], send_b[...] = halves_of(dot(act, g, FIRST), core, BLOCKS // per)
    keep_a[...], send_a[...] = halves_of(dot(x, grad_hidden, FIRST), core)


def mlp(info, x, g, pieces, bias, at, carried=None):
    tokens, width = x.shape
    block, per = 512, width // 512
    lead, rows = BLOCKS // 2, width // BLOCKS
    part_a = pl.BlockSpec((lead, rows, block), lambda f: (0, 0, f))
    part_b = pl.BlockSpec((lead, rows, width), lambda f: (0, 0, f // per))
    if len(pieces) == 5:
        matrices = pieces[1:]
        total = matrices[0].shape[2]
        sources = [part_a, part_a, part_b, part_b]
    else:
        matrices = [pieces[0].reshape(lead, 2, rows, -1)] * 4
        total = matrices[0].shape[3] // 2
        skip = total // width
        sources = [
            pl.BlockSpec((lead, None, rows, block), lambda f: (0, 0, 0, f)),
            pl.BlockSpec((lead, None, rows, block), lambda f: (0, 1, 0, f)),
            pl.BlockSpec((lead, None, rows, width), lambda f: (0, 0, 0, skip + f // per)),
            pl.BlockSpec((lead, None, rows, width), lambda f: (0, 1, 0, skip + f // per)),
        ]
    steps = total // block
    grad_b = pl.BlockSpec((lead // per, rows, width), lambda f: (f % per, 0, f // per))
    single = pl.BlockSpec((tokens, width), lambda f: (0, 0), pipeline_mode=pl.Buffered(1))
    carried = () if carried is None else tuple(carried)
    return pl.pallas_call(
        partial(mlp_body, first=not carried),
        grid=(steps,),
        in_specs=[pl.BlockSpec(memory_space=pltpu.SMEM), single, single]
        + sources
        + [pl.BlockSpec((1, block), lambda f: (0, at * per + f))]
        + [single] * len(carried),
        out_specs=[single, single, part_a, part_a, grad_b, grad_b]
        + [pl.BlockSpec((1, block), lambda f: (0, f))],
        out_shape=[jax.ShapeDtypeStruct((tokens, width), F32)] * 2
        + [jax.ShapeDtypeStruct((lead, rows, total), BF)] * 4
        + [jax.ShapeDtypeStruct((1, total), F32)],
        scratch_shapes=[pltpu.VMEM((width, block), BF), pltpu.VMEM((width, width), BF)],
        input_output_aliases={8 + i: i for i in range(len(carried))},
        compiler_params=PARAMS,
        cost_estimate=cost(
            12 * tokens * width * total,
            (8 + 8 * len(carried)) * tokens * width + 8 * total * width,
            tokens * total,
            20 if carried else 0.3,
        ),
        name="mlp",
    )(info, x, g, *matrices, bias, *carried)


def fold_body(bit_ref, *refs, plan, out_count):
    ins, outs = refs[:-out_count], refs[-out_count:]
    for source, cols, bit, stride, out, column in plan:
        kept, came = ins[2 * source], ins[2 * source + 1]
        at_cols = slice(column, column + cols.stop - cols.start)
        if bit is None:
            outs[out][:, :, at_cols] = kept[:, :, cols].astype(F32) + came[:, :, cols].astype(F32)
            continue
        mine = bit_ref[bit]
        for m in range(kept.shape[0] // 2):
            base = m // stride * 2 * stride + m % stride
            for side, value in ((0, mine), (1, 1 - mine)):
                at = base + value * stride
                outs[out + side][m, :, at_cols] = (
                    kept[at, :, cols].astype(F32) + came[at, :, cols].astype(F32)
                ).astype(BF)


def fold(bits, parts, plan, outs, split=1, weight=0):
    def spec(shape):
        return pl.BlockSpec(tuple(shape[:2]) + (shape[2] // split,), lambda n: (0, 0, n))

    return pl.pallas_call(
        partial(fold_body, plan=plan, out_count=len(outs)),
        grid=(split,),
        in_specs=[pl.BlockSpec(memory_space=pltpu.SMEM)] + [spec(p.shape) for p in parts],
        out_specs=[spec(s) for s, _ in outs],
        out_shape=[jax.ShapeDtypeStruct(s, t) for s, t in outs],
        compiler_params=PARAMS,
        cost_estimate=cost(weight, 8),
        name="fold",
    )(bits, *parts)


def swap(block, count, mask):
    return lax.ppermute(block, AXES, [(i, i ^ mask) for i in range(count)])


def after(value, *others):
    return lax.optimization_barrier((value,) + others)


def join(block, came):
    return jnp.concatenate([block, came])


def codes(order, me):
    code = [0]
    for bit in order:
        code = code + [c | (1 << bit) for c in code]
    return jnp.asarray(np.array(code, np.int32)) ^ me


def gathered_pieces(full):
    rows, cols = full.shape
    cut = full.reshape(BLOCKS // 2, 2, rows // BLOCKS, 2, cols // 2)
    return [cut[:, i, :, j] for j in range(2) for i in range(2)]


def halve(pieces, axis, bit_value, count, mask):
    total = pieces[0]
    if len(pieces) > 1:
        total = (pieces[0].astype(F32) + pieces[1].astype(F32)).astype(BF)
    keep = lax.dynamic_index_in_dim(total, bit_value, axis, keepdims=False)
    send = lax.dynamic_index_in_dim(total, 1 - bit_value, axis, keepdims=False)
    return [keep, swap(send, count, mask)]


def scatter_rows(kept, send, count, me):
    grads = [jnp.stack(pair, axis=1).reshape(-1, pair[0].shape[2]) for pair in zip(kept, send)]
    grad = jnp.concatenate(grads, axis=1)
    rows, width = grad.shape
    bits = count.bit_length() - 1
    own = rows // count
    bit = [lax.rem(lax.div(me, np.int32(1 << b)), np.int32(2)) for b in range(bits)]
    part = [grad.reshape((2,) * bits + (own, width))]
    for b in range(bits):
        part = halve(part, bits - 1 - b, bit[b], count, 1 << b)
    return (part[0].astype(F32) + part[1].astype(F32)).reshape(own, width)


def tie(*groups):
    flat = lax.optimization_barrier(tuple(a for g in groups for a in g))
    for g in groups:
        g[:], flat = flat[: len(g)], flat[len(g) :]


def land(value, *moves):
    box = [value]
    tie(box, *[m.came for m in moves])
    return box[0]


def leave(value, *scatters):
    for s in scatters:
        s.add()
    box = [value]
    tie(box, *[s.send for s in scatters])
    for s in scatters:
        if s.done is None:
            s.start()
    return box[0]


class Gather:
    def __init__(self, shard, count):
        self.count = count
        self.block = shard[None]
        self.came = None

    def start_z(self, bit):
        self.came = [swap(self.block, self.count, 1 << bit)]

    def end_z(self):
        self.block = join(self.block, self.came[0])

    def start_xy(self, first, second):
        if not isinstance(self.block, list):
            half = self.block.shape[2] // 2
            self.block = [self.block[:, :, :half], self.block[:, :, half:]]
        self.came = [
            swap(b, self.count, 1 << bit) for b, bit in zip(self.block, (first, second))
        ]

    def end_xy(self):
        self.block = [join(b, c) for b, c in zip(self.block, self.came)]

    def start_core(self):
        self.came = [swap(b, self.count, 1) for b in self.block]

    def pieces(self, code):
        return (code, self.block[0], self.came[0], self.block[1], self.came[1])


class Scatter:
    def __init__(self, kept, send, bits, count, heavy=0):
        self.bits, self.count, self.heavy = bits, count, heavy
        self.kept, self.send = list(kept), list(send)
        self.left = 0
        self.done = None
        self.start()

    def start(self):
        masks = ([1] * len(self.send), (2, 4), (4, 2), (8,), (16,))[self.left]
        self.came = [swap(s, self.count, mask) for s, mask in zip(self.send, masks)]
        self.left += 1

    def add(self):
        parts = [p for pair in zip(self.kept, self.came) for p in pair]
        lead, own, width = self.kept[0].shape
        split = {1: 4, 2: 2}.get(self.left, 1)
        everything = slice(0, width // split)
        half = lambda cols: ((lead // 2, own, cols), BF)
        if self.left == 5:
            plan = ((0, everything, None, 1, 0, 0),)
            outs = [((lead, own, width), F32)]
        elif self.left == 1:
            plan, sums = [], [0, 0]
            for side in range(2):
                plan.append((side, everything, (1, 2)[side], (1, 2)[side], 2 * side, 0))
            outs = [half(width)] * 4
        elif self.left == 2:
            plan = tuple((i, everything, 2 - i, 1, 2 * i, 0) for i in range(2))
            outs = [half(width)] * 4
        elif self.left == 3:
            plan = tuple((i, everything, 3, 1, 0, i * width) for i in range(2))
            outs = [half(2 * width)] * 2
        else:
            plan = ((0, everything, 4, 1, 0, 0),)
            outs = [half(width)] * 2
        weight = self.heavy if self.left == 5 else 0
        outs = fold(self.bits, parts, tuple(plan), outs, split, weight)
        if self.left == 5:
            self.done, self.send = outs[0][0], list(outs)
        else:
            self.kept, self.send = list(outs[0::2]), list(outs[1::2])


def per_device(
    tokens,
    labels,
    stop_scale,
    class_table,
    ada_weight,
    ada_bias,
    qkv_weight,
    head_scale,
    out_weight,
    up_weight,
    up_bias,
    down_weight,
    cotangent,
    count,
):
    image_count, seq_len, model_width = tokens.shape
    row_count = image_count * seq_len
    me = lax.axis_index(AXES).astype(jnp.int32)
    levels = position_scale(SCALES)
    ends = jnp.asarray(LEVEL_ENDS)
    live = jnp.take(ends, stop_scale - 1).astype(jnp.int32)
    limit = jnp.asarray(LEVEL_ENDS[levels][None, :])
    start = jnp.asarray((LEVEL_ENDS - np.square(np.array(scale_sides)))[levels][None, :].astype(np.int32))
    class_count = class_table.shape[0]
    own = model_width // count
    ratio = down_weight.shape[0] // own
    hidden_width = up_weight.shape[1]

    def hidden_order(matrix):
        lead = matrix.shape[:-1]
        cut = matrix.reshape(lead + (count, ratio, own))
        return jnp.swapaxes(cut, -3, -2).reshape(lead + (hidden_width,))

    def hidden_back(matrix):
        lead = matrix.shape[:-1]
        cut = matrix.reshape(lead + (ratio, count, own))
        return jnp.swapaxes(cut, -3, -2).reshape(lead + (hidden_width,))

    down_wide = jnp.swapaxes(down_weight.reshape(ratio, own, model_width), 0, 1).reshape(
        own, hidden_width
    )
    half = hidden_width // 2
    up_order = hidden_order(up_weight)
    shards = [jnp.concatenate([qkv_weight, out_weight], axis=1)] + [
        jnp.concatenate([m[:, i : i + half] for m in (up_order, down_wide)], axis=1)
        for i in (0, half)
    ]
    quick = count == BLOCKS and own % 16 == 0
    plain = jnp.asarray(np.tile(np.arange(0, BLOCKS, 2, dtype=np.int32), (2, 1)))
    if quick:
        one, two = [Gather(s, count) for s in shards[:2]]
        orders = ((4, 3, 2, 1), (4, 3, 1, 2))
        code = jnp.stack([codes(o, me) for o in orders])
        bits = jnp.stack([lax.rem(lax.div(me, np.int32(1 << b)), np.int32(2)) for b in range(5)])
        one.start_z(4)
    else:
        wide = [lax.all_gather(s, AXES, axis=0, tiled=True) for s in shards]
        code = plain
        bits = jnp.zeros((5,), jnp.int32)
    core = bits[:1]
    info, info_plain = [
        jnp.concatenate([c, jnp.full((1, c.shape[1]), bits[0])]) for c in (code, plain)
    ]

    first_row = jnp.concatenate(
        [lax.div(labels, 32).astype(BF), lax.rem(labels, 32).astype(BF), up_bias]
    )
    rows = lax.all_to_all(
        jnp.broadcast_to(first_row[None, :], (count, first_row.shape[0])), AXES, 0, 0, tiled=True
    )
    labels_all = 32 * rows[:, 0].astype(jnp.int32) + rows[:, 1].astype(jnp.int32)
    up_bias_full = rows[:, 2:].astype(F32).reshape(1, hidden_width)
    onehot = labels_all[:, None] == jnp.arange(class_count, dtype=jnp.int32)[None, :]
    condition = jnp.dot(onehot.astype(BF), class_table, preferred_element_type=F32)
    cond_act = jax.nn.silu(condition).astype(BF)
    exponent = count.bit_length() - 1
    order = tuple(range(exponent - 1, -1, -1)) + (exponent,)
    backwards = cond_act.reshape((2,) * exponent + (own,)).transpose(order).reshape(count, own)
    modul_part = jnp.dot(backwards, ada_weight, preferred_element_type=F32)
    bias_own = ada_bias.shape[0]
    bias_row = lax.dynamic_update_slice(
        jnp.zeros((6 * model_width,), F32), ada_bias.astype(F32), (me * bias_own,)
    )
    part = modul_part + bias_row[None, :]
    if quick:
        part = land(part, one)
        one.end_z()
        one.start_z(3)
    bit_values = [lax.rem(lax.div(me, np.int32(1 << b)), np.int32(2)) for b in range(exponent)]
    for b in range(exponent):
        size = part.shape[0] // 2
        keep = lax.dynamic_slice_in_dim(part, bit_values[b] * size, size)
        send = lax.dynamic_slice_in_dim(part, (1 - bit_values[b]) * size, size)
        came = swap(send, count, 1 << b)
        if quick and b == 0:
            came = land(came, one)
            one.end_z()
            came, two.block = after(came, two.block)
            one.start_xy(2, 1)
            two.start_z(4)
        elif quick and b == 2:
            came = land(came, one, two)
            one.end_xy()
            two.end_z()
            came, last_shard = after(came, shards[2])
            last_full = lax.all_gather(last_shard, AXES, axis=0, tiled=True)
            one.start_xy(1, 2)
            two.start_z(3)
        part = keep + came
    mod = part.reshape(6, model_width)
    if quick:
        mod = land(mod, one, two)
        one.end_xy()
        two.end_z()
        one.start_core()
        two.start_xy(2, 1)
        mod = land(mod, one)
        pieces = one.pieces(code)
    else:
        pieces = (code, *gathered_pieces(wide[0]))
    heads = head_scale.shape[0]
    gain = jnp.repeat(jnp.exp(head_scale), HDIM)[None, :]
    seg = jnp.asarray(
        np.arange(model_width)[:, None] // HDIM == np.arange(128)[None, :], dtype=BF
    )
    x = tokens.reshape(row_count, model_width)
    cot = cotangent.reshape(row_count, model_width)

    attn_in, qkv, norms, weights = qkv_rows(x, mod, pieces, gain, seg)
    if quick:
        qkv = land(qkv, two)
        two.end_xy()
        qkv, *two.block = after(qkv, *two.block)
        two.start_xy(1, 2)
    attended, low, inverse = attend(qkv, start)
    projected, mlp_in, grad_mlp = project(live, x, attended, weights, mod, cot)
    if quick:
        mlp_in = land(mlp_in, two)
        two.end_xy()
        two.start_core()
    bias = hidden_order(up_bias_full)
    pieces = two.pieces(code) if quick else (wide[1],)
    *carried, keep_a, send_a, keep_b, send_b, bias_one = mlp(info, mlp_in, grad_mlp, pieces, bias, 0)
    kept_one, send_one = (keep_a, keep_b), (send_a, send_b)
    if quick:
        first = Scatter(kept_one, send_one, bits, count, 1 << 33)
        carried[0] = land(carried[0], first)
        carried[0] = leave(carried[0], first)
    pieces = (last_full if quick else wide[2],)
    mlp_out, grad_mlp_in, keep_a, send_a, keep_b, send_b, bias_two = mlp(
        info_plain, mlp_in, grad_mlp, pieces, bias, half // model_width, carried
    )
    kept_two, send_two = (keep_a, keep_b), (send_a, send_b)
    up_bias_grad = jnp.concatenate([bias_one, bias_two], axis=1)
    if quick:
        second = Scatter(kept_two, send_two, bits, count)
        mlp_out = land(mlp_out, first)
        mlp_out = leave(mlp_out, first)
    block_out, grad_resid, grad_attended, grad_proj, sums_two = residual_back(
        live, x, projected, mlp_out, grad_mlp_in, cot, mod, weights
    )
    if quick:
        grad_attended = land(grad_attended, first, second)
        grad_attended = leave(grad_attended, first, second)
    dqkv, head_sums = attend_back(
        qkv, grad_attended, attended, low, inverse, norms, gain, limit, 0, heads // 2
    )
    if quick:
        dqkv = land(dqkv, first, second)
        dqkv = leave(dqkv, first, second)
    head_scale_part = jnp.sum(head_sums[0].reshape(heads, HDIM), axis=1)
    keep_a, send_a, keep_b, send_b = weight_grad(core, attn_in, dqkv, attended, grad_proj)
    kept_three, send_three = (keep_a, keep_b), (send_a, send_b)
    if quick:
        third = Scatter(kept_three, send_three, bits, count)
        dqkv = land(dqkv, first, second)
        dqkv = leave(dqkv, first, second)
        dqkv = land(dqkv, third)
        dqkv = leave(dqkv, third)
    input_grad, sums_one = input_back(x, grad_resid, mod, dqkv, weights)
    if not quick:
        mlp_own = [scatter_rows(kept_one, send_one, count, me), scatter_rows(kept_two, send_two, count, me)]
        attn_own = scatter_rows(kept_three, send_three, count, me)
    block_out = block_out.reshape(tokens.shape)
    input_grad = input_grad.reshape(tokens.shape)
    grad_modul = jnp.concatenate(
        [sums_two[0], sums_two[1], sums_one[0], sums_two[2], sums_one[1], sums_two[3]]
    ).astype(BF)
    bias_high, bias_low = split_low(hidden_back(up_bias_grad).reshape(count, -1))
    head_high, head_low = split_low(head_scale_part)
    common = jnp.concatenate([grad_modul.reshape(-1), head_high, head_low])
    small = jnp.concatenate(
        [jnp.broadcast_to(common[None, :], (count, common.shape[0])), bias_high, bias_low], axis=1
    )
    small = lax.all_to_all(small, AXES, 0, 0, tiled=True)
    if quick:
        input_grad = land(input_grad, second, third)
        input_grad = leave(input_grad, second, third)
        input_grad = land(input_grad, second, third)
        input_grad = leave(input_grad, second, third)
        input_grad = land(input_grad, third)
        small, input_grad = after(small, input_grad)
        small = leave(small, third)
        third.add()
        mlp_own = [first.done, second.done]
        attn_own = third.done
    up_own = jnp.concatenate([m[:, :half] for m in mlp_own], axis=1)
    down_own = jnp.concatenate([m[:, half:] for m in mlp_own], axis=1)
    modul_cols = image_count * 6 * model_width
    grad_modul_all = small[:, :modul_cols].reshape(count * image_count, 6 * model_width)
    tail = jnp.sum(small[:, modul_cols:].astype(F32), axis=0)
    head_scale_grad = tail[:heads] + tail[heads : 2 * heads]
    tail = tail[2 * heads :].reshape(2, -1)
    up_bias_own = tail[0] + tail[1]
    ada_bias_own = jnp.sum(
        lax.dynamic_slice_in_dim(grad_modul_all, me * bias_own, bias_own, axis=1).astype(F32), axis=0
    )
    ada_own = lax.dot_general(
        cond_act, grad_modul_all, (((0,), (0,)), ((), ())), preferred_element_type=F32
    )
    grad_cond_act = lax.dot_general(
        grad_modul_all, ada_weight, (((1,), (1,)), ((), ())), preferred_element_type=F32
    )
    grad_condition = jax.vjp(jax.nn.silu, condition)[1](grad_cond_act)[0]
    table_own = lax.dot_general(
        onehot.astype(F32),
        grad_condition,
        (((0,), (0,)), ((), ())),
        precision=lax.Precision.HIGHEST,
        preferred_element_type=F32,
    )
    qkv_own = attn_own[:, : 3 * model_width]
    out_own = attn_own[:, 3 * model_width :]
    up_own = hidden_back(up_own)
    down_own = jnp.swapaxes(down_own.reshape(own, ratio, model_width), 0, 1).reshape(
        ratio * own, model_width
    )
    return (
        block_out,
        input_grad,
        table_own,
        ada_own,
        ada_bias_own,
        qkv_own,
        head_scale_grad,
        out_own,
        up_own,
        up_bias_own,
        down_own,
    )


def solution(mesh):
    count = mesh.shape["wide"] * mesh.shape["narrow"]
    both = AXES
    in_specs = (
        P(both, None, None),
        P(both),
        P(both),
        P(None, both),
        P(both, None),
        P(both),
        P(both, None),
        P(),
        P(both, None),
        P(both, None),
        P(both),
        P(both, None),
        P(both, None, None),
    )
    out_specs = (
        P(both, None, None),
        P(both, None, None),
        P(None, both),
        P(both, None),
        P(both),
        P(both, None),
        P(),
        P(both, None),
        P(both, None),
        P(both),
        P(both, None),
    )
    return jax.shard_map(
        partial(per_device, count=count),
        mesh=mesh,
        in_specs=in_specs,
        out_specs=out_specs,
        check_vma=False,
    )
```

```python
from functools import partial

import jax
import jax.numpy as jnp
import numpy as np
from jax import lax
from jax.experimental import pallas as pl
from jax.experimental.pallas import tpu as pltpu
from jax.sharding import PartitionSpec as P

HDIM = 64
SCALES = 10
AXES = ("wide", "narrow")
BF = jnp.bfloat16
F32 = jnp.float32

scale_sides = (1, 2, 3, 4, 5, 6, 8, 10, 13, 16)


def position_scale(scale_count):
    return np.concatenate(
        [
            np.full(side_size * side_size, level_index, dtype=np.int32)
            for level_index, side_size in enumerate(scale_sides[:scale_count])
        ]
    )


BLOCKS = 32
LEVEL_ENDS = np.cumsum(np.square(np.array(scale_sides))).astype(np.int32)
LAST = (((1,), (1,)), ((), ()))
FIRST = (((0,), (0,)), ((), ()))
PARAMS = pltpu.CompilerParams(vmem_limit_bytes=58 << 20)


def dot(left, right, dims=(((1,), (0,)), ((), ()))):
    return lax.dot_general(left, right, dims, preferred_element_type=F32)


def split_low(value):
    high = value.astype(BF)
    return high, (value - high.astype(F32)).astype(BF)


def row_chunks(total, step=80):
    return [slice(i, min(i + step, total)) for i in range(0, total, step)]


def norm_parts(value):
    centred = value - jnp.mean(value, axis=-1, keepdims=True)
    inverse = lax.rsqrt(jnp.mean(centred * centred, axis=-1, keepdims=True) + 1e-06)
    return centred * inverse, inverse


def cost(flops, read, exps=0, scale=20):
    return pl.CostEstimate(flops=int(scale * flops), bytes_accessed=int(scale * read), transcendentals=int(scale * exps))


def whole(shape):
    return pl.BlockSpec(shape, lambda *_: (0,) * len(shape))


def fill(dst, code, pairs, block):
    position = 0
    for own, other in pairs:
        for m in range(own.shape[0]):
            at = code[position]
            dst[pl.ds(pl.multiple_of(at * block, block), block), :] = own[m]
            at = at ^ 1
            dst[pl.ds(pl.multiple_of(at * block, block), block), :] = other[m]
            position += 1


def paired(refs):
    return list(zip(refs[0::2], refs[1::2]))


def halves_of(value, core, count=None):
    rows, cols = value.shape
    block = rows // (count or BLOCKS)
    cut = value.reshape(rows // (2 * block), 2, block, cols)
    even, odd = cut[:, 0], cut[:, 1]
    return (
        jnp.where(core == 0, even, odd).astype(BF),
        jnp.where(core == 0, odd, even).astype(BF),
    )


def qkv_body(code_ref, x_ref, mod_ref, gain_ref, seg_ref, *refs):
    *sources, attn_ref, out_ref, inv_ref, w_ref = refs
    half = len(sources) // 2
    first, second = paired(sources[:half]), paired(sources[half:])
    step = pl.program_id(0)
    block = x_ref.shape[1] // BLOCKS

    @pl.when(step == 0)
    def _():
        for rows in row_chunks(x_ref.shape[0]):
            unit, _ = norm_parts(x_ref[rows, :].astype(F32))
            attn_ref[rows, :] = (unit * (1.0 + mod_ref[2:3, :]) + mod_ref[4:5, :]).astype(BF)

    @pl.when(step < 2)
    def _():
        fill(w_ref, code_ref.at[0], first, block)
        raw = dot(attn_ref[...], w_ref[...])
        seg = seg_ref[...]
        high, low = split_low(raw * raw)
        inverse = lax.rsqrt(dot(high, seg) + dot(low, seg) + 1e-06)
        high, low = split_low(inverse)
        spread = dot(high, seg, LAST) + dot(low, seg, LAST)
        gain = jnp.where(step == 0, gain_ref[...], 1.0)
        out_ref[...] = (raw * spread * gain).astype(BF)
        inv_ref[...] = spread

    @pl.when(step >= 2)
    def _():
        fill(w_ref, code_ref.at[1], second, block)

    @pl.when(step == 2)
    def _():
        out_ref[...] = dot(attn_ref[...], w_ref[...]).astype(BF)


def qkv_rows(x, mod, pieces, gain, seg):
    tokens, width = x.shape
    code, first, second = pieces
    one = [
        pl.BlockSpec(a.shape[:2] + (width,), lambda n: (0, 0, jnp.minimum(n, 1))) for a in first
    ]
    two = [
        pl.BlockSpec(a.shape[:2] + (width,), lambda n: (0, 0, jnp.maximum(n - 2, 0)))
        for a in second
    ]
    return pl.pallas_call(
        qkv_body,
        grid=(4,),
        in_specs=[
            pl.BlockSpec(memory_space=pltpu.SMEM),
            whole((tokens, width)),
            whole(mod.shape),
            whole(gain.shape),
            whole(seg.shape),
            *one,
            *two,
        ],
        out_specs=[
            whole((tokens, width)),
            pl.BlockSpec((tokens, width), lambda n: (0, jnp.minimum(n, 2))),
            pl.BlockSpec((tokens, width), lambda n: (0, jnp.minimum(n, 1))),
            pl.BlockSpec((width, width), lambda n: (0, n)),
        ],
        out_shape=[
            jax.ShapeDtypeStruct((tokens, width), BF),
            jax.ShapeDtypeStruct((tokens, 3 * width), BF),
            jax.ShapeDtypeStruct((tokens, 2 * width), F32),
            jax.ShapeDtypeStruct((width, 4 * width), BF),
        ],
        compiler_params=PARAMS,
        cost_estimate=cost(6 * tokens * width * width, 16 * tokens * width + 16 * width * width, 0, 2),
        name="qkv",
    )(code, x, mod, gain, seg, *first, *second)


def attend_body(q_ref, k_ref, v_ref, start_ref, out_ref, low_ref, inv_ref):
    q, k, v = q_ref[...], k_ref[...], v_ref[...]
    lane = lax.broadcasted_iota(jnp.int32, q.shape, 1)
    zero = jnp.zeros_like(q)
    one = jnp.ones_like(q)
    tokens = q.shape[0]
    queries = [jnp.where(lane < HDIM, q, zero), jnp.where(lane >= HDIM, q, zero)]
    values = [
        jnp.where(lane < HDIM, v, jnp.where(lane == HDIM, one, zero)),
        jnp.where(lane >= HDIM, v, jnp.where(lane == 0, one, zero)),
    ]
    for first, last, keys in ((0, 240, 256), (240, 416, 432), (416, tokens, tokens)):
        row = lax.broadcasted_iota(jnp.int32, (last - first, keys), 0) + first
        seen = row >= start_ref[:, :keys]
        tiles, sums = [], []
        for h in range(2):
            score = dot(queries[h][first:last], k[:keys], LAST)
            weight = jnp.where(seen, jnp.exp(score), 0.0).astype(BF)
            tile = dot(weight, values[h][:keys])
            inverse = 1.0 / tile[:, HDIM * (1 - h) : HDIM * (1 - h) + 1]
            tiles.append(tile * inverse)
            sums.append(jnp.broadcast_to(inverse, tile.shape))
        left = lane[first:last] < HDIM
        high, low = split_low(jnp.where(left, tiles[0], tiles[1]))
        out_ref[first:last, :] = high
        low_ref[first:last, :] = low
        inv_ref[first:last, :] = jnp.where(left, sums[0], sums[1])


def attend(qkv, start):
    tokens = qkv.shape[0]
    pairs = qkv.shape[1] // (6 * HDIM)
    pair = lambda base: pl.BlockSpec((tokens, 2 * HDIM), lambda p: (0, base + p))
    return pl.pallas_call(
        attend_body,
        grid=(pairs,),
        in_specs=[pair(0), pair(pairs), pair(2 * pairs), whole(start.shape)],
        out_specs=[pair(0), pair(0), pair(0)],
        out_shape=[
            jax.ShapeDtypeStruct((tokens, 2 * HDIM * pairs), BF),
            jax.ShapeDtypeStruct((tokens, 2 * HDIM * pairs), BF),
            jax.ShapeDtypeStruct((tokens, 2 * HDIM * pairs), F32),
        ],
        compiler_params=PARAMS,
        cost_estimate=cost(
            16 * pairs * tokens * tokens * HDIM, 20 * tokens * HDIM * pairs, 2 * pairs * tokens * tokens, 0.02
        ),
        name="attend",
    )(qkv, qkv, qkv, start)


def attend_back_body(
    q_ref, k_ref, v_ref, g_ref, att_ref, low_ref, inv_ref, rq_ref, rk_ref, gain_ref, limit_ref,
    grad_ref, hs_ref, acc_q, acc_k, acc_v,
):
    q, k, v = q_ref[...], k_ref[...], v_ref[...]
    tokens = q.shape[0]
    lane = lax.broadcasted_iota(jnp.int32, q.shape, 1)
    zero, one = jnp.zeros_like(q), jnp.ones_like(q)
    left = lane < HDIM

    def head_sums(value):
        first = jnp.sum(jnp.where(left, value, 0.0), axis=1, keepdims=True)
        second = jnp.sum(jnp.where(left, 0.0, value), axis=1, keepdims=True)
        return first, second

    scaled = (g_ref[...].astype(F32) * inv_ref[...]).astype(BF)
    fine = att_ref[...].astype(F32) + low_ref[...].astype(F32)
    inner = head_sums(scaled.astype(F32) * fine)
    acc_q[...] = jnp.zeros_like(acc_q)
    for h in range(2):
        mine = left if h == 0 else lane >= HDIM
        spare = HDIM * (1 - h)
        q_own = jnp.where(mine, q, zero)
        k_own = jnp.where(mine, k, zero)
        g_own = jnp.where(mine, scaled, zero)
        high, low = split_low(-inner[h])
        wide = q.shape
        g_more = jnp.where(
            lane == spare,
            jnp.broadcast_to(high, wide),
            jnp.where(lane == spare + 1, jnp.broadcast_to(low, wide), g_own),
        )
        v_more = jnp.where(mine, v, jnp.where((lane >= spare) & (lane < spare + 2), one, zero))
        for first, last, row in ((0, 256, 0), (256, 432, 128), (432, tokens, 384)):
            score = dot(k[first:last], q_own[row:], LAST)
            key = lax.broadcasted_iota(jnp.int32, score.shape, 0) + first
            weight = jnp.where(key < limit_ref[:, row:], jnp.exp(score), 0.0).astype(BF)
            slope = dot(v_more[first:last], g_more[row:], LAST)
            slope = (weight.astype(F32) * slope).astype(BF)
            dv = dot(weight, g_own[row:])
            dk = dot(slope, q_own[row:])
            if h == 0:
                acc_v[first:last, :] = dv
                acc_k[first:last, :] = dk
            else:
                acc_v[first:last, :] += dv
                acc_k[first:last, :] += dk
            acc_q[row:, :] += dot(slope, k_own[first:last], FIRST)
    gain = gain_ref[...]
    dq, dk = acc_q[...], acc_k[...]
    q, k = q.astype(F32), k.astype(F32)
    along = dq * q
    first, second = head_sums(along)
    grad_ref[0] = (
        rq_ref[...] * (dq * gain - q * (jnp.where(left, first, second) / gain))
    ).astype(BF)
    hs_ref[...] = jnp.broadcast_to(jnp.sum(along, axis=0, keepdims=True), hs_ref.shape)
    first, second = head_sums(dk * k)
    grad_ref[1] = (rk_ref[...] * (dk - k * jnp.where(left, first, second))).astype(BF)
    grad_ref[2] = acc_v[...].astype(BF)


def attend_back(qkv, grad, attended, low, inverse, norms, gain, limit, base, some):
    tokens = qkv.shape[0]
    pairs = qkv.shape[1] // (6 * HDIM)
    pair = lambda at: pl.BlockSpec((tokens, 2 * HDIM), lambda p: (0, at + base + p))
    return pl.pallas_call(
        attend_back_body,
        grid=(some,),
        in_specs=[
            pair(0),
            pair(pairs),
            pair(2 * pairs),
            pair(0),
            pair(0),
            pair(0),
            pair(0),
            pair(0),
            pair(pairs),
            pl.BlockSpec((1, 2 * HDIM), lambda p: (0, base + p)),
            whole(limit.shape),
        ],
        out_specs=[
            pl.BlockSpec((3, tokens, 2 * HDIM), lambda p: (0, 0, p)),
            pl.BlockSpec((8, 2 * HDIM), lambda p: (0, p)),
        ],
        out_shape=[
            jax.ShapeDtypeStruct((3, tokens, 2 * HDIM * some), BF),
            jax.ShapeDtypeStruct((8, 2 * HDIM * some), F32),
        ],
        scratch_shapes=[pltpu.VMEM((tokens, 2 * HDIM), F32)] * 3,
        compiler_params=PARAMS,
        cost_estimate=cost(
            40 * some * tokens * tokens * HDIM, 60 * tokens * HDIM * some, 2 * some * tokens * tokens
        ),
        name="attend_back",
    )(qkv, qkv, qkv, grad, attended, low, inverse, norms, norms, gain, limit)


def project_body(live_ref, x_ref, att_ref, w_ref, mod_ref, cot_ref, proj_ref, mlp_ref, grad_ref):
    proj_ref[...] = dot(att_ref[...], w_ref[...])
    for rows in row_chunks(x_ref.shape[0]):
        residual = x_ref[rows, :].astype(F32) + mod_ref[0:1, :] * proj_ref[rows, :]
        unit, _ = norm_parts(residual)
        mlp_ref[rows, :] = (unit * (1.0 + mod_ref[3:4, :]) + mod_ref[5:6, :]).astype(BF)
        at = lax.broadcasted_iota(jnp.int32, residual.shape, 0) + rows.start
        live = jnp.where(at < live_ref[0], 1.0, 0.0)
        grad_ref[rows, :] = (mod_ref[1:2, :] * (cot_ref[rows, :].astype(F32) * live)).astype(BF)


def project(live, x, attended, w_vo, mod, cot):
    tokens, width = x.shape
    full = whole((tokens, width))
    return pl.pallas_call(
        project_body,
        grid=(1,),
        in_specs=[
            pl.BlockSpec(memory_space=pltpu.SMEM),
            full,
            full,
            pl.BlockSpec((width, width), lambda _: (0, 3)),
            whole(mod.shape),
            full,
        ],
        out_specs=[full] * 3,
        out_shape=[jax.ShapeDtypeStruct((tokens, width), t) for t in (F32, BF, BF)],
        compiler_params=PARAMS,
        cost_estimate=cost(2 * tokens * width * width, 14 * tokens * width + 2 * width * width, 0, 1),
        name="project",
    )(live, x, attended, w_vo, mod, cot)


def residual_back_body(
    live_ref, x_ref, proj_ref, out_ref, gx_ref, cot_ref, mod_ref, w_ref,
    block_ref, resid_ref, gatt_ref, gproj, sums_ref,
):
    totals = [0.0] * 4
    for rows in row_chunks(x_ref.shape[0]):
        proj, mlp_out, g = proj_ref[rows, :], out_ref[rows, :], gx_ref[rows, :]
        residual = x_ref[rows, :].astype(F32) + mod_ref[0:1, :] * proj
        at = lax.broadcasted_iota(jnp.int32, residual.shape, 0) + rows.start
        live = jnp.where(at < live_ref[0], 1.0, 0.0)
        block_ref[rows, :] = ((residual + mod_ref[1:2, :] * mlp_out) * live).astype(BF)
        grad_out = cot_ref[rows, :].astype(F32) * live
        unit, inverse = norm_parts(residual)
        dn = g * (1.0 + mod_ref[3:4, :])
        mean_dn = jnp.mean(dn, axis=-1, keepdims=True)
        mean_in = jnp.mean(dn * unit, axis=-1, keepdims=True)
        grad_resid = grad_out + inverse * (dn - mean_dn - unit * mean_in)
        resid_ref[rows, :] = grad_resid
        gproj[rows, :] = (mod_ref[0:1, :] * grad_resid).astype(BF)
        for i, part in enumerate((grad_resid * proj, grad_out * mlp_out, g * unit, g)):
            totals[i] = totals[i] + jnp.sum(part, axis=0, keepdims=True)
    for i in range(4):
        sums_ref[i : i + 1, :] = totals[i]
    sums_ref[4:, :] = jnp.zeros((4, sums_ref.shape[1]), F32)
    gatt_ref[...] = dot(gproj[...], w_ref[...], LAST).astype(BF)


def residual_back(live, x, proj, mlp_out, gx, cot, mod, weights):
    tokens, width = x.shape
    full = whole((tokens, width))
    return pl.pallas_call(
        residual_back_body,
        grid=(1,),
        in_specs=[
            pl.BlockSpec(memory_space=pltpu.SMEM),
            full,
            full,
            full,
            full,
            full,
            whole(mod.shape),
            pl.BlockSpec((width, width), lambda _: (0, 3)),
        ],
        out_specs=[full, full, full, full, whole((8, width))],
        out_shape=[jax.ShapeDtypeStruct((tokens, width), t) for t in (BF, F32, BF, BF)]
        + [jax.ShapeDtypeStruct((8, width), F32)],
        compiler_params=PARAMS,
        cost_estimate=cost(2 * tokens * width * width, 28 * tokens * width + 4 * width * width),
        name="residual_back",
    )(live, x, proj, mlp_out, gx, cot, mod, weights)


def weight_grad_body(core_ref, x_ref, g_ref, att_ref, proj_ref, keep_a, send_a, keep_b, send_b):
    step = pl.program_id(0)
    core = core_ref[0]

    @pl.when(step < 2)
    def _():
        keep_a[...], send_a[...] = halves_of(dot(x_ref[...], g_ref[0], FIRST), core)

    @pl.when(step == 2)
    def _():
        keep_b[...], send_b[...] = halves_of(dot(x_ref[...], g_ref[0], FIRST), core)

    @pl.when(step == 3)
    def _():
        keep_b[...], send_b[...] = halves_of(dot(att_ref[...], proj_ref[...], FIRST), core)


def weight_grad(core, x, g, attended, grad_proj):
    tokens, width = x.shape
    full = whole((tokens, width))
    part = (BLOCKS // 2, width // BLOCKS, width)
    first = pl.BlockSpec(part, lambda n: (0, 0, jnp.minimum(n, 1)))
    second = pl.BlockSpec(part, lambda n: (0, 0, jnp.maximum(n - 2, 0)))
    return pl.pallas_call(
        weight_grad_body,
        grid=(4,),
        in_specs=[
            pl.BlockSpec(memory_space=pltpu.SMEM),
            full,
            pl.BlockSpec((1, tokens, width), lambda n: (jnp.minimum(n, 2), 0, 0)),
            full,
            full,
        ],
        out_specs=[first, first, second, second],
        out_shape=[jax.ShapeDtypeStruct(part[:2] + (2 * width,), BF)] * 4,
        compiler_params=PARAMS,
        cost_estimate=cost(8 * tokens * width * width, 12 * tokens * width + 8 * width * width),
        name="weight_grad",
    )(core, x, g, attended, grad_proj)


def input_back_body(x_ref, resid_ref, mod_ref, g_ref, w_ref, out_ref, sums_ref):
    step = pl.program_id(0)
    part = dot(g_ref[0], w_ref[...], LAST)

    @pl.when(step == 0)
    def _():
        out_ref[...] = part

    @pl.when(step > 0)
    def _():
        out_ref[...] += part

    @pl.when(step == 2)
    def _():
        totals = [0.0] * 2
        for rows in row_chunks(x_ref.shape[0]):
            g = out_ref[rows, :]
            unit, inverse = norm_parts(x_ref[rows, :].astype(F32))
            dn = g * (1.0 + mod_ref[2:3, :])
            mean_dn = jnp.mean(dn, axis=-1, keepdims=True)
            mean_in = jnp.mean(dn * unit, axis=-1, keepdims=True)
            out_ref[rows, :] = resid_ref[rows, :] + inverse * (dn - mean_dn - unit * mean_in)
            for i, part in enumerate((g * unit, g)):
                totals[i] = totals[i] + jnp.sum(part, axis=0, keepdims=True)
        for i in range(2):
            sums_ref[i : i + 1, :] = totals[i]
        sums_ref[2:, :] = jnp.zeros((6, x_ref.shape[1]), F32)


def input_back(x, resid, mod, g, weights):
    tokens, width = x.shape
    full = whole((tokens, width))
    return pl.pallas_call(
        input_back_body,
        grid=(3,),
        in_specs=[
            full,
            full,
            whole(mod.shape),
            pl.BlockSpec((1, tokens, width), lambda n: (n, 0, 0)),
            pl.BlockSpec((width, width), lambda n: (0, n)),
        ],
        out_specs=[full, whole((8, width))],
        out_shape=[
            jax.ShapeDtypeStruct((tokens, width), F32),
            jax.ShapeDtypeStruct((8, width), F32),
        ],
        compiler_params=PARAMS,
        cost_estimate=cost(6 * tokens * width * width, 16 * tokens * width + 6 * width * width),
        name="input_back",
    )(x, resid, mod, g, weights)


def mlp_body(info_ref, x_ref, g_ref, bias_ref, *refs, first, sources):
    a_refs, b_refs, refs = refs[:sources], refs[sources : 2 * sources], refs[2 * sources :]
    if first:
        out_ref, gx_ref, keep_a, send_a, keep_b, send_b, bias_g, up_w, down_w = refs
    else:
        out_in, gx_in, out_ref, gx_ref, keep_a, send_a, keep_b, send_b, bias_g, up_w, down_w = refs
    core = info_ref[2, 0]
    block = x_ref.shape[1] // BLOCKS

    @pl.when(pl.program_id(0) == 0)
    def _():
        out_ref[...] = jnp.zeros_like(out_ref) if first else out_in[...]
        gx_ref[...] = jnp.zeros_like(gx_ref) if first else gx_in[...]

    step = pl.program_id(0)
    size = up_w.shape[1]
    per = down_w.shape[0] // size
    fill(up_w, info_ref.at[0], paired(a_refs), block)

    @pl.when(step % per == 0)
    def _():
        fill(down_w, info_ref.at[1], paired(b_refs), block)

    root = np.float32(np.sqrt(2.0 / np.pi))
    x, g, up = x_ref[...], g_ref[...], up_w[...]
    down = down_w[pl.ds(pl.multiple_of(step % per * size, size), size), :]
    hidden = dot(x, up) + bias_ref[...]
    square = hidden * hidden
    bend = jnp.tanh(root * hidden * (1.0 + 0.044715 * square))
    act = (0.5 * hidden * (1.0 + bend)).astype(BF)
    out_ref[...] += dot(act, down)
    slope = 0.5 * (1.0 + bend) + 0.5 * hidden * (1.0 - bend * bend) * root * (
        1.0 + (3 * 0.044715) * square
    )
    grad_hidden = (dot(g, down, LAST) * slope).astype(BF)
    bias_g[...] = jnp.sum(grad_hidden.astype(F32), axis=0, keepdims=True)
    gx_ref[...] += dot(grad_hidden, up, LAST)
    keep_b[...], send_b[...] = halves_of(dot(act, g, FIRST), core, BLOCKS // per)
    keep_a[...], send_a[...] = halves_of(dot(x, grad_hidden, FIRST), core)


def mlp(info, x, g, pieces, bias, at, carried=None):
    tokens, width = x.shape
    block, per = 512, width // 512
    lead, rows = BLOCKS // 2, width // BLOCKS
    part_a = pl.BlockSpec((lead, rows, block), lambda f: (0, 0, f))
    if len(pieces) == 3:
        matrices = (*pieces[1], *pieces[2])
        total = matrices[0].shape[2]
        sources = [
            pl.BlockSpec(m.shape[:2] + (block,), lambda f: (0, 0, f)) for m in pieces[1]
        ] + [pl.BlockSpec(m.shape[:2] + (width,), lambda f: (0, 0, f // per)) for m in pieces[2]]
    else:
        matrices = [pieces[0].reshape(lead, 2, rows, -1)] * 4
        total = matrices[0].shape[3] // 2
        skip = total // width
        sources = [
            pl.BlockSpec((lead, None, rows, block), lambda f: (0, 0, 0, f)),
            pl.BlockSpec((lead, None, rows, block), lambda f: (0, 1, 0, f)),
            pl.BlockSpec((lead, None, rows, width), lambda f: (0, 0, 0, skip + f // per)),
            pl.BlockSpec((lead, None, rows, width), lambda f: (0, 1, 0, skip + f // per)),
        ]
    steps = total // block
    grad_b = pl.BlockSpec((lead // per, rows, width), lambda f: (f % per, 0, f // per))
    single = pl.BlockSpec((tokens, width), lambda f: (0, 0), pipeline_mode=pl.Buffered(1))
    carried = () if carried is None else tuple(carried)
    return pl.pallas_call(
        partial(mlp_body, first=not carried, sources=len(matrices) // 2),
        grid=(steps,),
        in_specs=[pl.BlockSpec(memory_space=pltpu.SMEM), single, single]
        + [pl.BlockSpec((1, block), lambda f: (0, at * per + f))]
        + sources
        + [single] * len(carried),
        out_specs=[single, single, part_a, part_a, grad_b, grad_b]
        + [pl.BlockSpec((1, block), lambda f: (0, f))],
        out_shape=[jax.ShapeDtypeStruct((tokens, width), F32)] * 2
        + [jax.ShapeDtypeStruct((lead, rows, total), BF)] * 4
        + [jax.ShapeDtypeStruct((1, total), F32)],
        scratch_shapes=[pltpu.VMEM((width, block), BF), pltpu.VMEM((width, width), BF)],
        input_output_aliases={4 + len(matrices) + i: i for i in range(len(carried))},
        compiler_params=PARAMS,
        cost_estimate=cost(
            12 * tokens * width * total,
            (8 + 8 * len(carried)) * tokens * width + 8 * total * width,
            tokens * total,
            20 if carried else 0.3,
        ),
        name="mlp",
    )(info, x, g, bias, *matrices, *carried)


def fold_body(bit_ref, *refs, plan, out_count):
    ins, outs = refs[:-out_count], refs[-out_count:]
    for source, cols, bit, stride, out, column in plan:
        kept, came = ins[2 * source], ins[2 * source + 1]
        at_cols = slice(column, column + cols.stop - cols.start)
        if bit is None:
            outs[out][:, :, at_cols] = kept[:, :, cols].astype(F32) + came[:, :, cols].astype(F32)
            continue
        mine = bit_ref[bit]
        for m in range(kept.shape[0] // 2):
            base = m // stride * 2 * stride + m % stride
            for side, value in ((0, mine), (1, 1 - mine)):
                at = base + value * stride
                outs[out + side][m, :, at_cols] = (
                    kept[at, :, cols].astype(F32) + came[at, :, cols].astype(F32)
                ).astype(BF)


def fold(bits, parts, plan, outs, split=1, weight=0):
    def spec(shape):
        return pl.BlockSpec(tuple(shape[:2]) + (shape[2] // split,), lambda n: (0, 0, n))

    return pl.pallas_call(
        partial(fold_body, plan=plan, out_count=len(outs)),
        grid=(split,),
        in_specs=[pl.BlockSpec(memory_space=pltpu.SMEM)] + [spec(p.shape) for p in parts],
        out_specs=[spec(s) for s, _ in outs],
        out_shape=[jax.ShapeDtypeStruct(s, t) for s, t in outs],
        compiler_params=PARAMS,
        cost_estimate=cost(weight, 8),
        name="fold",
    )(bits, *parts)


def swap(block, count, mask):
    return lax.ppermute(block, AXES, [(i, i ^ mask) for i in range(count)])


def after(value, *others):
    return lax.optimization_barrier((value,) + others)


def join(block, came):
    return jnp.concatenate([block, came])


def codes(order, me):
    code = [0]
    for bit in order:
        code = code + [c | (1 << bit) for c in code]
    return jnp.asarray(np.array(code, np.int32)) ^ me


def gathered_pieces(full):
    rows, cols = full.shape
    cut = full.reshape(BLOCKS // 2, 2, rows // BLOCKS, 2, cols // 2)
    return [tuple(cut[:, i, :, j] for i in range(2)) for j in range(2)]


def halve(pieces, axis, bit_value, count, mask):
    total = pieces[0]
    if len(pieces) > 1:
        total = (pieces[0].astype(F32) + pieces[1].astype(F32)).astype(BF)
    keep = lax.dynamic_index_in_dim(total, bit_value, axis, keepdims=False)
    send = lax.dynamic_index_in_dim(total, 1 - bit_value, axis, keepdims=False)
    return [keep, swap(send, count, mask)]


def scatter_rows(kept, send, count, me):
    grads = [jnp.stack(pair, axis=1).reshape(-1, pair[0].shape[2]) for pair in zip(kept, send)]
    grad = jnp.concatenate(grads, axis=1)
    rows, width = grad.shape
    bits = count.bit_length() - 1
    own = rows // count
    bit = [lax.rem(lax.div(me, np.int32(1 << b)), np.int32(2)) for b in range(bits)]
    part = [grad.reshape((2,) * bits + (own, width))]
    for b in range(bits):
        part = halve(part, bits - 1 - b, bit[b], count, 1 << b)
    return (part[0].astype(F32) + part[1].astype(F32)).reshape(own, width)


def tie(*groups):
    flat = lax.optimization_barrier(tuple(a for g in groups for a in g))
    for g in groups:
        g[:], flat = flat[: len(g)], flat[len(g) :]


def land(value, *moves):
    box = [value]
    tie(box, *[m.came for m in moves])
    return box[0]


def leave(value, *scatters):
    for s in scatters:
        s.add()
    box = [value]
    tie(box, *[s.send for s in scatters])
    for s in scatters:
        if s.done is None:
            s.start()
    return box[0]


class Gather:
    def __init__(self, shard, count):
        self.count = count
        self.block = shard[None]
        self.came = None

    def start_z(self, bit):
        self.came = [swap(self.block, self.count, 1 << bit)]

    def end_z(self):
        self.block = join(self.block, self.came[0])

    def start_xy(self, first, second):
        if not isinstance(self.block, list):
            half = self.block.shape[2] // 2
            self.block = [self.block[:, :, :half], self.block[:, :, half:]]
        self.came = [
            swap(b, self.count, 1 << bit) for b, bit in zip(self.block, (first, second))
        ]

    def end_xy(self):
        self.block = [join(b, c) for b, c in zip(self.block, self.came)]

    def start_early(self):
        self.early = [swap(b, self.count, 1) for b in self.block]

    def start_late(self):
        self.late = [swap(c, self.count, 1) for c in self.came]

    def pieces(self, code):
        sides = [
            (b, e, c, l) for b, e, c, l in zip(self.block, self.early, self.came, self.late)
        ]
        return (code, *sides)


class Scatter:
    def __init__(self, kept, send, pieces, bits, count, heavy=0):
        self.bits, self.count, self.heavy = bits, count, heavy
        self.pieces = pieces
        self.kept, self.send = list(kept), list(send)
        self.left = 0
        self.done = None
        self.start()

    def start(self):
        masks = ([1] * len(self.send), (2, 4), (4, 2), (8,), (16,))[self.left]
        self.came = [swap(s, self.count, mask) for s, mask in zip(self.send, masks)]
        self.left += 1

    def add(self):
        parts = [p for pair in zip(self.kept, self.came) for p in pair]
        lead, own, width = self.kept[0].shape
        split = {1: 4, 2: 2}.get(self.left, 1)
        everything = slice(0, width // split)
        half = lambda cols: ((lead // 2, own, cols), BF)
        if self.left == 5:
            plan, outs, at = [], [], 0
            for i, cols in enumerate(self.pieces):
                plan.append((0, slice(at, at + cols), None, 1, i, 0))
                outs.append(((lead, own, cols), F32))
                at += cols
        elif self.left == 1:
            plan, sums = [], [0, 0]
            for side in range(2):
                plan.append((side, everything, (1, 2)[side], (1, 2)[side], 2 * side, 0))
            outs = [half(width)] * 4
        elif self.left == 2:
            plan = tuple((i, everything, 2 - i, 1, 2 * i, 0) for i in range(2))
            outs = [half(width)] * 4
        elif self.left == 3:
            plan = tuple((i, everything, 3, 1, 0, i * width) for i in range(2))
            outs = [half(2 * width)] * 2
        else:
            plan = ((0, everything, 4, 1, 0, 0),)
            outs = [half(width)] * 2
        weight = self.heavy if self.left == 5 else 0
        outs = fold(self.bits, parts, tuple(plan), outs, split, weight)
        if self.left == 5:
            self.done, self.send = [o[0] for o in outs], list(outs)
        else:
            self.kept, self.send = list(outs[0::2]), list(outs[1::2])


def per_device(
    tokens,
    labels,
    stop_scale,
    class_table,
    ada_weight,
    ada_bias,
    qkv_weight,
    head_scale,
    out_weight,
    up_weight,
    up_bias,
    down_weight,
    cotangent,
    count,
):
    image_count, seq_len, model_width = tokens.shape
    row_count = image_count * seq_len
    me = lax.axis_index(AXES).astype(jnp.int32)
    levels = position_scale(SCALES)
    ends = jnp.asarray(LEVEL_ENDS)
    live = jnp.take(ends, stop_scale - 1).astype(jnp.int32)
    limit = jnp.asarray(LEVEL_ENDS[levels][None, :])
    start = jnp.asarray((LEVEL_ENDS - np.square(np.array(scale_sides)))[levels][None, :].astype(np.int32))
    class_count = class_table.shape[0]
    own = model_width // count
    ratio = down_weight.shape[0] // own
    hidden_width = up_weight.shape[1]

    def hidden_order(matrix):
        lead = matrix.shape[:-1]
        cut = matrix.reshape(lead + (count, ratio, own))
        return jnp.swapaxes(cut, -3, -2).reshape(lead + (hidden_width,))

    def hidden_back(matrix):
        lead = matrix.shape[:-1]
        cut = matrix.reshape(lead + (ratio, count, own))
        return jnp.swapaxes(cut, -3, -2).reshape(lead + (hidden_width,))

    down_wide = jnp.swapaxes(down_weight.reshape(ratio, own, model_width), 0, 1).reshape(
        own, hidden_width
    )
    half = hidden_width // 2
    up_order = hidden_order(up_weight)
    shards = [jnp.concatenate([qkv_weight, out_weight], axis=1)] + [
        jnp.concatenate([m[:, i : i + half] for m in (up_order, down_wide)], axis=1)
        for i in (0, half)
    ]
    quick = count == BLOCKS and own % 16 == 0
    plain = jnp.asarray(np.tile(np.arange(0, BLOCKS, 2, dtype=np.int32), (2, 1)))
    if quick:
        one, two = [Gather(s, count) for s in shards[:2]]
        orders = ((4, 3, 2, 1), (4, 3, 1, 2))
        code = jnp.stack([codes(o, me) for o in orders])
        bits = jnp.stack([lax.rem(lax.div(me, np.int32(1 << b)), np.int32(2)) for b in range(5)])
        one.start_z(4)
        one.came[0], two.block = after(one.came[0], two.block)
        one.end_z()
        one.start_z(3)
    else:
        wide = [lax.all_gather(s, AXES, axis=0, tiled=True) for s in shards]
        code = plain
        bits = jnp.zeros((5,), jnp.int32)
    core = bits[:1]
    info, info_plain = [
        jnp.concatenate([c, jnp.full((1, c.shape[1]), bits[0])]) for c in (code, plain)
    ]

    first_row = jnp.concatenate(
        [lax.div(labels, 32).astype(BF), lax.rem(labels, 32).astype(BF), up_bias]
    )
    rows = lax.all_to_all(
        jnp.broadcast_to(first_row[None, :], (count, first_row.shape[0])), AXES, 0, 0, tiled=True
    )
    labels_all = 32 * rows[:, 0].astype(jnp.int32) + rows[:, 1].astype(jnp.int32)
    up_bias_full = rows[:, 2:].astype(F32).reshape(1, hidden_width)
    onehot = labels_all[:, None] == jnp.arange(class_count, dtype=jnp.int32)[None, :]
    condition = jnp.dot(onehot.astype(BF), class_table, preferred_element_type=F32)
    cond_act = jax.nn.silu(condition).astype(BF)
    exponent = count.bit_length() - 1
    order = tuple(range(exponent - 1, -1, -1)) + (exponent,)
    backwards = cond_act.reshape((2,) * exponent + (own,)).transpose(order).reshape(count, own)
    modul_part = jnp.dot(backwards, ada_weight, preferred_element_type=F32)
    bias_own = ada_bias.shape[0]
    bias_row = lax.dynamic_update_slice(
        jnp.zeros((6 * model_width,), F32), ada_bias.astype(F32), (me * bias_own,)
    )
    part = modul_part + bias_row[None, :]
    bit_values = [lax.rem(lax.div(me, np.int32(1 << b)), np.int32(2)) for b in range(exponent)]
    for b in range(exponent):
        size = part.shape[0] // 2
        keep = lax.dynamic_slice_in_dim(part, bit_values[b] * size, size)
        send = lax.dynamic_slice_in_dim(part, (1 - bit_values[b]) * size, size)
        came = swap(send, count, 1 << b)
        if quick and b == 0:
            came = land(came, one)
            one.end_z()
            came, two.block = after(came, two.block)
            one.start_xy(2, 1)
            two.start_z(4)
        elif quick and b == 2:
            came = land(came, one, two)
            one.end_xy()
            two.end_z()
            one.start_early()
            one.start_xy(1, 2)
            two.start_z(3)
        part = keep + came
    mod = part.reshape(6, model_width)
    if quick:
        mod = land(mod, one, two)
        two.end_z()
        one.start_late()
        two.start_xy(2, 1)
        pieces = one.pieces(code)
    else:
        pieces = (code, *gathered_pieces(wide[0]))
    heads = head_scale.shape[0]
    gain = jnp.repeat(jnp.exp(head_scale), HDIM)[None, :]
    seg = jnp.asarray(
        np.arange(model_width)[:, None] // HDIM == np.arange(128)[None, :], dtype=BF
    )
    x = tokens.reshape(row_count, model_width)
    cot = cotangent.reshape(row_count, model_width)

    attn_in, qkv, norms, weights = qkv_rows(x, mod, pieces, gain, seg)
    if quick:
        qkv = land(qkv, two)
        two.end_xy()
        qkv, last_shard, *two.block = after(qkv, shards[2], *two.block)
        last_full = lax.all_gather(last_shard, AXES, axis=0, tiled=True)
        two.start_early()
        two.start_xy(1, 2)
    attended, low, inverse = attend(qkv, start)
    projected, mlp_in, grad_mlp = project(live, x, attended, weights, mod, cot)
    if quick:
        mlp_in = land(mlp_in, two)
        two.start_late()
    bias = hidden_order(up_bias_full)
    pieces = two.pieces(code) if quick else (wide[1],)
    *carried, keep_a, send_a, keep_b, send_b, bias_one = mlp(info, mlp_in, grad_mlp, pieces, bias, 0)
    kept_one, send_one = (keep_a, keep_b), (send_a, send_b)
    if quick:
        first = Scatter(kept_one, send_one, (half, half), bits, count, 1 << 33)
        carried[0] = land(carried[0], first)
        carried[0] = leave(carried[0], first)
    pieces = (last_full if quick else wide[2],)
    mlp_out, grad_mlp_in, keep_a, send_a, keep_b, send_b, bias_two = mlp(
        info_plain, mlp_in, grad_mlp, pieces, bias, half // model_width, carried
    )
    kept_two, send_two = (keep_a, keep_b), (send_a, send_b)
    if quick:
        second = Scatter(kept_two, send_two, (half, half), bits, count)
        mlp_out = land(mlp_out, first)
        mlp_out = leave(mlp_out, first)
    block_out, grad_resid, grad_attended, grad_proj, sums_two = residual_back(
        live, x, projected, mlp_out, grad_mlp_in, cot, mod, weights
    )
    if quick:
        grad_attended = land(grad_attended, first, second)
        grad_attended = leave(grad_attended, first, second)
    dqkv, head_sums = attend_back(
        qkv, grad_attended, attended, low, inverse, norms, gain, limit, 0, heads // 2
    )
    if quick:
        dqkv = land(dqkv, first, second)
        dqkv = leave(dqkv, first, second)
    keep_a, send_a, keep_b, send_b = weight_grad(core, attn_in, dqkv, attended, grad_proj)
    kept_three, send_three = (keep_a, keep_b), (send_a, send_b)
    if quick:
        third = Scatter(
            kept_three, send_three, (3 * model_width, model_width), bits, count
        )
        dqkv = land(dqkv, first, second)
        dqkv = leave(dqkv, first, second)
        dqkv = land(dqkv, third)
        dqkv = leave(dqkv, third)
    input_grad, sums_one = input_back(x, grad_resid, mod, dqkv, weights)
    if not quick:
        mlp_own = [
            scatter_rows(kept_one, send_one, count, me),
            scatter_rows(kept_two, send_two, count, me),
        ]
        up_own = jnp.concatenate([m[:, :half] for m in mlp_own], axis=1)
        down_own = jnp.concatenate([m[:, half:] for m in mlp_own], axis=1)
        attn_own = scatter_rows(kept_three, send_three, count, me)
        qkv_own, out_own = attn_own[:, : 3 * model_width], attn_own[:, 3 * model_width :]
    block_out = block_out.reshape(tokens.shape)
    input_grad = input_grad.reshape(tokens.shape)
    if quick:
        sums_one, bias_one, bias_two, head_sums, sums_two = after(
            sums_one, bias_one, bias_two, head_sums, sums_two
        )
    up_bias_grad = jnp.concatenate([bias_one, bias_two], axis=1)
    grad_modul = jnp.concatenate(
        [sums_two[0], sums_two[1], sums_one[0], sums_two[2], sums_one[1], sums_two[3]]
    ).astype(BF)
    head_scale_part = jnp.sum(head_sums[0].reshape(heads, HDIM), axis=1)
    bias_high, bias_low = split_low(hidden_back(up_bias_grad).reshape(count, -1))
    head_high, head_low = split_low(head_scale_part)
    common = jnp.concatenate([grad_modul.reshape(-1), head_high, head_low])
    small = jnp.concatenate(
        [jnp.broadcast_to(common[None, :], (count, common.shape[0])), bias_high, bias_low], axis=1
    )
    small = lax.all_to_all(small, AXES, 0, 0, tiled=True)
    if quick:
        input_grad = land(input_grad, second, third)
        input_grad = leave(input_grad, second, third)
        input_grad = land(input_grad, second, third)
        input_grad = leave(input_grad, second, third)
        input_grad = land(input_grad, third)
        small, input_grad = after(small, input_grad)
        small = leave(small, third)
        third.add()
        up_own, down_own = [jnp.concatenate(m, axis=1) for m in zip(first.done, second.done)]
        qkv_own, out_own = third.done
    modul_cols = image_count * 6 * model_width
    grad_modul_all = small[:, :modul_cols].reshape(count * image_count, 6 * model_width)
    tail = jnp.sum(small[:, modul_cols:].astype(F32), axis=0)
    head_scale_grad = tail[:heads] + tail[heads : 2 * heads]
    tail = tail[2 * heads :].reshape(2, -1)
    up_bias_own = tail[0] + tail[1]
    ada_bias_own = jnp.sum(
        lax.dynamic_slice_in_dim(grad_modul_all, me * bias_own, bias_own, axis=1).astype(F32), axis=0
    )
    ada_own = lax.dot_general(
        cond_act, grad_modul_all, (((0,), (0,)), ((), ())), preferred_element_type=F32
    )
    grad_cond_act = lax.dot_general(
        grad_modul_all, ada_weight, (((1,), (1,)), ((), ())), preferred_element_type=F32
    )
    grad_condition = jax.vjp(jax.nn.silu, condition)[1](grad_cond_act)[0]
    table_own = lax.dot_general(
        onehot.astype(F32),
        grad_condition,
        (((0,), (0,)), ((), ())),
        precision=lax.Precision.HIGHEST,
        preferred_element_type=F32,
    )
    up_own = hidden_back(up_own)
    down_own = jnp.swapaxes(down_own.reshape(own, ratio, model_width), 0, 1).reshape(
        ratio * own, model_width
    )
    return (
        block_out,
        input_grad,
        table_own,
        ada_own,
        ada_bias_own,
        qkv_own,
        head_scale_grad,
        out_own,
        up_own,
        up_bias_own,
        down_own,
    )


def solution(mesh):
    count = mesh.shape["wide"] * mesh.shape["narrow"]
    both = AXES
    in_specs = (
        P(both, None, None),
        P(both),
        P(both),
        P(None, both),
        P(both, None),
        P(both),
        P(both, None),
        P(),
        P(both, None),
        P(both, None),
        P(both),
        P(both, None),
        P(both, None, None),
    )
    out_specs = (
        P(both, None, None),
        P(both, None, None),
        P(None, both),
        P(both, None),
        P(both),
        P(both, None),
        P(),
        P(both, None),
        P(both, None),
        P(both),
        P(both, None),
    )
    return jax.shard_map(
        partial(per_device, count=count),
        mesh=mesh,
        in_specs=in_specs,
        out_specs=out_specs,
        check_vma=False,
    )
```

```python
from functools import partial

import jax
import jax.numpy as jnp
import numpy as np
from jax import lax
from jax.experimental import pallas as pl
from jax.experimental.pallas import tpu as pltpu
from jax.sharding import PartitionSpec as P

HDIM = 64
SCALES = 10
AXES = ("wide", "narrow")
BF = jnp.bfloat16
F32 = jnp.float32

scale_sides = (1, 2, 3, 4, 5, 6, 8, 10, 13, 16)


def position_scale(scale_count):
    return np.concatenate(
        [
            np.full(side_size * side_size, level_index, dtype=np.int32)
            for level_index, side_size in enumerate(scale_sides[:scale_count])
        ]
    )


BLOCKS = 32
LEVEL_ENDS = np.cumsum(np.square(np.array(scale_sides))).astype(np.int32)
LAST = (((1,), (1,)), ((), ()))
FIRST = (((0,), (0,)), ((), ()))


def grant(mebibytes):
    return pltpu.CompilerParams(vmem_limit_bytes=mebibytes << 20)


def dot(left, right, dims=(((1,), (0,)), ((), ()))):
    return lax.dot_general(left, right, dims, preferred_element_type=F32)


def split_low(value):
    high = value.astype(BF)
    return high, (value - high.astype(F32)).astype(BF)


def row_chunks(total, step=80):
    return [slice(i, min(i + step, total)) for i in range(0, total, step)]


def norm_parts(value):
    centred = value - jnp.mean(value, axis=-1, keepdims=True)
    inverse = lax.rsqrt(jnp.mean(centred * centred, axis=-1, keepdims=True) + 1e-06)
    return centred * inverse, inverse


def cost(flops, read, exps=0, scale=20):
    return pl.CostEstimate(flops=int(scale * flops), bytes_accessed=int(scale * read), transcendentals=int(scale * exps))


def whole(shape):
    return pl.BlockSpec(shape, lambda *_: (0,) * len(shape), pipeline_mode=pl.Buffered(1))


def fill(dst, code, pairs, block):
    position = 0
    for own, other in pairs:
        for m in range(own.shape[0]):
            at = code[position]
            dst[pl.ds(pl.multiple_of(at * block, block), block), :] = own[m]
            at = at ^ 1
            dst[pl.ds(pl.multiple_of(at * block, block), block), :] = other[m]
            position += 1


def paired(refs):
    return list(zip(refs[0::2], refs[1::2]))


def halves_of(value, core, count=None):
    rows, cols = value.shape
    block = rows // (count or BLOCKS)
    cut = value.reshape(rows // (2 * block), 2, block, cols)
    even, odd = cut[:, 0], cut[:, 1]
    return (
        jnp.where(core == 0, even, odd).astype(BF),
        jnp.where(core == 0, odd, even).astype(BF),
    )


def qkv_body(code_ref, x_ref, mod_ref, gain_ref, seg_ref, *refs):
    *sources, attn_ref, out_ref, inv_ref, w_ref = refs
    half = len(sources) // 2
    first, second = paired(sources[:half]), paired(sources[half:])
    step = pl.program_id(0)
    block = x_ref.shape[1] // BLOCKS

    @pl.when(step == 0)
    def _():
        for rows in row_chunks(x_ref.shape[0]):
            unit, _ = norm_parts(x_ref[rows, :].astype(F32))
            attn_ref[rows, :] = (unit * (1.0 + mod_ref[2:3, :]) + mod_ref[4:5, :]).astype(BF)

    @pl.when(step < 2)
    def _():
        fill(w_ref, code_ref.at[0], first, block)
        raw = dot(attn_ref[...], w_ref[...])
        seg = seg_ref[...]
        high, low = split_low(raw * raw)
        inverse = lax.rsqrt(dot(high, seg) + dot(low, seg) + 1e-06)
        high, low = split_low(inverse)
        spread = dot(high, seg, LAST) + dot(low, seg, LAST)
        gain = jnp.where(step == 0, gain_ref[...], 1.0)
        out_ref[...] = (raw * spread * gain).astype(BF)
        inv_ref[...] = spread

    @pl.when(step >= 2)
    def _():
        fill(w_ref, code_ref.at[1], second, block)

    @pl.when(step == 2)
    def _():
        out_ref[...] = dot(attn_ref[...], w_ref[...]).astype(BF)


def qkv_rows(x, mod, pieces, gain, seg):
    tokens, width = x.shape
    code, first, second = pieces
    one = [
        pl.BlockSpec(a.shape[:2] + (width,), lambda n: (0, 0, jnp.minimum(n, 1))) for a in first
    ]
    two = [
        pl.BlockSpec(a.shape[:2] + (width,), lambda n: (0, 0, jnp.maximum(n - 2, 0)))
        for a in second
    ]
    return pl.pallas_call(
        qkv_body,
        grid=(4,),
        in_specs=[
            pl.BlockSpec(memory_space=pltpu.SMEM),
            whole((tokens, width)),
            whole(mod.shape),
            whole(gain.shape),
            whole(seg.shape),
            *one,
            *two,
        ],
        out_specs=[
            whole((tokens, width)),
            pl.BlockSpec((tokens, width), lambda n: (0, jnp.minimum(n, 2))),
            pl.BlockSpec((tokens, width), lambda n: (0, jnp.minimum(n, 1))),
            pl.BlockSpec((width, width), lambda n: (0, n)),
        ],
        out_shape=[
            jax.ShapeDtypeStruct((tokens, width), BF),
            jax.ShapeDtypeStruct((tokens, 3 * width), BF),
            jax.ShapeDtypeStruct((tokens, 2 * width), F32),
            jax.ShapeDtypeStruct((width, 4 * width), BF),
        ],
        compiler_params=grant(58),
        cost_estimate=cost(6 * tokens * width * width, 16 * tokens * width + 16 * width * width, 0, 2),
        name="qkv",
    )(code, x, mod, gain, seg, *first, *second)


def attend_body(q_ref, k_ref, v_ref, start_ref, out_ref, low_ref, inv_ref):
    q, k, v = q_ref[...], k_ref[...], v_ref[...]
    lane = lax.broadcasted_iota(jnp.int32, q.shape, 1)
    zero = jnp.zeros_like(q)
    one = jnp.ones_like(q)
    tokens = q.shape[0]
    queries = [jnp.where(lane < HDIM, q, zero), jnp.where(lane >= HDIM, q, zero)]
    values = [
        jnp.where(lane < HDIM, v, jnp.where(lane == HDIM, one, zero)),
        jnp.where(lane >= HDIM, v, jnp.where(lane == 0, one, zero)),
    ]
    for first, last, keys in ((0, 240, 256), (240, 416, 432), (416, tokens, tokens)):
        row = lax.broadcasted_iota(jnp.int32, (last - first, keys), 0) + first
        seen = row >= start_ref[:, :keys]
        tiles, sums = [], []
        for h in range(2):
            score = dot(queries[h][first:last], k[:keys], LAST)
            weight = jnp.where(seen, jnp.exp(score), 0.0).astype(BF)
            tile = dot(weight, values[h][:keys])
            inverse = 1.0 / tile[:, HDIM * (1 - h) : HDIM * (1 - h) + 1]
            tiles.append(tile * inverse)
            sums.append(jnp.broadcast_to(inverse, tile.shape))
        left = lane[first:last] < HDIM
        high, low = split_low(jnp.where(left, tiles[0], tiles[1]))
        out_ref[first:last, :] = high
        low_ref[first:last, :] = low
        inv_ref[first:last, :] = jnp.where(left, sums[0], sums[1])


def attend(qkv, start):
    tokens = qkv.shape[0]
    pairs = qkv.shape[1] // (6 * HDIM)
    pair = lambda base: pl.BlockSpec((tokens, 2 * HDIM), lambda p: (0, base + p))
    return pl.pallas_call(
        attend_body,
        grid=(pairs,),
        in_specs=[pair(0), pair(pairs), pair(2 * pairs), whole(start.shape)],
        out_specs=[pair(0), pair(0), pair(0)],
        out_shape=[
            jax.ShapeDtypeStruct((tokens, 2 * HDIM * pairs), BF),
            jax.ShapeDtypeStruct((tokens, 2 * HDIM * pairs), BF),
            jax.ShapeDtypeStruct((tokens, 2 * HDIM * pairs), F32),
        ],
        compiler_params=grant(12),
        cost_estimate=cost(
            16 * pairs * tokens * tokens * HDIM, 20 * tokens * HDIM * pairs, 2 * pairs * tokens * tokens, 0.02
        ),
        name="attend",
    )(qkv, qkv, qkv, start)


def attend_back_body(
    q_ref, k_ref, v_ref, g_ref, att_ref, low_ref, inv_ref, rq_ref, rk_ref, gain_ref, limit_ref,
    grad_ref, hs_ref, acc_q, acc_k, acc_v,
):
    q, k, v = q_ref[...], k_ref[...], v_ref[...]
    tokens = q.shape[0]
    lane = lax.broadcasted_iota(jnp.int32, q.shape, 1)
    zero, one = jnp.zeros_like(q), jnp.ones_like(q)
    left = lane < HDIM

    def head_sums(value):
        first = jnp.sum(jnp.where(left, value, 0.0), axis=1, keepdims=True)
        second = jnp.sum(jnp.where(left, 0.0, value), axis=1, keepdims=True)
        return first, second

    scaled = (g_ref[...].astype(F32) * inv_ref[...]).astype(BF)
    fine = att_ref[...].astype(F32) + low_ref[...].astype(F32)
    inner = head_sums(scaled.astype(F32) * fine)
    acc_q[...] = jnp.zeros_like(acc_q)
    spans = ((0, 256, 0), (256, 432, 128), (432, tokens, 384))
    q_turned = q.T
    k_turned = [k[first:last].T for first, last, _ in spans]
    upper = lax.broadcasted_iota(jnp.int32, q_turned.shape, 0) < HDIM
    nothing = jnp.zeros_like(q_turned)
    for h in range(2):
        mine = left if h == 0 else lane >= HDIM
        spare = HDIM * (1 - h)
        q_own = jnp.where(mine, q, zero)
        queries = jnp.where(upper if h == 0 else ~upper, q_turned, nothing)
        heads = slice(HDIM * h, HDIM * (h + 1))
        g_own = jnp.where(mine, scaled, zero)
        high, low = split_low(-inner[h])
        wide = q.shape
        g_more = jnp.where(
            lane == spare,
            jnp.broadcast_to(high, wide),
            jnp.where(lane == spare + 1, jnp.broadcast_to(low, wide), g_own),
        )
        v_more = jnp.where(mine, v, jnp.where((lane >= spare) & (lane < spare + 2), one, zero))
        g_turned = g_more.T
        for (first, last, row), k_part in zip(spans, k_turned):
            score = dot(k[first:last], queries[:, row:])
            key = lax.broadcasted_iota(jnp.int32, score.shape, 0) + first
            weight = jnp.where(key < limit_ref[:, row:], jnp.exp(score), 0.0).astype(BF)
            slope = dot(v_more[first:last], g_turned[:, row:])
            slope = (weight.astype(F32) * slope).astype(BF)
            dv = dot(weight, g_own[row:])
            dk = dot(slope, q_own[row:])
            if h == 0:
                acc_v[first:last, :] = dv
                acc_k[first:last, :] = dk
            else:
                acc_v[first:last, :] += dv
                acc_k[first:last, :] += dk
            acc_q[heads, row:] += dot(k_part[heads], slope)
    gain = gain_ref[...]
    dq, dk = acc_q[...].T, acc_k[...]
    q, k = q.astype(F32), k.astype(F32)
    along = dq * q
    first, second = head_sums(along)
    grad_ref[0] = (
        rq_ref[...] * (dq * gain - q * (jnp.where(left, first, second) / gain))
    ).astype(BF)
    hs_ref[...] = jnp.broadcast_to(jnp.sum(along, axis=0, keepdims=True), hs_ref.shape)
    first, second = head_sums(dk * k)
    grad_ref[1] = (rk_ref[...] * (dk - k * jnp.where(left, first, second))).astype(BF)
    grad_ref[2] = acc_v[...].astype(BF)


def attend_back(qkv, grad, attended, low, inverse, norms, gain, limit, base, some):
    tokens = qkv.shape[0]
    pairs = qkv.shape[1] // (6 * HDIM)
    pair = lambda at: pl.BlockSpec((tokens, 2 * HDIM), lambda p: (0, at + base + p))
    return pl.pallas_call(
        attend_back_body,
        grid=(some,),
        in_specs=[
            pair(0),
            pair(pairs),
            pair(2 * pairs),
            pair(0),
            pair(0),
            pair(0),
            pair(0),
            pair(0),
            pair(pairs),
            pl.BlockSpec((1, 2 * HDIM), lambda p: (0, base + p)),
            whole(limit.shape),
        ],
        out_specs=[
            pl.BlockSpec((3, tokens, 2 * HDIM), lambda p: (0, 0, p)),
            pl.BlockSpec((8, 2 * HDIM), lambda p: (0, p)),
        ],
        out_shape=[
            jax.ShapeDtypeStruct((3, tokens, 2 * HDIM * some), BF),
            jax.ShapeDtypeStruct((8, 2 * HDIM * some), F32),
        ],
        scratch_shapes=[pltpu.VMEM((2 * HDIM, tokens), F32)]
        + [pltpu.VMEM((tokens, 2 * HDIM), F32)] * 2,
        compiler_params=grant(58),
        cost_estimate=cost(
            40 * some * tokens * tokens * HDIM, 60 * tokens * HDIM * some, 2 * some * tokens * tokens
        ),
        name="attend_back",
    )(qkv, qkv, qkv, grad, attended, low, inverse, norms, norms, gain, limit)


def project_body(live_ref, x_ref, att_ref, w_ref, mod_ref, cot_ref, proj_ref, mlp_ref, grad_ref):
    proj_ref[...] = dot(att_ref[...], w_ref[...])
    for rows in row_chunks(x_ref.shape[0]):
        residual = x_ref[rows, :].astype(F32) + mod_ref[0:1, :] * proj_ref[rows, :]
        unit, _ = norm_parts(residual)
        mlp_ref[rows, :] = (unit * (1.0 + mod_ref[3:4, :]) + mod_ref[5:6, :]).astype(BF)
        at = lax.broadcasted_iota(jnp.int32, residual.shape, 0) + rows.start
        live = jnp.where(at < live_ref[0], 1.0, 0.0)
        grad_ref[rows, :] = (mod_ref[1:2, :] * (cot_ref[rows, :].astype(F32) * live)).astype(BF)


def project(live, x, attended, w_vo, mod, cot):
    tokens, width = x.shape
    full = whole((tokens, width))
    return pl.pallas_call(
        project_body,
        grid=(1,),
        in_specs=[
            pl.BlockSpec(memory_space=pltpu.SMEM),
            full,
            full,
            pl.BlockSpec((width, width), lambda _: (0, 3)),
            whole(mod.shape),
            full,
        ],
        out_specs=[full] * 3,
        out_shape=[jax.ShapeDtypeStruct((tokens, width), t) for t in (F32, BF, BF)],
        compiler_params=grant(22),
        cost_estimate=cost(2 * tokens * width * width, 14 * tokens * width + 2 * width * width, 0, 1),
        name="project",
    )(live, x, attended, w_vo, mod, cot)


def residual_back_body(
    live_ref, x_ref, proj_ref, out_ref, gx_ref, cot_ref, mod_ref, w_ref,
    block_ref, resid_ref, gatt_ref, gproj, sums_ref,
):
    totals = [0.0] * 4
    for rows in row_chunks(x_ref.shape[0]):
        proj, mlp_out, g = proj_ref[rows, :], out_ref[rows, :], gx_ref[rows, :]
        residual = x_ref[rows, :].astype(F32) + mod_ref[0:1, :] * proj
        at = lax.broadcasted_iota(jnp.int32, residual.shape, 0) + rows.start
        live = jnp.where(at < live_ref[0], 1.0, 0.0)
        block_ref[rows, :] = ((residual + mod_ref[1:2, :] * mlp_out) * live).astype(BF)
        grad_out = cot_ref[rows, :].astype(F32) * live
        unit, inverse = norm_parts(residual)
        dn = g * (1.0 + mod_ref[3:4, :])
        mean_dn = jnp.mean(dn, axis=-1, keepdims=True)
        mean_in = jnp.mean(dn * unit, axis=-1, keepdims=True)
        grad_resid = grad_out + inverse * (dn - mean_dn - unit * mean_in)
        resid_ref[rows, :] = grad_resid
        gproj[rows, :] = (mod_ref[0:1, :] * grad_resid).astype(BF)
        for i, part in enumerate((grad_resid * proj, grad_out * mlp_out, g * unit, g)):
            totals[i] = totals[i] + jnp.sum(part, axis=0, keepdims=True)
    for i in range(4):
        sums_ref[i : i + 1, :] = totals[i]
    sums_ref[4:, :] = jnp.zeros((4, sums_ref.shape[1]), F32)
    gatt_ref[...] = dot(gproj[...], w_ref[...], LAST).astype(BF)


def residual_back(live, x, proj, mlp_out, gx, cot, mod, weights):
    tokens, width = x.shape
    full = whole((tokens, width))
    return pl.pallas_call(
        residual_back_body,
        grid=(1,),
        in_specs=[
            pl.BlockSpec(memory_space=pltpu.SMEM),
            full,
            full,
            full,
            full,
            full,
            whole(mod.shape),
            pl.BlockSpec((width, width), lambda _: (0, 3)),
        ],
        out_specs=[full, full, full, full, whole((8, width))],
        out_shape=[jax.ShapeDtypeStruct((tokens, width), t) for t in (BF, F32, BF, BF)]
        + [jax.ShapeDtypeStruct((8, width), F32)],
        compiler_params=grant(58),
        cost_estimate=cost(2 * tokens * width * width, 28 * tokens * width + 4 * width * width),
        name="residual_back",
    )(live, x, proj, mlp_out, gx, cot, mod, weights)


def weight_grad_body(core_ref, x_ref, g_ref, att_ref, proj_ref, keep_a, send_a, keep_b, send_b):
    step = pl.program_id(0)
    core = core_ref[0]

    @pl.when(step < 2)
    def _():
        keep_a[...], send_a[...] = halves_of(dot(x_ref[...], g_ref[0], FIRST), core)

    @pl.when(step == 2)
    def _():
        keep_b[...], send_b[...] = halves_of(dot(x_ref[...], g_ref[0], FIRST), core)

    @pl.when(step == 3)
    def _():
        keep_b[...], send_b[...] = halves_of(dot(att_ref[...], proj_ref[...], FIRST), core)


def weight_grad(core, x, g, attended, grad_proj):
    tokens, width = x.shape
    full = whole((tokens, width))
    part = (BLOCKS // 2, width // BLOCKS, width)
    first = pl.BlockSpec(part, lambda n: (0, 0, jnp.minimum(n, 1)))
    second = pl.BlockSpec(part, lambda n: (0, 0, jnp.maximum(n - 2, 0)))
    return pl.pallas_call(
        weight_grad_body,
        grid=(4,),
        in_specs=[
            pl.BlockSpec(memory_space=pltpu.SMEM),
            full,
            pl.BlockSpec((1, tokens, width), lambda n: (jnp.minimum(n, 2), 0, 0)),
            full,
            full,
        ],
        out_specs=[first, first, second, second],
        out_shape=[jax.ShapeDtypeStruct(part[:2] + (2 * width,), BF)] * 4,
        compiler_params=grant(58),
        cost_estimate=cost(8 * tokens * width * width, 12 * tokens * width + 8 * width * width),
        name="weight_grad",
    )(core, x, g, attended, grad_proj)


def input_back_body(x_ref, resid_ref, mod_ref, g_ref, w_ref, out_ref, sums_ref):
    step = pl.program_id(0)
    part = dot(g_ref[0], w_ref[...], LAST)

    @pl.when(step == 0)
    def _():
        out_ref[...] = part

    @pl.when(step > 0)
    def _():
        out_ref[...] += part

    @pl.when(step == 2)
    def _():
        totals = [0.0] * 2
        for rows in row_chunks(x_ref.shape[0]):
            g = out_ref[rows, :]
            unit, inverse = norm_parts(x_ref[rows, :].astype(F32))
            dn = g * (1.0 + mod_ref[2:3, :])
            mean_dn = jnp.mean(dn, axis=-1, keepdims=True)
            mean_in = jnp.mean(dn * unit, axis=-1, keepdims=True)
            out_ref[rows, :] = resid_ref[rows, :] + inverse * (dn - mean_dn - unit * mean_in)
            for i, part in enumerate((g * unit, g)):
                totals[i] = totals[i] + jnp.sum(part, axis=0, keepdims=True)
        for i in range(2):
            sums_ref[i : i + 1, :] = totals[i]
        sums_ref[2:, :] = jnp.zeros((6, x_ref.shape[1]), F32)


def input_back(x, resid, mod, g, weights):
    tokens, width = x.shape
    full = whole((tokens, width))
    return pl.pallas_call(
        input_back_body,
        grid=(3,),
        in_specs=[
            full,
            full,
            whole(mod.shape),
            pl.BlockSpec((1, tokens, width), lambda n: (n, 0, 0)),
            pl.BlockSpec((width, width), lambda n: (0, n)),
        ],
        out_specs=[full, whole((8, width))],
        out_shape=[
            jax.ShapeDtypeStruct((tokens, width), F32),
            jax.ShapeDtypeStruct((8, width), F32),
        ],
        compiler_params=grant(58),
        cost_estimate=cost(6 * tokens * width * width, 16 * tokens * width + 6 * width * width),
        name="input_back",
    )(x, resid, mod, g, weights)


def mlp_body(info_ref, x_ref, g_ref, bias_ref, *refs, first, sources):
    a_refs, b_refs, refs = refs[:sources], refs[sources : 2 * sources], refs[2 * sources :]
    if first:
        out_ref, gx_ref, keep_a, send_a, keep_b, send_b, bias_g, up_w, down_w = refs
    else:
        out_in, gx_in, out_ref, gx_ref, keep_a, send_a, keep_b, send_b, bias_g, up_w, down_w = refs
    core = info_ref[2, 0]
    block = x_ref.shape[1] // BLOCKS

    @pl.when(pl.program_id(0) == 0)
    def _():
        out_ref[...] = jnp.zeros_like(out_ref) if first else out_in[...]
        gx_ref[...] = jnp.zeros_like(gx_ref) if first else gx_in[...]

    step = pl.program_id(0)
    size = up_w.shape[1]
    per = down_w.shape[0] // size
    fill(up_w, info_ref.at[0], paired(a_refs), block)

    @pl.when(step % per == 0)
    def _():
        fill(down_w, info_ref.at[1], paired(b_refs), block)

    root = np.float32(np.sqrt(2.0 / np.pi))
    x, g, up = x_ref[...], g_ref[...], up_w[...]
    down = down_w[pl.ds(pl.multiple_of(step % per * size, size), size), :]
    hidden = dot(x, up) + bias_ref[...]
    square = hidden * hidden
    bend = jnp.tanh(root * hidden * (1.0 + 0.044715 * square))
    act = (0.5 * hidden * (1.0 + bend)).astype(BF)
    out_ref[...] += dot(act, down)
    slope = 0.5 * (1.0 + bend) + 0.5 * hidden * (1.0 - bend * bend) * root * (
        1.0 + (3 * 0.044715) * square
    )
    grad_hidden = (dot(g, down, LAST) * slope).astype(BF)
    bias_g[...] = jnp.sum(grad_hidden.astype(F32), axis=0, keepdims=True)
    gx_ref[...] += dot(grad_hidden, up, LAST)
    keep_b[...], send_b[...] = halves_of(dot(act, g, FIRST), core, BLOCKS // per)
    keep_a[...], send_a[...] = halves_of(dot(x, grad_hidden, FIRST), core)


def mlp(info, x, g, pieces, bias, at, carried=None):
    tokens, width = x.shape
    block, per = 512, width // 512
    lead, rows = BLOCKS // 2, width // BLOCKS
    part_a = pl.BlockSpec((lead, rows, block), lambda f: (0, 0, f))
    if len(pieces) == 3:
        matrices = (*pieces[1], *pieces[2])
        total = matrices[0].shape[2]
        sources = [
            pl.BlockSpec(m.shape[:2] + (block,), lambda f: (0, 0, f)) for m in pieces[1]
        ] + [pl.BlockSpec(m.shape[:2] + (width,), lambda f: (0, 0, f // per)) for m in pieces[2]]
    else:
        matrices = [pieces[0].reshape(lead, 2, rows, -1)] * 4
        total = matrices[0].shape[3] // 2
        skip = total // width
        sources = [
            pl.BlockSpec((lead, None, rows, block), lambda f: (0, 0, 0, f)),
            pl.BlockSpec((lead, None, rows, block), lambda f: (0, 1, 0, f)),
            pl.BlockSpec((lead, None, rows, width), lambda f: (0, 0, 0, skip + f // per)),
            pl.BlockSpec((lead, None, rows, width), lambda f: (0, 1, 0, skip + f // per)),
        ]
    steps = total // block
    grad_b = pl.BlockSpec((lead // per, rows, width), lambda f: (f % per, 0, f // per))
    single = pl.BlockSpec((tokens, width), lambda f: (0, 0), pipeline_mode=pl.Buffered(1))
    carried = () if carried is None else tuple(carried)
    return pl.pallas_call(
        partial(mlp_body, first=not carried, sources=len(matrices) // 2),
        grid=(steps,),
        in_specs=[pl.BlockSpec(memory_space=pltpu.SMEM), single, single]
        + [pl.BlockSpec((1, block), lambda f: (0, at * per + f))]
        + sources
        + [single] * len(carried),
        out_specs=[single, single, part_a, part_a, grad_b, grad_b]
        + [pl.BlockSpec((1, block), lambda f: (0, f))],
        out_shape=[jax.ShapeDtypeStruct((tokens, width), F32)] * 2
        + [jax.ShapeDtypeStruct((lead, rows, total), BF)] * 4
        + [jax.ShapeDtypeStruct((1, total), F32)],
        scratch_shapes=[pltpu.VMEM((width, block), BF), pltpu.VMEM((width, width), BF)],
        input_output_aliases={4 + len(matrices) + i: i for i in range(len(carried))},
        compiler_params=grant(58),
        cost_estimate=cost(
            12 * tokens * width * total,
            (8 + 8 * len(carried)) * tokens * width + 8 * total * width,
            tokens * total,
            20 if carried else 0.3,
        ),
        name="mlp",
    )(info, x, g, bias, *matrices, *carried)


def fold_body(bit_ref, *refs, plan, out_count):
    ins, outs = refs[:-out_count], refs[-out_count:]
    for source, cols, bit, stride, out, column in plan:
        kept, came = ins[2 * source], ins[2 * source + 1]
        at_cols = slice(column, column + cols.stop - cols.start)
        if bit is None:
            outs[out][:, :, at_cols] = kept[:, :, cols].astype(F32) + came[:, :, cols].astype(F32)
            continue
        mine = bit_ref[bit]
        for m in range(kept.shape[0] // 2):
            base = m // stride * 2 * stride + m % stride
            for side, value in ((0, mine), (1, 1 - mine)):
                at = base + value * stride
                outs[out + side][m, :, at_cols] = (
                    kept[at, :, cols].astype(F32) + came[at, :, cols].astype(F32)
                ).astype(BF)


def fold(bits, parts, plan, outs, split=1, weight=0):
    def spec(shape):
        return pl.BlockSpec(tuple(shape[:2]) + (shape[2] // split,), lambda n: (0, 0, n))

    return pl.pallas_call(
        partial(fold_body, plan=plan, out_count=len(outs)),
        grid=(split,),
        in_specs=[pl.BlockSpec(memory_space=pltpu.SMEM)] + [spec(p.shape) for p in parts],
        out_specs=[spec(s) for s, _ in outs],
        out_shape=[jax.ShapeDtypeStruct(s, t) for s, t in outs],
        compiler_params=grant(58),
        cost_estimate=cost(weight, 8),
        name="fold",
    )(bits, *parts)


def swap(block, count, mask):
    return lax.ppermute(block, AXES, [(i, i ^ mask) for i in range(count)])


def after(value, *others):
    return lax.optimization_barrier((value,) + others)


def join(block, came):
    return jnp.concatenate([block, came])


def codes(order, me):
    code = [0]
    for bit in order:
        code = code + [c | (1 << bit) for c in code]
    return jnp.asarray(np.array(code, np.int32)) ^ me


def gathered_pieces(full):
    rows, cols = full.shape
    cut = full.reshape(BLOCKS // 2, 2, rows // BLOCKS, 2, cols // 2)
    return [tuple(cut[:, i, :, j] for i in range(2)) for j in range(2)]


def halve(pieces, axis, bit_value, count, mask):
    total = pieces[0]
    if len(pieces) > 1:
        total = (pieces[0].astype(F32) + pieces[1].astype(F32)).astype(BF)
    keep = lax.dynamic_index_in_dim(total, bit_value, axis, keepdims=False)
    send = lax.dynamic_index_in_dim(total, 1 - bit_value, axis, keepdims=False)
    return [keep, swap(send, count, mask)]


def scatter_rows(kept, send, count, me):
    grads = [jnp.stack(pair, axis=1).reshape(-1, pair[0].shape[2]) for pair in zip(kept, send)]
    grad = jnp.concatenate(grads, axis=1)
    rows, width = grad.shape
    bits = count.bit_length() - 1
    own = rows // count
    bit = [lax.rem(lax.div(me, np.int32(1 << b)), np.int32(2)) for b in range(bits)]
    part = [grad.reshape((2,) * bits + (own, width))]
    for b in range(bits):
        part = halve(part, bits - 1 - b, bit[b], count, 1 << b)
    return (part[0].astype(F32) + part[1].astype(F32)).reshape(own, width)


def tie(*groups):
    flat = lax.optimization_barrier(tuple(a for g in groups for a in g))
    for g in groups:
        g[:], flat = flat[: len(g)], flat[len(g) :]


def land(value, *moves):
    box = [value]
    tie(box, *[m.came for m in moves])
    return box[0]


def leave(value, *scatters):
    for s in scatters:
        s.add()
    box = [value]
    tie(box, *[s.send for s in scatters])
    for s in scatters:
        if s.done is None:
            s.start()
    return box[0]


class Gather:
    def __init__(self, shard, count):
        self.count = count
        self.block = shard[None]
        self.came = None

    def start_z(self, bit):
        self.came = [swap(self.block, self.count, 1 << bit)]

    def end_z(self):
        self.block = join(self.block, self.came[0])

    def start_xy(self, first, second):
        if not isinstance(self.block, list):
            half = self.block.shape[2] // 2
            self.block = [self.block[:, :, :half], self.block[:, :, half:]]
        self.came = [
            swap(b, self.count, 1 << bit) for b, bit in zip(self.block, (first, second))
        ]

    def end_xy(self):
        self.block = [join(b, c) for b, c in zip(self.block, self.came)]

    def start_early(self):
        self.early = [swap(b, self.count, 1) for b in self.block]

    def start_late(self):
        self.late = [swap(c, self.count, 1) for c in self.came]

    def pieces(self, code):
        sides = [
            (b, e, c, l) for b, e, c, l in zip(self.block, self.early, self.came, self.late)
        ]
        return (code, *sides)


class Scatter:
    def __init__(self, kept, send, pieces, bits, count, heavy=0):
        self.bits, self.count, self.heavy = bits, count, heavy
        self.pieces = pieces
        self.kept, self.send = list(kept), list(send)
        self.left = 0
        self.done = None
        self.start()

    def start(self):
        masks = ([1] * len(self.send), (2, 4), (4, 2), (8,), (16,))[self.left]
        self.came = [swap(s, self.count, mask) for s, mask in zip(self.send, masks)]
        self.left += 1

    def add(self):
        parts = [p for pair in zip(self.kept, self.came) for p in pair]
        lead, own, width = self.kept[0].shape
        split = {1: 2, 2: 2}.get(self.left, 1)
        everything = slice(0, width // split)
        half = lambda cols: ((lead // 2, own, cols), BF)
        if self.left == 5:
            plan, outs, at = [], [], 0
            for i, cols in enumerate(self.pieces):
                plan.append((0, slice(at, at + cols), None, 1, i, 0))
                outs.append(((lead, own, cols), F32))
                at += cols
        elif self.left == 1:
            plan, sums = [], [0, 0]
            for side in range(2):
                plan.append((side, everything, (1, 2)[side], (1, 2)[side], 2 * side, 0))
            outs = [half(width)] * 4
        elif self.left == 2:
            plan = tuple((i, everything, 2 - i, 1, 2 * i, 0) for i in range(2))
            outs = [half(width)] * 4
        elif self.left == 3:
            plan = tuple((i, everything, 3, 1, 0, i * width) for i in range(2))
            outs = [half(2 * width)] * 2
        else:
            plan = ((0, everything, 4, 1, 0, 0),)
            outs = [half(width)] * 2
        weight = self.heavy if self.left == 5 else 0
        outs = fold(self.bits, parts, tuple(plan), outs, split, weight)
        if self.left == 5:
            self.done, self.send = [o[0] for o in outs], list(outs)
        else:
            self.kept, self.send = list(outs[0::2]), list(outs[1::2])


def per_device(
    tokens,
    labels,
    stop_scale,
    class_table,
    ada_weight,
    ada_bias,
    qkv_weight,
    head_scale,
    out_weight,
    up_weight,
    up_bias,
    down_weight,
    cotangent,
    count,
):
    image_count, seq_len, model_width = tokens.shape
    row_count = image_count * seq_len
    me = lax.axis_index(AXES).astype(jnp.int32)
    levels = position_scale(SCALES)
    ends = jnp.asarray(LEVEL_ENDS)
    live = jnp.take(ends, stop_scale - 1).astype(jnp.int32)
    limit = jnp.asarray(LEVEL_ENDS[levels][None, :])
    start = jnp.asarray((LEVEL_ENDS - np.square(np.array(scale_sides)))[levels][None, :].astype(np.int32))
    class_count = class_table.shape[0]
    own = model_width // count
    ratio = down_weight.shape[0] // own
    hidden_width = up_weight.shape[1]

    def hidden_order(matrix):
        lead = matrix.shape[:-1]
        cut = matrix.reshape(lead + (count, ratio, own))
        return jnp.swapaxes(cut, -3, -2).reshape(lead + (hidden_width,))

    def hidden_back(matrix):
        lead = matrix.shape[:-1]
        cut = matrix.reshape(lead + (ratio, count, own))
        return jnp.swapaxes(cut, -3, -2).reshape(lead + (hidden_width,))

    down_wide = jnp.swapaxes(down_weight.reshape(ratio, own, model_width), 0, 1).reshape(
        own, hidden_width
    )
    half = hidden_width // 2
    up_order = hidden_order(up_weight)
    shards = [jnp.concatenate([qkv_weight, out_weight], axis=1)] + [
        jnp.concatenate([m[:, i : i + half] for m in (up_order, down_wide)], axis=1)
        for i in (0, half)
    ]
    quick = count == BLOCKS and own % 16 == 0
    plain = jnp.asarray(np.tile(np.arange(0, BLOCKS, 2, dtype=np.int32), (2, 1)))
    if quick:
        one, two = [Gather(s, count) for s in shards[:2]]
        orders = ((4, 3, 2, 1), (4, 3, 1, 2))
        code = jnp.stack([codes(o, me) for o in orders])
        bits = jnp.stack([lax.rem(lax.div(me, np.int32(1 << b)), np.int32(2)) for b in range(5)])
        one.start_z(4)
        one.came[0], two.block = after(one.came[0], two.block)
        one.end_z()
        one.start_z(3)
    else:
        wide = [lax.all_gather(s, AXES, axis=0, tiled=True) for s in shards]
        code = plain
        bits = jnp.zeros((5,), jnp.int32)
    core = bits[:1]
    info, info_plain = [
        jnp.concatenate([c, jnp.full((1, c.shape[1]), bits[0])]) for c in (code, plain)
    ]

    first_row = jnp.concatenate(
        [lax.div(labels, 32).astype(BF), lax.rem(labels, 32).astype(BF), up_bias]
    )
    rows = lax.all_to_all(
        jnp.broadcast_to(first_row[None, :], (count, first_row.shape[0])), AXES, 0, 0, tiled=True
    )
    labels_all = 32 * rows[:, 0].astype(jnp.int32) + rows[:, 1].astype(jnp.int32)
    up_bias_full = rows[:, 2:].astype(F32).reshape(1, hidden_width)
    onehot = labels_all[:, None] == jnp.arange(class_count, dtype=jnp.int32)[None, :]
    condition = jnp.dot(onehot.astype(BF), class_table, preferred_element_type=F32)
    cond_act = jax.nn.silu(condition).astype(BF)
    exponent = count.bit_length() - 1
    order = tuple(range(exponent - 1, -1, -1)) + (exponent,)
    backwards = cond_act.reshape((2,) * exponent + (own,)).transpose(order).reshape(count, own)
    modul_part = jnp.dot(backwards, ada_weight, preferred_element_type=F32)
    bias_own = ada_bias.shape[0]
    bias_row = lax.dynamic_update_slice(
        jnp.zeros((6 * model_width,), F32), ada_bias.astype(F32), (me * bias_own,)
    )
    part = modul_part + bias_row[None, :]
    bit_values = [lax.rem(lax.div(me, np.int32(1 << b)), np.int32(2)) for b in range(exponent)]
    for b in range(exponent):
        size = part.shape[0] // 2
        keep = lax.dynamic_slice_in_dim(part, bit_values[b] * size, size)
        send = lax.dynamic_slice_in_dim(part, (1 - bit_values[b]) * size, size)
        came = swap(send, count, 1 << b)
        if quick and b == 0:
            came = land(came, one)
            one.end_z()
            came, two.block = after(came, two.block)
            one.start_xy(2, 1)
            two.start_z(4)
        elif quick and b == 2:
            came = land(came, one, two)
            one.end_xy()
            two.end_z()
            one.start_early()
            one.start_xy(1, 2)
            two.start_z(3)
        part = keep + came
    mod = part.reshape(6, model_width)
    if quick:
        mod = land(mod, one, two)
        two.end_z()
        one.start_late()
        two.start_xy(2, 1)
        pieces = one.pieces(code)
    else:
        pieces = (code, *gathered_pieces(wide[0]))
    heads = head_scale.shape[0]
    gain = jnp.repeat(jnp.exp(head_scale), HDIM)[None, :]
    seg = jnp.asarray(
        np.arange(model_width)[:, None] // HDIM == np.arange(128)[None, :], dtype=BF
    )
    x = tokens.reshape(row_count, model_width)
    cot = cotangent.reshape(row_count, model_width)

    attn_in, qkv, norms, weights = qkv_rows(x, mod, pieces, gain, seg)
    if quick:
        qkv = land(qkv, two)
        two.end_xy()
        qkv, last_shard, *two.block = after(qkv, shards[2], *two.block)
        last_full = lax.all_gather(last_shard, AXES, axis=0, tiled=True)
        two.start_early()
        two.start_xy(1, 2)
    attended, low, inverse = attend(qkv, start)
    projected, mlp_in, grad_mlp = project(live, x, attended, weights, mod, cot)
    if quick:
        mlp_in = land(mlp_in, two)
        two.start_late()
    bias = hidden_order(up_bias_full)
    pieces = two.pieces(code) if quick else (wide[1],)
    *carried, keep_a, send_a, keep_b, send_b, bias_one = mlp(info, mlp_in, grad_mlp, pieces, bias, 0)
    kept_one, send_one = (keep_a, keep_b), (send_a, send_b)
    if quick:
        first = Scatter(kept_one, send_one, (half, half), bits, count, 1 << 33)
        carried[0] = land(carried[0], first)
        carried[0] = leave(carried[0], first)
    pieces = (last_full if quick else wide[2],)
    mlp_out, grad_mlp_in, keep_a, send_a, keep_b, send_b, bias_two = mlp(
        info_plain, mlp_in, grad_mlp, pieces, bias, half // model_width, carried
    )
    kept_two, send_two = (keep_a, keep_b), (send_a, send_b)
    if quick:
        second = Scatter(kept_two, send_two, (half, half), bits, count)
        mlp_out = land(mlp_out, first)
        mlp_out = leave(mlp_out, first)
    block_out, grad_resid, grad_attended, grad_proj, sums_two = residual_back(
        live, x, projected, mlp_out, grad_mlp_in, cot, mod, weights
    )
    if quick:
        grad_attended = land(grad_attended, first, second)
        grad_attended = leave(grad_attended, first, second)
    dqkv, head_sums = attend_back(
        qkv, grad_attended, attended, low, inverse, norms, gain, limit, 0, heads // 2
    )
    if quick:
        dqkv = land(dqkv, first, second)
        dqkv = leave(dqkv, first, second)
    keep_a, send_a, keep_b, send_b = weight_grad(core, attn_in, dqkv, attended, grad_proj)
    kept_three, send_three = (keep_a, keep_b), (send_a, send_b)
    if quick:
        third = Scatter(
            kept_three, send_three, (3 * model_width, model_width), bits, count
        )
        dqkv = land(dqkv, first, second)
        dqkv = leave(dqkv, first, second)
        dqkv = land(dqkv, third)
        dqkv = leave(dqkv, third)
    input_grad, sums_one = input_back(x, grad_resid, mod, dqkv, weights)
    if not quick:
        mlp_own = [
            scatter_rows(kept_one, send_one, count, me),
            scatter_rows(kept_two, send_two, count, me),
        ]
        up_own = jnp.concatenate([m[:, :half] for m in mlp_own], axis=1)
        down_own = jnp.concatenate([m[:, half:] for m in mlp_own], axis=1)
        attn_own = scatter_rows(kept_three, send_three, count, me)
        qkv_own, out_own = attn_own[:, : 3 * model_width], attn_own[:, 3 * model_width :]
    block_out = block_out.reshape(tokens.shape)
    input_grad = input_grad.reshape(tokens.shape)
    if quick:
        sums_one, bias_one, bias_two, head_sums, sums_two = after(
            sums_one, bias_one, bias_two, head_sums, sums_two
        )
    up_bias_grad = jnp.concatenate([bias_one, bias_two], axis=1)
    grad_modul = jnp.concatenate(
        [sums_two[0], sums_two[1], sums_one[0], sums_two[2], sums_one[1], sums_two[3]]
    ).astype(BF)
    head_scale_part = jnp.sum(head_sums[0].reshape(heads, HDIM), axis=1)
    bias_high, bias_low = split_low(hidden_back(up_bias_grad).reshape(count, -1))
    head_high, head_low = split_low(head_scale_part)
    common = jnp.concatenate([grad_modul.reshape(-1), head_high, head_low])
    small = jnp.concatenate(
        [jnp.broadcast_to(common[None, :], (count, common.shape[0])), bias_high, bias_low], axis=1
    )
    small = lax.all_to_all(small, AXES, 0, 0, tiled=True)
    if quick:
        input_grad = land(input_grad, second, third)
        input_grad = leave(input_grad, second, third)
        input_grad = land(input_grad, second, third)
        input_grad = leave(input_grad, second, third)
        input_grad = land(input_grad, third)
        small, input_grad = after(small, input_grad)
        small = leave(small, third)
        third.add()
        up_own, down_own = [jnp.concatenate(m, axis=1) for m in zip(first.done, second.done)]
        qkv_own, out_own = third.done
    modul_cols = image_count * 6 * model_width
    grad_modul_all = small[:, :modul_cols].reshape(count * image_count, 6 * model_width)
    tail = jnp.sum(small[:, modul_cols:].astype(F32), axis=0)
    head_scale_grad = tail[:heads] + tail[heads : 2 * heads]
    tail = tail[2 * heads :].reshape(2, -1)
    up_bias_own = tail[0] + tail[1]
    ada_bias_own = jnp.sum(
        lax.dynamic_slice_in_dim(grad_modul_all, me * bias_own, bias_own, axis=1).astype(F32), axis=0
    )
    ada_own = lax.dot_general(
        cond_act, grad_modul_all, (((0,), (0,)), ((), ())), preferred_element_type=F32
    )
    grad_cond_act = lax.dot_general(
        grad_modul_all, ada_weight, (((1,), (1,)), ((), ())), preferred_element_type=F32
    )
    grad_condition = jax.vjp(jax.nn.silu, condition)[1](grad_cond_act)[0]
    table_own = lax.dot_general(
        onehot.astype(F32),
        grad_condition,
        (((0,), (0,)), ((), ())),
        precision=lax.Precision.HIGHEST,
        preferred_element_type=F32,
    )
    up_own = hidden_back(up_own)
    down_own = jnp.swapaxes(down_own.reshape(own, ratio, model_width), 0, 1).reshape(
        ratio * own, model_width
    )
    return (
        block_out,
        input_grad,
        table_own,
        ada_own,
        ada_bias_own,
        qkv_own,
        head_scale_grad,
        out_own,
        up_own,
        up_bias_own,
        down_own,
    )


def solution(mesh):
    count = mesh.shape["wide"] * mesh.shape["narrow"]
    both = AXES
    in_specs = (
        P(both, None, None),
        P(both),
        P(both),
        P(None, both),
        P(both, None),
        P(both),
        P(both, None),
        P(),
        P(both, None),
        P(both, None),
        P(both),
        P(both, None),
        P(both, None, None),
    )
    out_specs = (
        P(both, None, None),
        P(both, None, None),
        P(None, both),
        P(both, None),
        P(both),
        P(both, None),
        P(),
        P(both, None),
        P(both, None),
        P(both),
        P(both, None),
    )
    return jax.shard_map(
        partial(per_device, count=count),
        mesh=mesh,
        in_specs=in_specs,
        out_specs=out_specs,
        check_vma=False,
    )
```

```python
from functools import partial

import jax
import jax.numpy as jnp
import numpy as np
from jax import lax
from jax.experimental import pallas as pl
from jax.experimental.pallas import tpu as pltpu
from jax.sharding import PartitionSpec as P

HDIM = 64
SCALES = 10
AXES = ("wide", "narrow")
BF = jnp.bfloat16
F32 = jnp.float32

scale_sides = (1, 2, 3, 4, 5, 6, 8, 10, 13, 16)


def position_scale(scale_count):
    return np.concatenate(
        [
            np.full(side_size * side_size, level_index, dtype=np.int32)
            for level_index, side_size in enumerate(scale_sides[:scale_count])
        ]
    )


BLOCKS = 32
LEVEL_ENDS = np.cumsum(np.square(np.array(scale_sides))).astype(np.int32)
LAST = (((1,), (1,)), ((), ()))
FIRST = (((0,), (0,)), ((), ()))


def grant(mebibytes):
    return pltpu.CompilerParams(vmem_limit_bytes=mebibytes << 20)


def dot(left, right, dims=(((1,), (0,)), ((), ()))):
    return lax.dot_general(left, right, dims, preferred_element_type=F32)


def split_low(value):
    high = value.astype(BF)
    return high, (value - high.astype(F32)).astype(BF)


def row_chunks(total, step=80):
    return [slice(i, min(i + step, total)) for i in range(0, total, step)]


def norm_parts(value):
    centred = value - jnp.mean(value, axis=-1, keepdims=True)
    inverse = lax.rsqrt(jnp.mean(centred * centred, axis=-1, keepdims=True) + 1e-06)
    return centred * inverse, inverse


def cost(flops, read, exps=0, scale=20):
    return pl.CostEstimate(flops=int(scale * flops), bytes_accessed=int(scale * read), transcendentals=int(scale * exps))


def whole(shape):
    return pl.BlockSpec(shape, lambda *_: (0,) * len(shape), pipeline_mode=pl.Buffered(1))


def fill(dst, code, pairs, block):
    position = 0
    for own, other in pairs:
        for m in range(own.shape[0]):
            at = code[position]
            dst[pl.ds(pl.multiple_of(at * block, block), block), :] = own[m]
            at = at ^ 1
            dst[pl.ds(pl.multiple_of(at * block, block), block), :] = other[m]
            position += 1


def paired(refs):
    return list(zip(refs[0::2], refs[1::2]))


def halves_of(value, core, count=None):
    rows, cols = value.shape
    block = rows // (count or BLOCKS)
    cut = value.reshape(rows // (2 * block), 2, block, cols)
    even, odd = cut[:, 0], cut[:, 1]
    return (
        jnp.where(core == 0, even, odd).astype(BF),
        jnp.where(core == 0, odd, even).astype(BF),
    )


def qkv_body(code_ref, x_ref, mod_ref, gain_ref, seg_ref, *refs):
    *sources, attn_ref, out_ref, inv_ref, w_ref = refs
    half = len(sources) // 2
    first, second = paired(sources[:half]), paired(sources[half:])
    step = pl.program_id(0)
    block = x_ref.shape[1] // BLOCKS

    @pl.when(step == 0)
    def _():
        for rows in row_chunks(x_ref.shape[0]):
            unit, _ = norm_parts(x_ref[rows, :].astype(F32))
            attn_ref[rows, :] = (unit * (1.0 + mod_ref[2:3, :]) + mod_ref[4:5, :]).astype(BF)

    @pl.when(step < 2)
    def _():
        fill(w_ref, code_ref.at[0], first, block)
        raw = dot(attn_ref[...], w_ref[...])
        seg = seg_ref[...]
        high, low = split_low(raw * raw)
        inverse = lax.rsqrt(dot(high, seg) + dot(low, seg) + 1e-06)
        high, low = split_low(inverse)
        spread = dot(high, seg, LAST) + dot(low, seg, LAST)
        gain = jnp.where(step == 0, gain_ref[...], 1.0)
        out_ref[...] = (raw * spread * gain).astype(BF)
        inv_ref[...] = spread.astype(BF)

    @pl.when(step >= 2)
    def _():
        fill(w_ref, code_ref.at[1], second, block)

    @pl.when(step == 2)
    def _():
        out_ref[...] = dot(attn_ref[...], w_ref[...]).astype(BF)


def qkv_rows(x, mod, pieces, gain, seg):
    tokens, width = x.shape
    code, first, second = pieces
    one = [
        pl.BlockSpec(a.shape[:2] + (width,), lambda n: (0, 0, jnp.minimum(n, 1))) for a in first
    ]
    two = [
        pl.BlockSpec(a.shape[:2] + (width,), lambda n: (0, 0, jnp.maximum(n - 2, 0)))
        for a in second
    ]
    return pl.pallas_call(
        qkv_body,
        grid=(4,),
        in_specs=[
            pl.BlockSpec(memory_space=pltpu.SMEM),
            whole((tokens, width)),
            whole(mod.shape),
            whole(gain.shape),
            whole(seg.shape),
            *one,
            *two,
        ],
        out_specs=[
            whole((tokens, width)),
            pl.BlockSpec((tokens, width), lambda n: (0, jnp.minimum(n, 2))),
            pl.BlockSpec((tokens, width), lambda n: (0, jnp.minimum(n, 1))),
            pl.BlockSpec((width, width), lambda n: (0, n)),
        ],
        out_shape=[
            jax.ShapeDtypeStruct((tokens, width), BF),
            jax.ShapeDtypeStruct((tokens, 3 * width), BF),
            jax.ShapeDtypeStruct((tokens, 2 * width), BF),
            jax.ShapeDtypeStruct((width, 4 * width), BF),
        ],
        compiler_params=grant(58),
        cost_estimate=cost(6 * tokens * width * width, 16 * tokens * width + 16 * width * width, 0, 2),
        name="qkv",
    )(code, x, mod, gain, seg, *first, *second)


def attend_body(q_ref, k_ref, v_ref, start_ref, out_ref, low_ref, inv_ref):
    q, k, v = q_ref[...], k_ref[...], v_ref[...]
    lane = lax.broadcasted_iota(jnp.int32, q.shape, 1)
    zero = jnp.zeros_like(q)
    one = jnp.ones_like(q)
    tokens = q.shape[0]
    queries = [jnp.where(lane < HDIM, q, zero), jnp.where(lane >= HDIM, q, zero)]
    values = [
        jnp.where(lane < HDIM, v, jnp.where(lane == HDIM, one, zero)),
        jnp.where(lane >= HDIM, v, jnp.where(lane == 0, one, zero)),
    ]
    for first, last, keys in ((0, 240, 256), (240, 416, 432), (416, tokens, tokens)):
        row = lax.broadcasted_iota(jnp.int32, (last - first, keys), 0) + first
        seen = row >= start_ref[:, :keys]
        tiles, sums = [], []
        for h in range(2):
            score = dot(queries[h][first:last], k[:keys], LAST)
            weight = jnp.where(seen, jnp.exp(score), 0.0).astype(BF)
            tile = dot(weight, values[h][:keys])
            inverse = 1.0 / tile[:, HDIM * (1 - h) : HDIM * (1 - h) + 1]
            tiles.append(tile * inverse)
            sums.append(jnp.broadcast_to(inverse, tile.shape))
        left = lane[first:last] < HDIM
        high, low = split_low(jnp.where(left, tiles[0], tiles[1]))
        out_ref[first:last, :] = high
        low_ref[first:last, :] = low
        inv_ref[first:last, :] = jnp.where(left, sums[0], sums[1])


def attend(qkv, start):
    tokens = qkv.shape[0]
    pairs = qkv.shape[1] // (6 * HDIM)
    pair = lambda base: pl.BlockSpec((tokens, 2 * HDIM), lambda p: (0, base + p))
    return pl.pallas_call(
        attend_body,
        grid=(pairs,),
        in_specs=[pair(0), pair(pairs), pair(2 * pairs), whole(start.shape)],
        out_specs=[pair(0), pair(0), pair(0)],
        out_shape=[
            jax.ShapeDtypeStruct((tokens, 2 * HDIM * pairs), BF),
            jax.ShapeDtypeStruct((tokens, 2 * HDIM * pairs), BF),
            jax.ShapeDtypeStruct((tokens, 2 * HDIM * pairs), F32),
        ],
        compiler_params=grant(12),
        cost_estimate=cost(
            16 * pairs * tokens * tokens * HDIM, 20 * tokens * HDIM * pairs, 2 * pairs * tokens * tokens, 0.02
        ),
        name="attend",
    )(qkv, qkv, qkv, start)


def attend_back_body(
    q_ref, k_ref, v_ref, g_ref, att_ref, low_ref, inv_ref, rq_ref, rk_ref, gain_ref, limit_ref,
    grad_ref, hs_ref, acc_q, acc_k, acc_v,
):
    q, k, v = q_ref[...], k_ref[...], v_ref[...]
    tokens = q.shape[0]
    lane = lax.broadcasted_iota(jnp.int32, q.shape, 1)
    zero, one = jnp.zeros_like(q), jnp.ones_like(q)
    left = lane < HDIM

    def head_sums(value):
        first = jnp.sum(jnp.where(left, value, 0.0), axis=1, keepdims=True)
        second = jnp.sum(jnp.where(left, 0.0, value), axis=1, keepdims=True)
        return first, second

    scaled = (g_ref[...].astype(F32) * inv_ref[...]).astype(BF)
    fine = att_ref[...].astype(F32) + low_ref[...].astype(F32)
    inner = head_sums(scaled.astype(F32) * fine)
    acc_q[...] = jnp.zeros_like(acc_q)
    spans = ((0, 256, 0), (256, 432, 128), (432, tokens, 384))
    q_turned = q.T
    k_turned = [k[first:last].T for first, last, _ in spans]
    upper = lax.broadcasted_iota(jnp.int32, q_turned.shape, 0) < HDIM
    nothing = jnp.zeros_like(q_turned)
    for h in range(2):
        mine = left if h == 0 else lane >= HDIM
        spare = HDIM * (1 - h)
        q_own = jnp.where(mine, q, zero)
        queries = jnp.where(upper if h == 0 else ~upper, q_turned, nothing)
        heads = slice(HDIM * h, HDIM * (h + 1))
        g_own = jnp.where(mine, scaled, zero)
        high, low = split_low(-inner[h])
        wide = q.shape
        g_more = jnp.where(
            lane == spare,
            jnp.broadcast_to(high, wide),
            jnp.where(lane == spare + 1, jnp.broadcast_to(low, wide), g_own),
        )
        v_more = jnp.where(mine, v, jnp.where((lane >= spare) & (lane < spare + 2), one, zero))
        g_turned = g_more.T
        for (first, last, row), k_part in zip(spans, k_turned):
            score = dot(k[first:last], queries[:, row:])
            key = lax.broadcasted_iota(jnp.int32, score.shape, 0) + first
            weight = jnp.where(key < limit_ref[:, row:], jnp.exp(score), 0.0).astype(BF)
            slope = dot(v_more[first:last], g_turned[:, row:])
            slope = (weight.astype(F32) * slope).astype(BF)
            dv = dot(weight, g_own[row:])
            dk = dot(slope, q_own[row:])
            if h == 0:
                acc_v[first:last, :] = dv
                acc_k[first:last, :] = dk
            else:
                acc_v[first:last, :] += dv
                acc_k[first:last, :] += dk
            acc_q[heads, row:] += dot(k_part[heads], slope)
    gain = gain_ref[...]
    dq, dk = acc_q[...].T, acc_k[...]
    q, k = q.astype(F32), k.astype(F32)
    along = dq * q
    first, second = head_sums(along)
    grad_ref[0] = (
        rq_ref[...].astype(F32) * (dq * gain - q * (jnp.where(left, first, second) / gain))
    ).astype(BF)
    hs_ref[...] = jnp.broadcast_to(jnp.sum(along, axis=0, keepdims=True), hs_ref.shape)
    first, second = head_sums(dk * k)
    grad_ref[1] = (rk_ref[...].astype(F32) * (dk - k * jnp.where(left, first, second))).astype(BF)
    grad_ref[2] = acc_v[...].astype(BF)


def attend_back(qkv, grad, attended, low, inverse, norms, gain, limit, base, some):
    tokens = qkv.shape[0]
    pairs = qkv.shape[1] // (6 * HDIM)
    pair = lambda at: pl.BlockSpec((tokens, 2 * HDIM), lambda p: (0, at + base + p))
    return pl.pallas_call(
        attend_back_body,
        grid=(some,),
        in_specs=[
            pair(0),
            pair(pairs),
            pair(2 * pairs),
            pair(0),
            pair(0),
            pair(0),
            pair(0),
            pair(0),
            pair(pairs),
            pl.BlockSpec((1, 2 * HDIM), lambda p: (0, base + p)),
            whole(limit.shape),
        ],
        out_specs=[
            pl.BlockSpec((3, tokens, 2 * HDIM), lambda p: (0, 0, p)),
            pl.BlockSpec((8, 2 * HDIM), lambda p: (0, p)),
        ],
        out_shape=[
            jax.ShapeDtypeStruct((3, tokens, 2 * HDIM * some), BF),
            jax.ShapeDtypeStruct((8, 2 * HDIM * some), F32),
        ],
        scratch_shapes=[pltpu.VMEM((2 * HDIM, tokens), F32)]
        + [pltpu.VMEM((tokens, 2 * HDIM), F32)] * 2,
        compiler_params=grant(58),
        cost_estimate=cost(
            40 * some * tokens * tokens * HDIM, 60 * tokens * HDIM * some, 2 * some * tokens * tokens
        ),
        name="attend_back",
    )(qkv, qkv, qkv, grad, attended, low, inverse, norms, norms, gain, limit)


def project_body(live_ref, x_ref, att_ref, w_ref, mod_ref, cot_ref, proj_ref, mlp_ref, grad_ref):
    proj_ref[...] = dot(att_ref[...], w_ref[...])
    for rows in row_chunks(x_ref.shape[0]):
        residual = x_ref[rows, :].astype(F32) + mod_ref[0:1, :] * proj_ref[rows, :]
        unit, _ = norm_parts(residual)
        mlp_ref[rows, :] = (unit * (1.0 + mod_ref[3:4, :]) + mod_ref[5:6, :]).astype(BF)
        at = lax.broadcasted_iota(jnp.int32, residual.shape, 0) + rows.start
        live = jnp.where(at < live_ref[0], 1.0, 0.0)
        grad_ref[rows, :] = (mod_ref[1:2, :] * (cot_ref[rows, :].astype(F32) * live)).astype(BF)


def project(live, x, attended, w_vo, mod, cot):
    tokens, width = x.shape
    full = whole((tokens, width))
    return pl.pallas_call(
        project_body,
        grid=(1,),
        in_specs=[
            pl.BlockSpec(memory_space=pltpu.SMEM),
            full,
            full,
            pl.BlockSpec((width, width), lambda _: (0, 3)),
            whole(mod.shape),
            full,
        ],
        out_specs=[full] * 3,
        out_shape=[jax.ShapeDtypeStruct((tokens, width), t) for t in (F32, BF, BF)],
        compiler_params=grant(22),
        cost_estimate=cost(2 * tokens * width * width, 14 * tokens * width + 2 * width * width, 0, 1),
        name="project",
    )(live, x, attended, w_vo, mod, cot)


def residual_back_body(
    live_ref, x_ref, proj_ref, out_ref, gx_ref, cot_ref, mod_ref, w_ref,
    block_ref, resid_ref, gatt_ref, gproj, sums_ref,
):
    totals = [0.0] * 4
    for rows in row_chunks(x_ref.shape[0]):
        proj, mlp_out, g = proj_ref[rows, :], out_ref[rows, :], gx_ref[rows, :]
        residual = x_ref[rows, :].astype(F32) + mod_ref[0:1, :] * proj
        at = lax.broadcasted_iota(jnp.int32, residual.shape, 0) + rows.start
        live = jnp.where(at < live_ref[0], 1.0, 0.0)
        block_ref[rows, :] = ((residual + mod_ref[1:2, :] * mlp_out) * live).astype(BF)
        grad_out = cot_ref[rows, :].astype(F32) * live
        unit, inverse = norm_parts(residual)
        dn = g * (1.0 + mod_ref[3:4, :])
        mean_dn = jnp.mean(dn, axis=-1, keepdims=True)
        mean_in = jnp.mean(dn * unit, axis=-1, keepdims=True)
        grad_resid = grad_out + inverse * (dn - mean_dn - unit * mean_in)
        resid_ref[rows, :] = grad_resid
        gproj[rows, :] = (mod_ref[0:1, :] * grad_resid).astype(BF)
        for i, part in enumerate((grad_resid * proj, grad_out * mlp_out, g * unit, g)):
            totals[i] = totals[i] + jnp.sum(part, axis=0, keepdims=True)
    for i in range(4):
        sums_ref[i : i + 1, :] = totals[i]
    sums_ref[4:, :] = jnp.zeros((4, sums_ref.shape[1]), F32)
    gatt_ref[...] = dot(gproj[...], w_ref[...], LAST).astype(BF)


def residual_back(live, x, proj, mlp_out, gx, cot, mod, weights):
    tokens, width = x.shape
    full = whole((tokens, width))
    return pl.pallas_call(
        residual_back_body,
        grid=(1,),
        in_specs=[
            pl.BlockSpec(memory_space=pltpu.SMEM),
            full,
            full,
            full,
            full,
            full,
            whole(mod.shape),
            pl.BlockSpec((width, width), lambda _: (0, 3)),
        ],
        out_specs=[full, full, full, full, whole((8, width))],
        out_shape=[jax.ShapeDtypeStruct((tokens, width), t) for t in (BF, F32, BF, BF)]
        + [jax.ShapeDtypeStruct((8, width), F32)],
        compiler_params=grant(58),
        cost_estimate=cost(2 * tokens * width * width, 28 * tokens * width + 4 * width * width),
        name="residual_back",
    )(live, x, proj, mlp_out, gx, cot, mod, weights)


def weight_grad_body(core_ref, x_ref, g_ref, att_ref, proj_ref, keep_a, send_a, keep_b, send_b):
    step = pl.program_id(0)
    core = core_ref[0]

    @pl.when(step < 2)
    def _():
        keep_a[...], send_a[...] = halves_of(dot(x_ref[...], g_ref[0], FIRST), core)

    @pl.when(step == 2)
    def _():
        keep_b[...], send_b[...] = halves_of(dot(x_ref[...], g_ref[0], FIRST), core)

    @pl.when(step == 3)
    def _():
        keep_b[...], send_b[...] = halves_of(dot(att_ref[...], proj_ref[...], FIRST), core)


def weight_grad(core, x, g, attended, grad_proj):
    tokens, width = x.shape
    full = whole((tokens, width))
    part = (BLOCKS // 2, width // BLOCKS, width)
    first = pl.BlockSpec(part, lambda n: (0, 0, jnp.minimum(n, 1)))
    second = pl.BlockSpec(part, lambda n: (0, 0, jnp.maximum(n - 2, 0)))
    return pl.pallas_call(
        weight_grad_body,
        grid=(4,),
        in_specs=[
            pl.BlockSpec(memory_space=pltpu.SMEM),
            full,
            pl.BlockSpec((1, tokens, width), lambda n: (jnp.minimum(n, 2), 0, 0)),
            full,
            full,
        ],
        out_specs=[first, first, second, second],
        out_shape=[jax.ShapeDtypeStruct(part[:2] + (2 * width,), BF)] * 4,
        compiler_params=grant(58),
        cost_estimate=cost(8 * tokens * width * width, 12 * tokens * width + 8 * width * width),
        name="weight_grad",
    )(core, x, g, attended, grad_proj)


def input_back_body(x_ref, resid_ref, mod_ref, g_ref, w_ref, out_ref, sums_ref):
    step = pl.program_id(0)
    part = dot(g_ref[0], w_ref[...], LAST)

    @pl.when(step == 0)
    def _():
        out_ref[...] = part

    @pl.when(step > 0)
    def _():
        out_ref[...] += part

    @pl.when(step == 2)
    def _():
        totals = [0.0] * 2
        for rows in row_chunks(x_ref.shape[0]):
            g = out_ref[rows, :]
            unit, inverse = norm_parts(x_ref[rows, :].astype(F32))
            dn = g * (1.0 + mod_ref[2:3, :])
            mean_dn = jnp.mean(dn, axis=-1, keepdims=True)
            mean_in = jnp.mean(dn * unit, axis=-1, keepdims=True)
            out_ref[rows, :] = resid_ref[rows, :] + inverse * (dn - mean_dn - unit * mean_in)
            for i, part in enumerate((g * unit, g)):
                totals[i] = totals[i] + jnp.sum(part, axis=0, keepdims=True)
        for i in range(2):
            sums_ref[i : i + 1, :] = totals[i]
        sums_ref[2:, :] = jnp.zeros((6, x_ref.shape[1]), F32)


def input_back(x, resid, mod, g, weights):
    tokens, width = x.shape
    full = whole((tokens, width))
    return pl.pallas_call(
        input_back_body,
        grid=(3,),
        in_specs=[
            full,
            full,
            whole(mod.shape),
            pl.BlockSpec((1, tokens, width), lambda n: (n, 0, 0)),
            pl.BlockSpec((width, width), lambda n: (0, n)),
        ],
        out_specs=[full, whole((8, width))],
        out_shape=[
            jax.ShapeDtypeStruct((tokens, width), F32),
            jax.ShapeDtypeStruct((8, width), F32),
        ],
        compiler_params=grant(58),
        cost_estimate=cost(6 * tokens * width * width, 16 * tokens * width + 6 * width * width),
        name="input_back",
    )(x, resid, mod, g, weights)


def mlp_body(info_ref, x_ref, g_ref, bias_ref, *refs, first, sources):
    a_refs, b_refs, refs = refs[:sources], refs[sources : 2 * sources], refs[2 * sources :]
    if first:
        out_ref, gx_ref, keep_a, send_a, keep_b, send_b, bias_g, up_w, down_w = refs
    else:
        out_in, gx_in, out_ref, gx_ref, keep_a, send_a, keep_b, send_b, bias_g, up_w, down_w = refs
    core = info_ref[2, 0]
    block = x_ref.shape[1] // BLOCKS

    @pl.when(pl.program_id(0) == 0)
    def _():
        out_ref[...] = jnp.zeros_like(out_ref) if first else out_in[...]
        gx_ref[...] = jnp.zeros_like(gx_ref) if first else gx_in[...]

    step = pl.program_id(0)
    size = up_w.shape[1]
    per = down_w.shape[0] // size
    fill(up_w, info_ref.at[0], paired(a_refs), block)

    @pl.when(step % per == 0)
    def _():
        fill(down_w, info_ref.at[1], paired(b_refs), block)

    root = np.float32(np.sqrt(2.0 / np.pi))
    x, g, up = x_ref[...], g_ref[...], up_w[...]
    down = down_w[pl.ds(pl.multiple_of(step % per * size, size), size), :]
    hidden = dot(x, up) + bias_ref[...]
    square = hidden * hidden
    bend = jnp.tanh(root * hidden * (1.0 + 0.044715 * square))
    act = (0.5 * hidden * (1.0 + bend)).astype(BF)
    out_ref[...] += dot(act, down)
    slope = 0.5 * (1.0 + bend) + 0.5 * hidden * (1.0 - bend * bend) * root * (
        1.0 + (3 * 0.044715) * square
    )
    grad_hidden = (dot(g, down, LAST) * slope).astype(BF)
    bias_g[...] = jnp.sum(grad_hidden.astype(F32), axis=0, keepdims=True)
    gx_ref[...] += dot(grad_hidden, up, LAST)
    keep_b[...], send_b[...] = halves_of(dot(act, g, FIRST), core, BLOCKS // per)
    keep_a[...], send_a[...] = halves_of(dot(x, grad_hidden, FIRST), core)


def mlp(info, x, g, pieces, bias, at, carried=None):
    tokens, width = x.shape
    block, per = 512, width // 512
    lead, rows = BLOCKS // 2, width // BLOCKS
    part_a = pl.BlockSpec((lead, rows, block), lambda f: (0, 0, f))
    if len(pieces) == 3:
        matrices = (*pieces[1], *pieces[2])
        total = matrices[0].shape[2]
        sources = [
            pl.BlockSpec(m.shape[:2] + (block,), lambda f: (0, 0, f)) for m in pieces[1]
        ] + [pl.BlockSpec(m.shape[:2] + (width,), lambda f: (0, 0, f // per)) for m in pieces[2]]
    else:
        matrices = [pieces[0].reshape(lead, 2, rows, -1)] * 4
        total = matrices[0].shape[3] // 2
        skip = total // width
        sources = [
            pl.BlockSpec((lead, None, rows, block), lambda f: (0, 0, 0, f)),
            pl.BlockSpec((lead, None, rows, block), lambda f: (0, 1, 0, f)),
            pl.BlockSpec((lead, None, rows, width), lambda f: (0, 0, 0, skip + f // per)),
            pl.BlockSpec((lead, None, rows, width), lambda f: (0, 1, 0, skip + f // per)),
        ]
    steps = total // block
    grad_b = pl.BlockSpec((lead // per, rows, width), lambda f: (f % per, 0, f // per))
    single = pl.BlockSpec((tokens, width), lambda f: (0, 0), pipeline_mode=pl.Buffered(1))
    carried = () if carried is None else tuple(carried)
    return pl.pallas_call(
        partial(mlp_body, first=not carried, sources=len(matrices) // 2),
        grid=(steps,),
        in_specs=[pl.BlockSpec(memory_space=pltpu.SMEM), single, single]
        + [pl.BlockSpec((1, block), lambda f: (0, at * per + f))]
        + sources
        + [single] * len(carried),
        out_specs=[single, single, part_a, part_a, grad_b, grad_b]
        + [pl.BlockSpec((1, block), lambda f: (0, f))],
        out_shape=[jax.ShapeDtypeStruct((tokens, width), F32)] * 2
        + [jax.ShapeDtypeStruct((lead, rows, total), BF)] * 4
        + [jax.ShapeDtypeStruct((1, total), F32)],
        scratch_shapes=[pltpu.VMEM((width, block), BF), pltpu.VMEM((width, width), BF)],
        input_output_aliases={4 + len(matrices) + i: i for i in range(len(carried))},
        compiler_params=grant(58 if carried else 50),
        cost_estimate=cost(
            12 * tokens * width * total,
            (8 + 8 * len(carried)) * tokens * width + 8 * total * width,
            tokens * total,
            20 if carried else 0.3,
        ),
        name="mlp",
    )(info, x, g, bias, *matrices, *carried)


def fold_body(bit_ref, *refs, plan, out_count):
    ins, outs = refs[:-out_count], refs[-out_count:]
    for source, cols, bit, stride, out, column in plan:
        kept, came = ins[2 * source], ins[2 * source + 1]
        at_cols = slice(column, column + cols.stop - cols.start)
        if bit is None:
            outs[out][:, :, at_cols] = kept[:, :, cols].astype(F32) + came[:, :, cols].astype(F32)
            continue
        mine = bit_ref[bit]
        for m in range(kept.shape[0] // 2):
            base = m // stride * 2 * stride + m % stride
            for side, value in ((0, mine), (1, 1 - mine)):
                at = base + value * stride
                outs[out + side][m, :, at_cols] = (
                    kept[at, :, cols].astype(F32) + came[at, :, cols].astype(F32)
                ).astype(BF)


def fold(bits, parts, plan, outs, split=1, weight=0):
    def spec(shape):
        return pl.BlockSpec(tuple(shape[:2]) + (shape[2] // split,), lambda n: (0, 0, n))

    return pl.pallas_call(
        partial(fold_body, plan=plan, out_count=len(outs)),
        grid=(split,),
        in_specs=[pl.BlockSpec(memory_space=pltpu.SMEM)] + [spec(p.shape) for p in parts],
        out_specs=[spec(s) for s, _ in outs],
        out_shape=[jax.ShapeDtypeStruct(s, t) for s, t in outs],
        compiler_params=grant(58),
        cost_estimate=cost(weight, 8),
        name="fold",
    )(bits, *parts)


def swap(block, count, mask):
    return lax.ppermute(block, AXES, [(i, i ^ mask) for i in range(count)])


def after(value, *others):
    return lax.optimization_barrier((value,) + others)


def join(block, came):
    return jnp.concatenate([block, came])


def codes(order, me):
    code = [0]
    for bit in order:
        code = code + [c | (1 << bit) for c in code]
    return jnp.asarray(np.array(code, np.int32)) ^ me


def gathered_pieces(full):
    rows, cols = full.shape
    cut = full.reshape(BLOCKS // 2, 2, rows // BLOCKS, 2, cols // 2)
    return [tuple(cut[:, i, :, j] for i in range(2)) for j in range(2)]


def halve(pieces, axis, bit_value, count, mask):
    total = pieces[0]
    if len(pieces) > 1:
        total = (pieces[0].astype(F32) + pieces[1].astype(F32)).astype(BF)
    keep = lax.dynamic_index_in_dim(total, bit_value, axis, keepdims=False)
    send = lax.dynamic_index_in_dim(total, 1 - bit_value, axis, keepdims=False)
    return [keep, swap(send, count, mask)]


def scatter_rows(kept, send, count, me):
    grads = [jnp.stack(pair, axis=1).reshape(-1, pair[0].shape[2]) for pair in zip(kept, send)]
    grad = jnp.concatenate(grads, axis=1)
    rows, width = grad.shape
    bits = count.bit_length() - 1
    own = rows // count
    bit = [lax.rem(lax.div(me, np.int32(1 << b)), np.int32(2)) for b in range(bits)]
    part = [grad.reshape((2,) * bits + (own, width))]
    for b in range(bits):
        part = halve(part, bits - 1 - b, bit[b], count, 1 << b)
    return (part[0].astype(F32) + part[1].astype(F32)).reshape(own, width)


def tie(*groups):
    flat = lax.optimization_barrier(tuple(a for g in groups for a in g))
    for g in groups:
        g[:], flat = flat[: len(g)], flat[len(g) :]


def land(value, *moves):
    box = [value]
    tie(box, *[m.came for m in moves])
    return box[0]


def leave(value, *scatters):
    for s in scatters:
        s.add()
    box = [value]
    tie(box, *[s.send for s in scatters])
    for s in scatters:
        if s.done is None:
            s.start()
    return box[0]


class Gather:
    def __init__(self, shard, count):
        self.count = count
        self.block = shard[None]
        self.came = None

    def start_z(self, bit):
        self.came = [swap(self.block, self.count, 1 << bit)]

    def end_z(self):
        self.block = join(self.block, self.came[0])

    def start_xy(self, first, second):
        if not isinstance(self.block, list):
            half = self.block.shape[2] // 2
            self.block = [self.block[:, :, :half], self.block[:, :, half:]]
        self.came = [
            swap(b, self.count, 1 << bit) for b, bit in zip(self.block, (first, second))
        ]

    def end_xy(self):
        self.block = [join(b, c) for b, c in zip(self.block, self.came)]

    def start_early(self):
        self.early = [swap(b, self.count, 1) for b in self.block]

    def start_late(self):
        self.late = [swap(c, self.count, 1) for c in self.came]

    def pieces(self, code):
        sides = [
            (b, e, c, l) for b, e, c, l in zip(self.block, self.early, self.came, self.late)
        ]
        return (code, *sides)


class Scatter:
    def __init__(self, kept, send, pieces, bits, count, heavy=0):
        self.bits, self.count, self.heavy = bits, count, heavy
        self.pieces = pieces
        self.kept, self.send = list(kept), list(send)
        self.left = 0
        self.done = None
        self.start()

    def start(self):
        masks = ([1] * len(self.send), (2, 4), (4, 2), (8,), (16,))[self.left]
        self.came = [swap(s, self.count, mask) for s, mask in zip(self.send, masks)]
        self.left += 1

    def add(self):
        parts = [p for pair in zip(self.kept, self.came) for p in pair]
        lead, own, width = self.kept[0].shape
        split = {1: 2, 2: 2}.get(self.left, 1)
        everything = slice(0, width // split)
        half = lambda cols: ((lead // 2, own, cols), BF)
        if self.left == 5:
            plan, outs, at = [], [], 0
            for i, cols in enumerate(self.pieces):
                plan.append((0, slice(at, at + cols), None, 1, i, 0))
                outs.append(((lead, own, cols), F32))
                at += cols
        elif self.left == 1:
            plan, sums = [], [0, 0]
            for side in range(2):
                plan.append((side, everything, (1, 2)[side], (1, 2)[side], 2 * side, 0))
            outs = [half(width)] * 4
        elif self.left == 2:
            plan = tuple((i, everything, 2 - i, 1, 2 * i, 0) for i in range(2))
            outs = [half(width)] * 4
        elif self.left == 3:
            plan = tuple((i, everything, 3, 1, 0, i * width) for i in range(2))
            outs = [half(2 * width)] * 2
        else:
            plan = ((0, everything, 4, 1, 0, 0),)
            outs = [half(width)] * 2
        weight = self.heavy if self.left == 5 else 0
        outs = fold(self.bits, parts, tuple(plan), outs, split, weight)
        if self.left == 5:
            self.done, self.send = [o[0] for o in outs], list(outs)
        else:
            self.kept, self.send = list(outs[0::2]), list(outs[1::2])


def per_device(
    tokens,
    labels,
    stop_scale,
    class_table,
    ada_weight,
    ada_bias,
    qkv_weight,
    head_scale,
    out_weight,
    up_weight,
    up_bias,
    down_weight,
    cotangent,
    count,
):
    image_count, seq_len, model_width = tokens.shape
    row_count = image_count * seq_len
    me = lax.axis_index(AXES).astype(jnp.int32)
    levels = position_scale(SCALES)
    ends = jnp.asarray(LEVEL_ENDS)
    live = jnp.take(ends, stop_scale - 1).astype(jnp.int32)
    limit = jnp.asarray(LEVEL_ENDS[levels][None, :])
    start = jnp.asarray((LEVEL_ENDS - np.square(np.array(scale_sides)))[levels][None, :].astype(np.int32))
    class_count = class_table.shape[0]
    own = model_width // count
    ratio = down_weight.shape[0] // own
    hidden_width = up_weight.shape[1]

    def hidden_order(matrix):
        lead = matrix.shape[:-1]
        cut = matrix.reshape(lead + (count, ratio, own))
        return jnp.swapaxes(cut, -3, -2).reshape(lead + (hidden_width,))

    def hidden_back(matrix):
        lead = matrix.shape[:-1]
        cut = matrix.reshape(lead + (ratio, count, own))
        return jnp.swapaxes(cut, -3, -2).reshape(lead + (hidden_width,))

    down_wide = jnp.swapaxes(down_weight.reshape(ratio, own, model_width), 0, 1).reshape(
        own, hidden_width
    )
    half = hidden_width // 2
    up_order = hidden_order(up_weight)
    shards = [jnp.concatenate([qkv_weight, out_weight], axis=1)] + [
        jnp.concatenate([m[:, i : i + half] for m in (up_order, down_wide)], axis=1)
        for i in (0, half)
    ]
    quick = count == BLOCKS and own % 16 == 0
    plain = jnp.asarray(np.tile(np.arange(0, BLOCKS, 2, dtype=np.int32), (2, 1)))
    if quick:
        one, two = [Gather(s, count) for s in shards[:2]]
        orders = ((4, 3, 2, 1), (4, 3, 1, 2))
        code = jnp.stack([codes(o, me) for o in orders])
        bits = jnp.stack([lax.rem(lax.div(me, np.int32(1 << b)), np.int32(2)) for b in range(5)])
        one.start_z(4)
        one.came[0], two.block = after(one.came[0], two.block)
        one.end_z()
        one.start_z(3)
    else:
        wide = [lax.all_gather(s, AXES, axis=0, tiled=True) for s in shards]
        code = plain
        bits = jnp.zeros((5,), jnp.int32)
    core = bits[:1]
    info, info_plain = [
        jnp.concatenate([c, jnp.full((1, c.shape[1]), bits[0])]) for c in (code, plain)
    ]

    first_row = jnp.concatenate(
        [lax.div(labels, 32).astype(BF), lax.rem(labels, 32).astype(BF), up_bias]
    )
    rows = lax.all_to_all(
        jnp.broadcast_to(first_row[None, :], (count, first_row.shape[0])), AXES, 0, 0, tiled=True
    )
    labels_all = 32 * rows[:, 0].astype(jnp.int32) + rows[:, 1].astype(jnp.int32)
    up_bias_full = rows[:, 2:].astype(F32).reshape(1, hidden_width)
    onehot = labels_all[:, None] == jnp.arange(class_count, dtype=jnp.int32)[None, :]
    condition = jnp.dot(onehot.astype(BF), class_table, preferred_element_type=F32)
    cond_act = jax.nn.silu(condition).astype(BF)
    exponent = count.bit_length() - 1
    order = tuple(range(exponent - 1, -1, -1)) + (exponent,)
    backwards = cond_act.reshape((2,) * exponent + (own,)).transpose(order).reshape(count, own)
    modul_part = jnp.dot(backwards, ada_weight, preferred_element_type=F32)
    bias_own = ada_bias.shape[0]
    bias_row = lax.dynamic_update_slice(
        jnp.zeros((6 * model_width,), F32), ada_bias.astype(F32), (me * bias_own,)
    )
    part = modul_part + bias_row[None, :]
    bit_values = [lax.rem(lax.div(me, np.int32(1 << b)), np.int32(2)) for b in range(exponent)]
    for b in range(exponent):
        size = part.shape[0] // 2
        keep = lax.dynamic_slice_in_dim(part, bit_values[b] * size, size)
        send = lax.dynamic_slice_in_dim(part, (1 - bit_values[b]) * size, size)
        came = swap(send, count, 1 << b)
        if quick and b == 0:
            came = land(came, one)
            one.end_z()
            came, two.block = after(came, two.block)
            one.start_xy(2, 1)
            two.start_z(4)
        elif quick and b == 2:
            came = land(came, one, two)
            one.end_xy()
            two.end_z()
            one.start_early()
            one.start_xy(1, 2)
            two.start_z(3)
        part = keep + came
    mod = part.reshape(6, model_width)
    if quick:
        mod = land(mod, one, two)
        two.end_z()
        one.start_late()
        two.start_xy(2, 1)
        pieces = one.pieces(code)
    else:
        pieces = (code, *gathered_pieces(wide[0]))
    heads = head_scale.shape[0]
    gain = jnp.repeat(jnp.exp(head_scale), HDIM)[None, :]
    seg = jnp.asarray(
        np.arange(model_width)[:, None] // HDIM == np.arange(128)[None, :], dtype=BF
    )
    x = tokens.reshape(row_count, model_width)
    cot = cotangent.reshape(row_count, model_width)

    attn_in, qkv, norms, weights = qkv_rows(x, mod, pieces, gain, seg)
    if quick:
        qkv = land(qkv, two)
        two.end_xy()
        qkv, last_shard, *two.block = after(qkv, shards[2], *two.block)
        last_full = lax.all_gather(last_shard, AXES, axis=0, tiled=True)
        two.start_early()
        two.start_xy(1, 2)
    attended, low, inverse = attend(qkv, start)
    projected, mlp_in, grad_mlp = project(live, x, attended, weights, mod, cot)
    if quick:
        mlp_in = land(mlp_in, two)
        two.start_late()
    bias = hidden_order(up_bias_full)
    pieces = two.pieces(code) if quick else (wide[1],)
    *carried, keep_a, send_a, keep_b, send_b, bias_one = mlp(info, mlp_in, grad_mlp, pieces, bias, 0)
    kept_one, send_one = (keep_a, keep_b), (send_a, send_b)
    if quick:
        first = Scatter(kept_one, send_one, (half, half), bits, count, 1 << 33)
        carried[0] = land(carried[0], first)
        carried[0] = leave(carried[0], first)
    pieces = (last_full if quick else wide[2],)
    mlp_out, grad_mlp_in, keep_a, send_a, keep_b, send_b, bias_two = mlp(
        info_plain, mlp_in, grad_mlp, pieces, bias, half // model_width, carried
    )
    kept_two, send_two = (keep_a, keep_b), (send_a, send_b)
    if quick:
        second = Scatter(kept_two, send_two, (half, half), bits, count)
        mlp_out = land(mlp_out, first)
        mlp_out = leave(mlp_out, first)
    block_out, grad_resid, grad_attended, grad_proj, sums_two = residual_back(
        live, x, projected, mlp_out, grad_mlp_in, cot, mod, weights
    )
    if quick:
        grad_attended = land(grad_attended, first, second)
        grad_attended = leave(grad_attended, first, second)
    dqkv, head_sums = attend_back(
        qkv, grad_attended, attended, low, inverse, norms, gain, limit, 0, heads // 2
    )
    if quick:
        dqkv = land(dqkv, first, second)
        dqkv = leave(dqkv, first, second)
    keep_a, send_a, keep_b, send_b = weight_grad(core, attn_in, dqkv, attended, grad_proj)
    kept_three, send_three = (keep_a, keep_b), (send_a, send_b)
    if quick:
        third = Scatter(
            kept_three, send_three, (3 * model_width, model_width), bits, count
        )
        dqkv = land(dqkv, first, second)
        dqkv = leave(dqkv, first, second)
        dqkv = land(dqkv, third)
        dqkv = leave(dqkv, third)
    input_grad, sums_one = input_back(x, grad_resid, mod, dqkv, weights)
    if not quick:
        mlp_own = [
            scatter_rows(kept_one, send_one, count, me),
            scatter_rows(kept_two, send_two, count, me),
        ]
        up_own = jnp.concatenate([m[:, :half] for m in mlp_own], axis=1)
        down_own = jnp.concatenate([m[:, half:] for m in mlp_own], axis=1)
        attn_own = scatter_rows(kept_three, send_three, count, me)
        qkv_own, out_own = attn_own[:, : 3 * model_width], attn_own[:, 3 * model_width :]
    block_out = block_out.reshape(tokens.shape)
    input_grad = input_grad.reshape(tokens.shape)
    if quick:
        sums_one, bias_one, bias_two, head_sums, sums_two = after(
            sums_one, bias_one, bias_two, head_sums, sums_two
        )
    up_bias_grad = jnp.concatenate([bias_one, bias_two], axis=1)
    grad_modul = jnp.concatenate(
        [sums_two[0], sums_two[1], sums_one[0], sums_two[2], sums_one[1], sums_two[3]]
    ).astype(BF)
    head_scale_part = jnp.sum(head_sums[0].reshape(heads, HDIM), axis=1)
    bias_high, bias_low = split_low(hidden_back(up_bias_grad).reshape(count, -1))
    head_high, head_low = split_low(head_scale_part)
    common = jnp.concatenate([grad_modul.reshape(-1), head_high, head_low])
    small = jnp.concatenate(
        [jnp.broadcast_to(common[None, :], (count, common.shape[0])), bias_high, bias_low], axis=1
    )
    small = lax.all_to_all(small, AXES, 0, 0, tiled=True)
    if quick:
        input_grad = land(input_grad, second, third)
        input_grad = leave(input_grad, second, third)
        input_grad = land(input_grad, second, third)
        input_grad = leave(input_grad, second, third)
        input_grad = land(input_grad, third)
        small, input_grad = after(small, input_grad)
        small = leave(small, third)
        third.add()
        up_own, down_own = [jnp.concatenate(m, axis=1) for m in zip(first.done, second.done)]
        qkv_own, out_own = third.done
    modul_cols = image_count * 6 * model_width
    grad_modul_all = small[:, :modul_cols].reshape(count * image_count, 6 * model_width)
    tail = jnp.sum(small[:, modul_cols:].astype(F32), axis=0)
    head_scale_grad = tail[:heads] + tail[heads : 2 * heads]
    tail = tail[2 * heads :].reshape(2, -1)
    up_bias_own = tail[0] + tail[1]
    ada_bias_own = jnp.sum(
        lax.dynamic_slice_in_dim(grad_modul_all, me * bias_own, bias_own, axis=1).astype(F32), axis=0
    )
    ada_own = lax.dot_general(
        cond_act, grad_modul_all, (((0,), (0,)), ((), ())), preferred_element_type=F32
    )
    grad_cond_act = lax.dot_general(
        grad_modul_all, ada_weight, (((1,), (1,)), ((), ())), preferred_element_type=F32
    )
    grad_condition = jax.vjp(jax.nn.silu, condition)[1](grad_cond_act)[0]
    table_own = lax.dot_general(
        onehot.astype(F32),
        grad_condition,
        (((0,), (0,)), ((), ())),
        precision=lax.Precision.HIGHEST,
        preferred_element_type=F32,
    )
    up_own = hidden_back(up_own)
    down_own = jnp.swapaxes(down_own.reshape(own, ratio, model_width), 0, 1).reshape(
        ratio * own, model_width
    )
    return (
        block_out,
        input_grad,
        table_own,
        ada_own,
        ada_bias_own,
        qkv_own,
        head_scale_grad,
        out_own,
        up_own,
        up_bias_own,
        down_own,
    )


def solution(mesh):
    count = mesh.shape["wide"] * mesh.shape["narrow"]
    both = AXES
    in_specs = (
        P(both, None, None),
        P(both),
        P(both),
        P(None, both),
        P(both, None),
        P(both),
        P(both, None),
        P(),
        P(both, None),
        P(both, None),
        P(both),
        P(both, None),
        P(both, None, None),
    )
    out_specs = (
        P(both, None, None),
        P(both, None, None),
        P(None, both),
        P(both, None),
        P(both),
        P(both, None),
        P(),
        P(both, None),
        P(both, None),
        P(both),
        P(both, None),
    )
    return jax.shard_map(
        partial(per_device, count=count),
        mesh=mesh,
        in_specs=in_specs,
        out_specs=out_specs,
        check_vma=False,
    )
```
